32 devices in a mesh: lat: 4 (over y, x), lon: 8 (over z, core).
Axes of the slice: x: 2, y: 2, z: 4, core: 2. Of those that a mesh axis runs over, the one named last changes fastest.
Arguments:
- frame_one: bfloat16 [64, 256, 256], P('lat', 'lon'), may hold values from -6 to 6
- frame_two: bfloat16 [64, 256, 256], P('lat', 'lon'), may hold values from -6 to 6
- enc_weight: bfloat16 [3, 3, 256, 256], replicated, may hold values from -0.125 to 0.125
- mask_weight: bfloat16 [256, 576], replicated, may hold values from -0.375 to 0.375
Outputs:
- up_flow: float32 [2, 512, 2048], P(None, 'lat', 'lon')
The draws below stay inside these ranges and needn't reach their ends.
All inputs are finite; a program needn't handle non-finite values.
Results may differ from the reference program's by a relative error of at most 0.0011.
Values may be sent and summed in bfloat16 or wider, within the bound.
A program may use at most 64 MiB of HBM per device.

```python
import math
import jax
import jax.numpy as jnp
from jax import lax

CHANNELS = 256
BLOCK_ROWS = 8
BLOCK_COLS = 16
UPSCALE = 8
MASK_COLS = 576
GRID_ROWS = 64
GRID_COLS = 256


def level_of(rng, extent, cuts, low, largest):
    def one(axis_at, blocks):
        draws = jax.random.uniform(jax.random.fold_in(jax.random.fold_in(rng, 6), axis_at), (blocks,), jnp.float32, low / len(cuts), largest / len(cuts))
        return jnp.repeat(jnp.exp(draws), extent[axis_at] // blocks).reshape((-1,) + (1,) * (len(extent) - axis_at - 1))

    gain = one(*cuts[0])
    for cut in cuts[1:]:
        gain = gain * one(*cut)
    return gain


def scatter_about(own_key, extent, scale, reach, split=(), kind=jnp.bfloat16):
    result = jax.random.normal(own_key, extent, jnp.float32) * scale
    if len(split) > 0:
        result = level_of(own_key, extent, split, -0.22, 0.18) * result
    return jnp.clip(result, min=-reach, max=reach).astype(kind)


def setup_inputs(seed: int = 0) -> dict:
    streams_of = jax.random.split(jax.random.key(seed), 5)
    frame_one = scatter_about(streams_of[0], (GRID_ROWS, GRID_COLS, CHANNELS), 1.0, 6.0, ((0, 4), (1, 8)))
    frame_two = scatter_about(streams_of[1], (GRID_ROWS, GRID_COLS, CHANNELS), 1.0, 6.0, ((0, 4), (1, 8)))
    enc_weight = scatter_about(streams_of[2], (3, 3, CHANNELS, CHANNELS), (9 * CHANNELS) ** -0.5, 0.125)
    mask_weight = scatter_about(streams_of[3], (CHANNELS, MASK_COLS), CHANNELS ** -0.5, 0.375)
    return dict(frame_one=frame_one, frame_two=frame_two, enc_weight=enc_weight, mask_weight=mask_weight)


def encode_grid(source, weight):
    padded = jnp.pad(source, ((1, 1), (0, 0), (0, 0)))
    summed = jnp.zeros((GRID_ROWS, GRID_COLS, CHANNELS), jnp.float32)
    for row_off in range(3):
        for col_off in range(3):
            moved = jnp.roll(padded[row_off:row_off + GRID_ROWS], 1 - col_off, axis=1)
            summed = summed + jnp.dot(moved.reshape(GRID_ROWS * GRID_COLS, CHANNELS), weight[row_off, col_off], preferred_element_type=jnp.float32).reshape(GRID_ROWS, GRID_COLS, CHANNELS)
    return summed.astype(jnp.bfloat16)

def reference(frame_one, frame_two, enc_weight, mask_weight):
    enc_one = encode_grid(frame_one, enc_weight)
    enc_two = encode_grid(frame_two, enc_weight)
    padded_two = jnp.pad(enc_two, ((BLOCK_ROWS, BLOCK_ROWS), (0, 0), (0, 0)))
    block_size = BLOCK_ROWS * BLOCK_COLS
    column_blocks = GRID_COLS // BLOCK_COLS
    row_blocks = GRID_ROWS // BLOCK_ROWS
    key_row = (jnp.arange(block_size) // BLOCK_COLS).astype(jnp.float32)
    key_col = (jnp.arange(block_size) % BLOCK_COLS).astype(jnp.float32)
    scale = 1.0 / math.sqrt(CHANNELS)

    def block_row(index):
        query = lax.dynamic_slice_in_dim(enc_one, index * BLOCK_ROWS, BLOCK_ROWS, 0)
        query = query.reshape(BLOCK_ROWS, column_blocks, BLOCK_COLS, CHANNELS).transpose(1, 0, 2, 3)
        query = query.reshape(column_blocks, block_size, CHANNELS).astype(jnp.float32)
        window = lax.dynamic_slice_in_dim(padded_two, index * BLOCK_ROWS, 3 * BLOCK_ROWS, 0)
        window = window.reshape(3, BLOCK_ROWS, column_blocks, BLOCK_COLS, CHANNELS).transpose(0, 2, 1, 3, 4)
        window = window.reshape(3, column_blocks, block_size, CHANNELS).astype(jnp.float32)
        mass = jnp.zeros((column_blocks, block_size), jnp.float32)
        sum_y = jnp.zeros((column_blocks, block_size), jnp.float32)
        sum_x = jnp.zeros((column_blocks, block_size), jnp.float32)
        for row_off in range(3):
            target = index + row_off - 1
            inside = ((target >= 0) & (target < row_blocks)).astype(jnp.float32)
            for col_off in range(3):
                keyed = jnp.roll(window[row_off], 1 - col_off, axis=0)
                scores = jnp.einsum('jqc,jkc->jqk', query, keyed) * scale
                expo = jnp.exp(scores) * inside
                part = lax.optimization_barrier(jnp.sum(expo, axis=-1))
                mass = mass + part
                sum_y = sum_y + lax.optimization_barrier(jnp.sum(expo * key_row, axis=-1)) + BLOCK_ROWS * (row_off - 1) * part
                sum_x = sum_x + lax.optimization_barrier(jnp.sum(expo * key_col, axis=-1)) + BLOCK_COLS * (col_off - 1) * part
        flow_y = sum_y / mass - key_row
        flow_x = sum_x / mass - key_col
        stacked = jnp.stack([flow_y, flow_x]).reshape(2, column_blocks, BLOCK_ROWS, BLOCK_COLS)
        return stacked.transpose(0, 2, 1, 3).reshape(2, BLOCK_ROWS, GRID_COLS)
    rows_out = lax.map(block_row, jnp.arange(row_blocks, dtype=jnp.int32))
    flow = rows_out.transpose(1, 0, 2, 3).reshape(2, GRID_ROWS, GRID_COLS)
    logits = jnp.dot(enc_one.reshape(GRID_ROWS * GRID_COLS, CHANNELS), mask_weight, preferred_element_type=jnp.float32)
    logits = logits.reshape(GRID_ROWS, GRID_COLS, 9, UPSCALE * UPSCALE)
    expo = jnp.exp(logits)
    mix = expo / lax.optimization_barrier(jnp.sum(expo, axis=2, keepdims=True))
    padded_flow = jnp.pad(flow, ((0, 0), (1, 1), (0, 0)))
    upsampled = jnp.zeros((2, GRID_ROWS, GRID_COLS, UPSCALE * UPSCALE), jnp.float32)
    for row_off in range(3):
        for col_off in range(3):
            beside = jnp.roll(padded_flow[:, row_off:row_off + GRID_ROWS], 1 - col_off, axis=2) * UPSCALE
            upsampled = upsampled + mix[None, :, :, 3 * row_off + col_off, :] * beside[..., None]
    upsampled = upsampled.reshape(2, GRID_ROWS, GRID_COLS, UPSCALE, UPSCALE).transpose(0, 1, 3, 2, 4)
    return upsampled.reshape(2, GRID_ROWS * UPSCALE, GRID_COLS * UPSCALE)
```

```python
import functools
import math

import jax
import jax.numpy as jnp
from jax import lax
from jax.experimental import pallas as pl
from jax.experimental.pallas import tpu as pltpu
from jax.sharding import PartitionSpec as P

BLOCK_ROWS = 8
BLOCK_COLS = 16
BLOCK = BLOCK_ROWS * BLOCK_COLS
UPSCALE = 8
F32 = jnp.float32
BF16 = jnp.bfloat16
MESH = pl.DeviceIdType.MESH


def iota(shape, axis):
    return lax.broadcasted_iota(jnp.int32, shape, axis)


def mm(a, b):
    return jnp.dot(a, b, preferred_element_type=F32)


def mm_nt(a, b):
    return lax.dot_general(a, b, (((1,), (1,)), ((), ())), preferred_element_type=F32)


def swap_groups(xs, lane_group):
    xs = list(xs)
    for bit in (1, 2, 4):
        mask = (lane_group & bit) != 0
        shift = bit * BLOCK_COLS
        for a in range(8):
            if a & bit:
                continue
            lo, hi = xs[a], xs[a | bit]
            xs[a] = jnp.where(mask, pltpu.roll(hi, shift, 1), lo)
            xs[a | bit] = jnp.where(mask, hi, pltpu.roll(lo, BLOCK - shift, 1))
    return xs


def kernel(
    f1, f2, w_hbm, mw_hbm, mix, flows,
    fr, wv, mv, wp, acc, hal, strip_s, strip_r, corner_s, corner_r, keys, qs, fb,
    lsem, ssem, rsem,
):
    rows, cols, ch = f1.shape
    rb_n, cb_n = rows // BLOCK_ROWS, cols // BLOCK_COLS
    n_mask = mw_hbm.shape[0]
    lat, lon = lax.axis_index("lat"), lax.axis_index("lon")
    nlat, nlon = lax.axis_size("lat"), lax.axis_size("lon")
    has_n, has_s = lat > 0, lat < nlat - 1
    left = (lat, lax.rem(lon + nlon - 1, nlon))
    right = (lat, lax.rem(lon + 1, nlon))
    north, south = (lat - 1, lon), (lat + 1, lon)

    loads = [
        pltpu.make_async_copy(f1, fr.at[0, pl.ds(1, rows)], lsem.at[0]),
        pltpu.make_async_copy(f2, fr.at[1, pl.ds(1, rows)], lsem.at[1]),
        pltpu.make_async_copy(w_hbm, wv, lsem.at[2]),
        pltpu.make_async_copy(mw_hbm, mv, lsem.at[3]),
    ]
    for load in loads:
        load.start()

    barrier = pltpu.get_barrier_semaphore()

    def greet(peer):
        pl.semaphore_signal(barrier, inc=1, device_id=peer, device_id_type=MESH)

    greet(left)
    greet(right)
    pl.when(has_n)(lambda: greet(north))
    pl.when(has_s)(lambda: greet(south))

    def send(k, src, dst, peer):
        return pltpu.make_async_remote_copy(
            src_ref=src, dst_ref=dst, send_sem=ssem.at[k], recv_sem=rsem.at[k],
            device_id=peer, device_id_type=MESH,
        )

    zero_row = jnp.zeros((cols, ch), BF16)
    for f in range(2):
        fr[f, 0] = zero_row
        fr[f, rows + 1] = zero_row

    halo_rows = {
        0: [send(0, f1.at[0], hal.at[1, 0], north), send(1, f2.at[0], hal.at[1, 1], north)],
        1: [
            send(2, f1.at[rows - 1], hal.at[0, 0], south),
            send(3, f2.at[rows - 1], hal.at[0, 1], south),
        ],
    }
    strips = [
        send(4, strip_s.at[0], strip_r.at[1], left),
        send(5, strip_s.at[1], strip_r.at[0], right),
    ]
    corners = [
        send(6, corner_s.at[0], corner_r.at[1], left),
        send(7, corner_s.at[1], corner_r.at[0], right),
    ]

    def absent(side):
        return jnp.logical_not(has_n if side == 0 else has_s)

    def present(side):
        return has_n if side == 0 else has_s

    for side in range(2):

        @pl.when(absent(side))
        def _():
            hal[side] = jnp.zeros(hal.shape[1:], hal.dtype)
            lo = 0 if side == 0 else BLOCK_ROWS + rows
            keys[lo : lo + BLOCK_ROWS] = jnp.zeros((BLOCK_ROWS,) + keys.shape[1:], BF16)
            at = 0 if side == 0 else rb_n + 1
            fb[at] = jnp.zeros(fb.shape[1:], F32)

    loads[0].wait()
    loads[1].wait()
    for side in range(2):
        lo, pick = (0, 0) if side == 0 else (cols - 16, 15)
        for f in range(2):
            tile = fr[f, 1 : rows + 1, lo : lo + 16, :].astype(F32)
            one = jnp.sum(jnp.where(iota(tile.shape, 1) == pick, tile, 0.0), axis=1)
            strip_s[side, f * rows : (f + 1) * rows] = one.astype(BF16)

    pl.semaphore_wait(barrier, 2 + has_n.astype(jnp.int32) + has_s.astype(jnp.int32))

    for side in range(2):

        @pl.when(present(side))
        def _():
            for copy in halo_rows[side]:
                copy.start()

    for copy in strips:
        copy.start()

    loads[2].wait()

    def col_shift(y, side):
        flat = y.reshape(-1, ch)
        n = flat.shape[0]
        turned = pltpu.roll(flat, 1 if side == 0 else n - 1, 0).reshape(y.shape)
        edge = 0 if side == 0 else cols - 1
        return jnp.where(iota(y.shape, 1) == edge, 0.0, turned)

    for f in range(2):
        lhs = jnp.concatenate(
            [fr[f, a : a + rows].reshape(rows * cols, ch) for a in range(3)], axis=1
        )
        ys = [mm(lhs, wv[:, b].reshape(3 * ch, ch)).reshape(rows, cols, ch) for b in range(3)]
        acc[f] = ys[1] + col_shift(ys[0], 0) + col_shift(ys[2], 1)

    for side in range(2):

        @pl.when(present(side))
        def _():
            for copy in halo_rows[1 - side]:
                copy.wait_recv()

    for side in range(2):
        edge = 0 if side == 0 else cols - 1
        base = 0 if side == 0 else cols - 16
        got = jnp.zeros((16, ch), F32)
        for f in range(2):
            for end in range(2):
                tile = hal[end, f, base : base + 16, :].astype(F32)
                one = tile[edge - base : edge - base + 1]
                got = jnp.where(iota((16, ch), 0) == 2 * f + end, one, got)
        corner_s[side] = got.astype(BF16)
    for copy in corners:
        copy.start()

    for side in range(2):
        a = 0 if side == 0 else 2
        r = 0 if side == 0 else rows - 1
        flat = hal[side].reshape(2 * cols, ch)
        ys = [mm(flat, wv[a, b]).reshape(2, cols, ch) for b in range(3)]
        y = ys[1] + col_shift(ys[0], 0) + col_shift(ys[2], 1)
        for f in range(2):
            acc[f, r] = acc[f, r] + y[f]

    br, bc = BLOCK_ROWS, BLOCK_COLS
    own_r = pl.ds(br, rows)
    edge_w = 8
    mid = (bc + edge_w, cols - 2 * edge_w)
    lows, highs = (bc, edge_w), (bc + cols - edge_w, edge_w)

    def key_row_sends(k, span, at=0, n=br):
        c = pl.ds(*span)
        return [
            send(k, keys.at[pl.ds(br + at, n), c], keys.at[pl.ds(br + rows + at, n), c], north),
            send(k + 1, keys.at[pl.ds(rows + at, n), c], keys.at[pl.ds(at, n), c], south),
        ]

    def key_col_sends(k, r, early):
        off = edge_w if early else 0
        back = 0 if early else edge_w
        return [
            send(k, keys.at[r, pl.ds(bc + off, edge_w)],
                 keys.at[r, pl.ds(bc + cols + off, edge_w)], left),
            send(k + 1, keys.at[r, pl.ds(cols + back, edge_w)],
                 keys.at[r, pl.ds(back, edge_w)], right),
        ]

    rows_mid = key_row_sends(8, mid)
    half = br // 2
    rows_edge = [
        [key_row_sends(10, lows, 0, half), key_row_sends(12, highs, 0, half)],
        [key_row_sends(34, lows, half, half), key_row_sends(36, highs, half, half)],
    ]
    cols_early = key_col_sends(14, own_r, True)
    cols_late = key_col_sends(24, own_r, False)
    corners_early, corners_late = {}, [{}, {}]
    for side in range(2):
        r = pl.ds(0 if side == 0 else br + rows, br)
        corners_early[side] = key_col_sends(26 + 4 * side, r, True)
        for part in range(2):
            r = pl.ds((0 if side == 0 else br + rows) + part * half, half)
            k = 28 + 4 * side if part == 0 else 38 + 2 * side
            corners_late[part][side] = key_col_sends(k, r, False)

    keys[br : br + rows, mid[0] : mid[0] + mid[1]] = acc[
        1, :, edge_w : cols - edge_w, :
    ].astype(BF16)
    for side in range(2):

        @pl.when(present(side))
        def _():
            rows_mid[side].start()

    for copy in cols_early:
        copy.start()

    loads[3].wait()
    p = iota((n_mask, n_mask), 0)
    want = (p - (p & 63)) + ((p & 7) << 3) + ((p >> 3) & 7)
    perm = (iota((n_mask, n_mask), 1) == want).astype(F32).astype(BF16)
    wp[...] = mm(perm, mv[...]).astype(BF16)

    for copy in strips + corners:
        copy.wait_recv()
    row_id = iota((rows, ch), 0)
    rims = []
    for side in range(2):
        lhs = jnp.concatenate([strip_r[side], corner_r[side]], axis=0)
        rims.append([mm(lhs, wv[a, 2 * side]) for a in range(3)])

    def add_rim_columns(f):
        for side in range(2):
            z = rims[side]
            own = [z[a][f * rows : (f + 1) * rows] for a in range(3)]
            top = z[0][2 * rows + 2 * f : 2 * rows + 2 * f + 1]
            bottom = z[2][2 * rows + 2 * f + 1 : 2 * rows + 2 * f + 2]
            h = own[1] + jnp.where(row_id == 0, top, pltpu.roll(own[0], 1, 0))
            h = h + jnp.where(row_id == rows - 1, bottom, pltpu.roll(own[2], rows - 1, 0))
            lo, pick = (0, 0) if side == 0 else (cols - 8, 7)
            tile = acc[f, :, lo : lo + 8, :]
            acc[f, :, lo : lo + 8, :] = tile + jnp.where(
                iota(tile.shape, 1) == pick, h[:, None, :], 0.0
            )

    add_rim_columns(1)
    for lo in (0, cols - edge_w):
        keys[br : br + rows, bc + lo : bc + lo + edge_w] = acc[
            1, :, lo : lo + edge_w, :
        ].astype(BF16)
    for side in range(2):

        @pl.when(present(side))
        def _():
            for part in rows_edge:
                for rows_sent in part:
                    rows_sent[side].start()

    for copy in cols_late:
        copy.start()

    add_rim_columns(0)

    for cb in range(cb_n):
        for rb in range(rb_n):
            block = acc[0, rb * br : (rb + 1) * br, cb * bc : (cb + 1) * bc, :]
            qs[cb, rb * BLOCK : (rb + 1) * BLOCK] = block.astype(BF16).reshape(BLOCK, ch)

    scale = 1.0 / math.sqrt(ch)
    inside = [has_n.astype(F32), has_s.astype(F32)]
    zero = jnp.zeros((8, BLOCK), F32)
    totals = {(rb, cb): [zero, zero, zero] for rb in range(rb_n) for cb in range(cb_n)}
    sub = iota((8, BLOCK), 0).astype(F32)

    def correlate(kbs, kc):
        part = keys[kbs[0] * br : (kbs[-1] + 1) * br, kc * bc : (kc + 1) * bc, :]
        part = part.reshape(len(kbs) * BLOCK, ch)
        for cb in range(max(0, kc - 2), min(cb_n, kc + 1)):
            rbs = [rb for rb in range(rb_n) if any(0 <= kb - rb <= 2 for kb in kbs)]
            r0 = rbs[0]
            s = mm_nt(part, qs[cb, r0 * BLOCK : (rbs[-1] + 1) * BLOCK])
            for at, kb in enumerate(kbs):
                for rb in rbs:
                    if not 0 <= kb - rb <= 2:
                        continue
                    e = s[at * BLOCK : (at + 1) * BLOCK, (rb - r0) * BLOCK : (rb - r0 + 1) * BLOCK]
                    e = jnp.exp(e * scale).reshape(br, 2, 8, BLOCK)
                    lanes = [e[:, h] for h in range(2)]
                    by_row = lanes[0] + lanes[1]
                    y = by_row[0] * float(br * (kb - rb - 1))
                    for kr in range(1, br):
                        y = y + by_row[kr] * float(br * (kb - rb - 1) + kr)
                    by_col = [jnp.sum(h, axis=0) for h in lanes]
                    m = by_col[0] + by_col[1]
                    off = float(bc * (kc - cb - 1))
                    x = by_col[0] * (sub + off) + by_col[1] * (sub + (off + 8.0))
                    if kb == 0 or kb == rb_n + 1:
                        gate = inside[0] if kb == 0 else inside[1]
                        m, y, x = m * gate, y * gate, x * gate
                    old = totals[rb, cb]
                    totals[rb, cb] = [old[0] + m, old[1] + y, old[2] + x]

    own_kbs = list(range(1, rb_n + 1))
    for kc in range(1, cb_n + 1):
        correlate(own_kbs, kc)

    def pass_on(arrivals, relays):
        for side in range(2):

            @pl.when(present(side))
            def _():
                for rows_sent in arrivals:
                    rows_sent[1 - side].wait_recv()
                for copy in relays[side]:
                    copy.start()

    pass_on([rows_mid], corners_early)

    for cb in range(cb_n):
        logits = mm_nt(wp[...], qs[cb]).reshape(9, UPSCALE * UPSCALE, rb_n * BLOCK)
        e = jnp.exp(logits)
        mix[cb] = e / jnp.sum(e, axis=0, keepdims=True)

    for part in range(2):
        pass_on(rows_edge[part], corners_late[part])

    for kc in range(1, cb_n + 1):
        correlate([0], kc)
        correlate([rb_n + 1], kc)
    for copy in cols_early + cols_late:
        copy.wait_recv()
    for kc in (0, cb_n + 1):
        correlate(own_kbs, kc)
    for side in range(2):

        @pl.when(present(side))
        def _():
            for copy in corners_early[side] + corners_late[0][side] + corners_late[1][side]:
                copy.wait_recv()

    for kc in (0, cb_n + 1):
        correlate([0], kc)
        correlate([rb_n + 1], kc)

    lane = iota((8, BLOCK), 1)
    sublane = iota((8, BLOCK), 0)
    qr, qc = lane >> 4, lane & 15
    for (rb, cb), (m, y, x) in totals.items():
        m, y, x = [jnp.sum(t, axis=0, keepdims=True) for t in (m, y, x)]
        fy = y / m - qr.astype(F32)
        fx = x / m - qc.astype(F32)
        both = jnp.where(sublane == 0, fy, fx) * float(UPSCALE)
        fb[rb + 1, cb + 1] = both

    flow_rows = [
        send(16, fb.at[1, pl.ds(1, cb_n)], fb.at[rb_n + 1, pl.ds(1, cb_n)], north),
        send(17, fb.at[rb_n, pl.ds(1, cb_n)], fb.at[0, pl.ds(1, cb_n)], south),
    ]
    flow_cols = [
        send(18, fb.at[pl.ds(1, rb_n), 1], fb.at[pl.ds(1, rb_n), cb_n + 1], left),
        send(19, fb.at[pl.ds(1, rb_n), cb_n], fb.at[pl.ds(1, rb_n), 0], right),
    ]
    flow_corners = {}
    for side in range(2):
        src_r, dst_r = (1, rb_n + 1) if side == 0 else (rb_n, 0)
        to = lat - 1 if side == 0 else lat + 1
        flow_corners[side] = [
            send(20 + 2 * side, fb.at[src_r, 1], fb.at[dst_r, cb_n + 1], (to, left[1])),
            send(21 + 2 * side, fb.at[src_r, cb_n], fb.at[dst_r, 0], (to, right[1])),
        ]
    for side in range(2):

        @pl.when(present(side))
        def _():
            for copy in flow_corners[side] + [flow_rows[side]]:
                copy.start()

    for copy in flow_cols:
        copy.start()
    for copy in flow_cols:
        copy.wait_recv()
    for side in range(2):

        @pl.when(present(side))
        def _():
            for copy in flow_corners[1 - side] + [flow_rows[1 - side]]:
                copy.wait_recv()

    flows[...] = fb[...]

    for side in range(2):

        @pl.when(present(side))
        def _():
            for copy in halo_rows[side] + [
                rows_mid[side], flow_rows[side]
            ] + [sent[side] for part in rows_edge for sent in part]:
                copy.wait_send()
            for copy in corners_early[side] + corners_late[0][side] + corners_late[1][side] + flow_corners[side]:
                copy.wait_send()

    for copy in strips + corners + cols_early + cols_late + flow_cols:
        copy.wait_send()


def upsample(mix, fb, out_hbm, out, sem):
    cb_n, rb_n = mix.shape[0], mix.shape[3] // BLOCK
    lane = iota((8, BLOCK), 1)
    qr, qc = lane >> 4, lane & 15
    k = iota((BLOCK, BLOCK), 0)
    weave = (iota((BLOCK, BLOCK), 1) == ((k & 15) << 3) + (k >> 4)).astype(F32).astype(BF16)

    copies = []
    for cb in range(cb_n):
        for rb in range(rb_n):
            shifted = {}
            for r in range(rb, rb + 3):
                mid = fb[r, cb + 1]
                shifted[r, 0] = jnp.where(
                    qc == 0, pltpu.roll(fb[r, cb], BLOCK - 15, 1), pltpu.roll(mid, 1, 1)
                )
                shifted[r, 1] = mid
                shifted[r, 2] = jnp.where(
                    qc == 15, pltpu.roll(fb[r, cb + 2], 15, 1), pltpu.roll(mid, BLOCK - 1, 1)
                )
            beside = []
            for a in range(3):
                for b in range(3):
                    here = shifted[rb + 1, b]
                    if a == 0:
                        here = pltpu.roll(jnp.where(qr == 7, shifted[rb, b], here), BLOCK_COLS, 1)
                    if a == 2:
                        here = pltpu.roll(
                            jnp.where(qr == 0, shifted[rb + 2, b], here), BLOCK - BLOCK_COLS, 1
                        )
                    beside.append(here)
            for d in range(2):
                up = jnp.zeros((UPSCALE * UPSCALE, BLOCK), F32)
                for n in range(9):
                    share = mix[cb, n, :, rb * BLOCK : (rb + 1) * BLOCK]
                    up = up + share * beside[n][d : d + 1]
                xs = [up[8 * j : 8 * j + 8] for j in range(8)]
                rowed = jnp.concatenate(swap_groups(xs, qr), axis=0)
                high = rowed.astype(BF16)
                rest = rowed - high.astype(F32)
                mid = rest.astype(BF16)
                low = (rest - mid.astype(F32)).astype(BF16)
                woven = mm(high, weave) + mm(mid, weave) + mm(low, weave)
                out[d, rb * 64 : (rb + 1) * 64, cb * BLOCK : (cb + 1) * BLOCK] = woven
                copies.append(
                    pltpu.make_async_copy(
                        out.at[d, pl.ds(rb * 64, 64), pl.ds(cb * BLOCK, BLOCK)],
                        out_hbm.at[d, pl.ds(rb * 64, 64), pl.ds(cb * BLOCK, BLOCK)],
                        sem.at[len(copies)],
                    )
                )
                copies[-1].start()
    for copy in copies:
        copy.wait()


def body(frame_one, frame_two, enc_weight, mask_weight):
    rows, cols, ch = frame_one.shape
    n_mask = mask_weight.shape[1]
    rb_n, cb_n = rows // BLOCK_ROWS, cols // BLOCK_COLS
    mix, fb = pl.pallas_call(
        kernel,
        out_shape=[
            jax.ShapeDtypeStruct((cb_n, 9, UPSCALE * UPSCALE, rb_n * BLOCK), F32),
            jax.ShapeDtypeStruct((rb_n + 2, cb_n + 2, 8, BLOCK), F32),
        ],
        in_specs=[pl.BlockSpec(memory_space=pltpu.HBM)] * 4,
        out_specs=[pl.BlockSpec(memory_space=pltpu.VMEM)] * 2,
        scratch_shapes=[
            pltpu.VMEM((2, rows + 2, cols, ch), BF16),
            pltpu.VMEM(enc_weight.shape, BF16),
            pltpu.VMEM((n_mask, ch), BF16),
            pltpu.VMEM((n_mask, ch), BF16),
            pltpu.VMEM((2, rows, cols, ch), F32),
            pltpu.VMEM((2, 2, cols, ch), BF16),
            pltpu.VMEM((2, 2 * rows, ch), BF16),
            pltpu.VMEM((2, 2 * rows, ch), BF16),
            pltpu.VMEM((2, 16, ch), BF16),
            pltpu.VMEM((2, 16, ch), BF16),
            pltpu.VMEM((rows + 2 * BLOCK_ROWS, cols + 2 * BLOCK_COLS, ch), BF16),
            pltpu.VMEM((cb_n, rb_n * BLOCK, ch), BF16),
            pltpu.VMEM((rb_n + 2, cb_n + 2, 8, BLOCK), F32),
            pltpu.SemaphoreType.DMA((4,)),
            pltpu.SemaphoreType.DMA((42,)),
            pltpu.SemaphoreType.DMA((42,)),
        ],
        compiler_params=pltpu.CompilerParams(
            collective_id=0, has_side_effects=True, vmem_limit_bytes=32 * 2**20
        ),
        name="flow",
    )(*[pltpu.with_memory_space_constraint(a, pltpu.HBM) for a in (frame_one, frame_two, enc_weight, mask_weight.T)])
    shape = (2, rows * UPSCALE, cols * UPSCALE)
    return pl.pallas_call(
        upsample,
        out_shape=jax.ShapeDtypeStruct(shape, F32),
        in_specs=[pl.BlockSpec(memory_space=pltpu.VMEM)] * 2,
        out_specs=pl.BlockSpec(memory_space=pl.ANY),
        scratch_shapes=[
            pltpu.VMEM(shape, F32),
            pltpu.SemaphoreType.DMA((2 * rb_n * cb_n,)),
        ],
        compiler_params=pltpu.CompilerParams(vmem_limit_bytes=32 * 2**20),
        name="upsample",
    )(mix, fb)


def solution(mesh):
    in_specs = (P("lat", "lon", None), P("lat", "lon", None), P(), P())
    out_specs = P(None, "lat", "lon")
    return jax.shard_map(body, mesh=mesh, in_specs=in_specs, out_specs=out_specs, check_vma=False)
```

```python
import functools
import math

import jax
import jax.numpy as jnp
from jax import lax
from jax.experimental import pallas as pl
from jax.experimental.pallas import tpu as pltpu
from jax.sharding import PartitionSpec as P

BLOCK_ROWS = 8
BLOCK_COLS = 16
BLOCK = BLOCK_ROWS * BLOCK_COLS
UPSCALE = 8
F32 = jnp.float32
BF16 = jnp.bfloat16
MESH = pl.DeviceIdType.MESH


def iota(shape, axis):
    return lax.broadcasted_iota(jnp.int32, shape, axis)


def mm(a, b):
    return jnp.dot(a, b, preferred_element_type=F32)


def mm_nt(a, b):
    return lax.dot_general(a, b, (((1,), (1,)), ((), ())), preferred_element_type=F32)


def swap_groups(xs, lane_group):
    xs = list(xs)
    for bit in (1, 2, 4):
        mask = (lane_group & bit) != 0
        shift = bit * BLOCK_COLS
        for a in range(8):
            if a & bit:
                continue
            lo, hi = xs[a], xs[a | bit]
            xs[a] = jnp.where(mask, pltpu.roll(hi, shift, 1), lo)
            xs[a | bit] = jnp.where(mask, hi, pltpu.roll(lo, BLOCK - shift, 1))
    return xs


def kernel(
    f1, f2, w_hbm, mw_hbm, mix, flows,
    g1, g2, wv, mv, wp, a1, a2, strip_s, strip_r, early_s, early_r, late_s, late_r, keys, qs, fb,
    lsem, ssem, rsem, ready,
):
    rows, cols, ch = f1.shape
    br, bc = BLOCK_ROWS, BLOCK_COLS
    rb_n, cb_n = rows // br, cols // bc
    n_mask = mw_hbm.shape[0]
    rim = br + 1
    lat, lon = lax.axis_index("lat"), lax.axis_index("lon")
    nlat, nlon = lax.axis_size("lat"), lax.axis_size("lon")
    has_n, has_s = lat > 0, lat < nlat - 1
    left = (lat, lax.rem(lon + nlon - 1, nlon))
    right = (lat, lax.rem(lon + 1, nlon))
    north, south = (lat - 1, lon), (lat + 1, lon)

    barrier = pltpu.get_barrier_semaphore()

    def greet(peer):
        pl.semaphore_signal(barrier, inc=1, device_id=peer, device_id_type=MESH)

    first, last = lon == 0, lon == nlon - 1
    greet(left)
    pl.when(jnp.logical_not(last))(lambda: greet(right))
    pl.when(has_n)(lambda: greet(north))
    pl.when(has_s)(lambda: greet(south))

    own = pl.ds(rim, rows)
    loads = [
        pltpu.make_async_copy(f1, g1.at[pl.ds(1, rows)], lsem.at[0]),
        pltpu.make_async_copy(f2, g2.at[own, pl.ds(bc, cols)], lsem.at[1]),
        pltpu.make_async_copy(w_hbm, wv, lsem.at[2]),
        pltpu.make_async_copy(mw_hbm, mv, lsem.at[3]),
    ]
    for load in loads:
        load.start()

    def absent(side):
        return jnp.logical_not(has_n if side == 0 else has_s)

    def present(side):
        return has_n if side == 0 else has_s

    def send(k, src, dst, peer):
        return pltpu.make_async_remote_copy(
            src_ref=src, dst_ref=dst, send_sem=ssem.at[k], recv_sem=rsem.at[k],
            device_id=peer, device_id_type=MESH,
        )

    bands = [(0, 1), (1, 4), (5, 4)]

    def band_at(side, band):
        off, n = bands[band]
        return (rim - off - n if side == 0 else rim + rows + off), n

    def row_send(k, side, band):
        off, n = bands[band]
        src = off if side == 0 else rows - off - n
        dst, _ = band_at(1 - side, band)
        peer = north if side == 0 else south
        return send(k, f2.at[pl.ds(src, n)], g2.at[pl.ds(dst, n), pl.ds(bc, cols)], peer)

    lat_sends = [
        [
            [
                send(side, f1.at[0 if side == 0 else rows - 1],
                     g1.at[rows + 1 if side == 0 else 0], north if side == 0 else south),
                row_send(2 + side, side, 0),
            ]
            for side in range(2)
        ],
        [[row_send(4 + side, side, 1)] for side in range(2)],
        [[row_send(6 + side, side, 2)] for side in range(2)],
    ]
    mains = [
        send(8, f2.at[:, pl.ds(0, bc)], g2.at[own, pl.ds(bc + cols, bc)], left),
        send(9, f2.at[:, pl.ds(cols - bc, bc)], g2.at[own, pl.ds(0, bc)], right),
    ]
    strips = [
        send(10, strip_s.at[0], strip_r.at[1], left),
        send(11, strip_s.at[1], strip_r.at[0], right),
    ]
    earlies = [
        send(12, early_s.at[0], early_r.at[1], left),
        send(13, early_s.at[1], early_r.at[0], right),
    ]

    def relay(k, side, band):
        at, n = band_at(side, band)
        r = pl.ds(at, n)
        return [
            send(k, g2.at[r, pl.ds(bc, bc)], g2.at[r, pl.ds(bc + cols, bc)], left),
            send(k + 1, g2.at[r, pl.ds(cols, bc)], g2.at[r, pl.ds(0, bc)], right),
        ]

    relays = [[relay(24 + 4 * band + 2 * side, side, band) for side in range(2)] for band in range(3)]
    lates = [
        [
            send(36 + 2 * side, late_s.at[0, pl.ds(16 * side, 16)], late_r.at[1, pl.ds(16 * side, 16)], left),
            send(37 + 2 * side, late_s.at[1, pl.ds(16 * side, 16)], late_r.at[0, pl.ds(16 * side, 16)], right),
        ]
        for side in range(2)
    ]

    for side in range(2):

        @pl.when(absent(side))
        def _():
            g1[0 if side == 0 else rows + 1] = jnp.zeros((cols, ch), BF16)
            lo = 0 if side == 0 else rim + rows
            g2[lo : lo + rim] = jnp.zeros((rim,) + g2.shape[1:], BF16)
            late_r[:, 16 * side : 16 * side + 16] = jnp.zeros((2, 16, ch), BF16)
            at = 0 if side == 0 else rb_n + 1
            fb[at] = jnp.zeros(fb.shape[1:], F32)

    met = [jnp.logical_not(first), has_n, has_s]
    pl.semaphore_wait(barrier, 1 + sum(m.astype(jnp.int32) for m in met))

    @pl.when(last)
    def _():
        pl.semaphore_signal(ready, inc=1, device_id=right, device_id_type=MESH)

    for band in range(3):
        for side in range(2):

            @pl.when(present(side))
            def _():
                for copy in lat_sends[band][side]:
                    copy.start()

    loads[0].wait()
    loads[1].wait()

    def pick_col(tile, pick):
        return jnp.sum(jnp.where(iota(tile.shape, 1) == pick, tile.astype(F32), 0.0), axis=1)

    for side in range(2):
        lo, pick = (0, 0) if side == 0 else (cols - bc, bc - 1)
        strip_s[side, :rows] = pick_col(g1[1 : rows + 1, lo : lo + bc, :], pick).astype(BF16)
        lo, pick = (2 * bc, 0) if side == 0 else (cols - bc, bc - 1)
        strip_s[side, rows:] = pick_col(g2[rim : rim + rows, lo : lo + bc, :], pick).astype(BF16)
    strips[1].start()
    mains[1].start()

    @pl.when(jnp.logical_not(first))
    def _():
        strips[0].start()
        mains[0].start()

    loads[2].wait()


    def taps(lhs, n, w):
        ys = [mm(lhs, wv[:, b].reshape(3 * ch, ch)) for b in range(3)]
        t0 = pltpu.roll(ys[0], 1, 0).reshape(n, w, ch)
        t2 = pltpu.roll(ys[2], n * w - 1, 0).reshape(n, w, ch)
        at = iota((n, w, ch), 1)
        y = ys[1].reshape(n, w, ch) + jnp.where(at == 0, 0.0, t0) + jnp.where(at == w - 1, 0.0, t2)
        edge = iota((n, 8, ch), 1)
        to_right = jnp.concatenate([t0[1:, :8], t0[:1, :8]], axis=0)
        to_left = jnp.concatenate([t2[n - 1 :, w - 8 :], t2[: n - 1, w - 8 :]], axis=0)
        return y, jnp.where(edge == 0, to_right, 0.0), jnp.where(edge == 7, to_left, 0.0)

    def lhs1(r, n):
        return jnp.concatenate([g1[r + a : r + a + n].reshape(n * cols, ch) for a in range(3)], axis=1)

    def lhs2(r, n, c, w):
        return jnp.concatenate(
            [g2[r + a : r + a + n, c : c + w, :].reshape(n * w, ch) for a in range(3)], axis=1
        )

    east = bc + cols

    def put_center(r, y, to_right, to_left):
        n = y.shape[0]
        a2[r : r + n, bc:east] = y
        a2[r : r + n, east : east + 8] = to_right
        a2[r : r + n, bc - 8 : bc] = to_left

    inner = rows - 2
    y, _, _ = taps(lhs1(1, inner), inner, cols)
    a1[1 : rows - 1] = y
    put_center(br + 1, *taps(lhs2(br + 1, inner, bc, cols), inner, cols))

    @pl.when(first)
    def _():
        pl.semaphore_wait(ready, 1)
        strips[0].start()
        mains[0].start()

    def arrive(band):
        for side in range(2):

            @pl.when(present(side))
            def _():
                for copy in lat_sends[band][1 - side]:
                    copy.wait_recv()

    def pass_on(band):
        for side in range(2):

            @pl.when(present(side))
            def _():
                for copy in relays[band][side]:
                    copy.start()

    arrive(0)
    pass_on(0)
    at_row, at_key = iota((16, 64), 0), iota((16, 64), 1)
    for side in range(2):
        c1, p1 = (0, 0) if side == 0 else (cols - bc, bc - 1)
        c2, p2 = (2 * bc, 0) if side == 0 else (cols - bc, bc - 1)
        tiles = [g1[r, c1 : c1 + bc, :] for r in (0, rows + 1)]
        tiles += [g2[r, c2 : c2 + bc, :] for r in (rim - 1, rim + rows)]
        hit = jnp.where(at_row < 2, p1, p2) + at_row * bc == at_key
        early_s[side] = mm(hit.astype(F32).astype(BF16), jnp.concatenate(tiles, axis=0)).astype(BF16)
    for copy in earlies:
        copy.start()

    arrive(1)
    pass_on(1)

    arrive(2)
    pass_on(2)
    at_row, at_key = iota((32, 2 * rim * bc), 0), iota((32, 2 * rim * bc), 1)
    held = jnp.where(at_row < 16, at_row - (16 - rim), at_row - 16 + rim)
    held = jnp.where((at_row < 16 - rim) | (at_row >= 16 + rim), -bc, held)
    for side in range(2):
        c, pick = (2 * bc, 0) if side == 0 else (cols - bc, bc - 1)
        tiles = [g2[r : r + rim, c : c + bc, :].reshape(rim * bc, ch) for r in (0, rim + rows)]
        hit = (held * bc + pick == at_key).astype(F32).astype(BF16)
        late_s[side] = mm(hit, jnp.concatenate(tiles, axis=0)).astype(BF16)
    for side in range(2):

        @pl.when(present(side))
        def _():
            for copy in lates[side]:
                copy.start()

    lhs = [lhs2(0, rim, bc, cols), lhs2(br + rows - 1, rim, bc, cols), lhs1(0, 1), lhs1(rows - 1, 1)]
    y, to_right, to_left = taps(jnp.concatenate(lhs, axis=0), 2 * rim + 2, cols)
    for side in range(2):
        part = slice(side * rim, (side + 1) * rim)
        put_center(side * (br + rows - 1), y[part], to_right[part], to_left[part])
    a1[0] = y[2 * rim]
    a1[rows - 1] = y[2 * rim + 1]

    for copy in strips + mains + earlies:
        copy.wait_recv()

    row_id = iota((rows, ch), 0)
    for side in range(2):
        lhs = jnp.concatenate([strip_r[side], early_r[side]], axis=0)
        z = [mm(lhs, wv[a, 2 * side]) for a in range(3)]
        for f in range(2):
            mid = [z[a][f * rows : (f + 1) * rows] for a in range(3)]
            e = 2 * rows + 2 * f
            h = mid[1] + jnp.where(row_id == 0, z[0][e : e + 1], pltpu.roll(mid[0], 1, 0))
            h = h + jnp.where(row_id == rows - 1, z[2][e + 1 : e + 2], pltpu.roll(mid[2], rows - 1, 0))
            lo, pick = (0, 0) if side == 0 else (cols - 8, 7)
            spread = jnp.where(iota((rows, 8, ch), 1) == pick, h[:, None, :], 0.0)
            if f == 0:
                a1[:, lo : lo + 8, :] = a1[:, lo : lo + 8, :] + spread
            else:
                lo = 0 if side == 0 else east + 8
                a2[br : br + rows, lo : lo + 8] = spread

    for cb in range(cb_n):
        for rb in range(rb_n):
            block = a1[rb * br : (rb + 1) * br, cb * bc : (cb + 1) * bc, :]
            qs[cb, rb * BLOCK : (rb + 1) * BLOCK] = block.astype(BF16).reshape(BLOCK, ch)

    def relayed(band):
        for side in range(2):

            @pl.when(present(side))
            def _():
                for copy in relays[band][side]:
                    copy.wait_recv()

    relayed(0)


    def put_sides(r, n, y, to_right, to_left):
        a2[r : r + n, :bc] = a2[r : r + n, :bc] + y[:n]
        a2[r : r + n, east:] = a2[r : r + n, east:] + y[n:]
        a2[r : r + n, bc : bc + 8] = a2[r : r + n, bc : bc + 8] + to_right[:n]
        a2[r : r + n, east - 8 : east] = a2[r : r + n, east - 8 : east] + to_left[n:]

    lhs = [lhs2(br, rows, 0, bc), lhs2(br, rows, east, bc)]
    put_sides(br, rows, *taps(jnp.concatenate(lhs, axis=0), 2 * rows, bc))
    keys[br : br + rows] = a2[br : br + rows].astype(BF16)

    scale = 1.0 / math.sqrt(ch)
    inside = [has_n.astype(F32), has_s.astype(F32)]
    zero = jnp.zeros((8, BLOCK), F32)
    totals = {(rb, cb): [zero, zero, zero] for rb in range(rb_n) for cb in range(cb_n)}
    sub = iota((8, BLOCK), 0).astype(F32)

    def correlate(kbs, kc):
        part = keys[kbs[0] * br : (kbs[-1] + 1) * br, kc * bc : (kc + 1) * bc, :]
        part = part.reshape(len(kbs) * BLOCK, ch)
        for cb in range(max(0, kc - 2), min(cb_n, kc + 1)):
            rbs = [rb for rb in range(rb_n) if any(0 <= kb - rb <= 2 for kb in kbs)]
            r0 = rbs[0]
            s = mm_nt(part, qs[cb, r0 * BLOCK : (rbs[-1] + 1) * BLOCK])
            for at, kb in enumerate(kbs):
                for rb in rbs:
                    if not 0 <= kb - rb <= 2:
                        continue
                    e = s[at * BLOCK : (at + 1) * BLOCK, (rb - r0) * BLOCK : (rb - r0 + 1) * BLOCK]
                    e = jnp.exp(e * scale).reshape(br, 2, 8, BLOCK)
                    lanes = [e[:, h] for h in range(2)]
                    by_row = lanes[0] + lanes[1]
                    y = by_row[0] * float(br * (kb - rb - 1))
                    for kr in range(1, br):
                        y = y + by_row[kr] * float(br * (kb - rb - 1) + kr)
                    by_col = [jnp.sum(h, axis=0) for h in lanes]
                    m = by_col[0] + by_col[1]
                    off = float(bc * (kc - cb - 1))
                    x = by_col[0] * (sub + off) + by_col[1] * (sub + (off + 8.0))
                    if kb == 0 or kb == rb_n + 1:
                        gate = inside[0] if kb == 0 else inside[1]
                        m, y, x = m * gate, y * gate, x * gate
                    old = totals[rb, cb]
                    totals[rb, cb] = [old[0] + m, old[1] + y, old[2] + x]

    own_kbs = list(range(1, rb_n + 1))
    for kc in range(1, cb_n + 1):
        correlate(own_kbs, kc)
    for kc in (0, cb_n + 1):
        correlate(own_kbs, kc)

    relayed(1)
    relayed(2)
    for side in range(2):

        @pl.when(present(side))
        def _():
            for copy in lates[side]:
                copy.wait_recv()

    total = 32 + rows
    for side in range(2):
        lhs = jnp.concatenate([late_r[side, :16], strip_r[side, rows:], late_r[side, 16:]], axis=0)
        z = [mm(lhs, wv[a, 2 * side]) for a in range(3)]
        h = z[1] + pltpu.roll(z[0], 1, 0) + pltpu.roll(z[2], total - 1, 0)
        lo, pick = (0, 0) if side == 0 else (east + 8, 7)
        for end in range(2):
            part = h[8:16] if end == 0 else h[16 + rows : 24 + rows]
            r = end * (br + rows)
            a2[r : r + br, lo : lo + 8] = jnp.where(
                iota((br, 8, ch), 1) == pick, part[:, None, :], 0.0
            )
    lhs = [lhs2(r, br, c, bc) for r in (0, br + rows) for c in (0, east)]
    y, to_right, to_left = taps(jnp.concatenate(lhs, axis=0), 4 * br, bc)
    for end in range(2):
        part = slice(2 * end * br, 2 * (end + 1) * br)
        r = end * (br + rows)
        put_sides(r, br, y[part], to_right[part], to_left[part])
        keys[r : r + br] = (a2[r : r + br] * inside[end]).astype(BF16)

    for kc in range(cb_n + 2):
        correlate([0], kc)
        correlate([rb_n + 1], kc)

    lane = iota((8, BLOCK), 1)
    sublane = iota((8, BLOCK), 0)
    qr, qc = lane >> 4, lane & 15
    for (rb, cb), (m, y, x) in totals.items():
        m, y, x = [jnp.sum(t, axis=0, keepdims=True) for t in (m, y, x)]
        fy = y / m - qr.astype(F32)
        fx = x / m - qc.astype(F32)
        both = jnp.where(sublane == 0, fy, fx) * float(UPSCALE)
        fb[rb + 1, cb + 1] = both

    flow_rows = [
        send(16, fb.at[1, pl.ds(1, cb_n)], fb.at[rb_n + 1, pl.ds(1, cb_n)], north),
        send(17, fb.at[rb_n, pl.ds(1, cb_n)], fb.at[0, pl.ds(1, cb_n)], south),
    ]
    flow_cols = [
        send(18, fb.at[pl.ds(1, rb_n), 1], fb.at[pl.ds(1, rb_n), cb_n + 1], left),
        send(19, fb.at[pl.ds(1, rb_n), cb_n], fb.at[pl.ds(1, rb_n), 0], right),
    ]
    flow_corners = {}
    for side in range(2):
        src_r, dst_r = (1, rb_n + 1) if side == 0 else (rb_n, 0)
        to = lat - 1 if side == 0 else lat + 1
        flow_corners[side] = [
            send(20 + 2 * side, fb.at[src_r, 1], fb.at[dst_r, cb_n + 1], (to, left[1])),
            send(21 + 2 * side, fb.at[src_r, cb_n], fb.at[dst_r, 0], (to, right[1])),
        ]
    for side in range(2):

        @pl.when(present(side))
        def _():
            for copy in flow_corners[side] + [flow_rows[side]]:
                copy.start()

    for copy in flow_cols:
        copy.start()
    loads[3].wait()
    p = iota((n_mask, n_mask), 0)
    want = (p - (p & 63)) + ((p & 7) << 3) + ((p >> 3) & 7)
    perm = (iota((n_mask, n_mask), 1) == want).astype(F32).astype(BF16)
    wp[...] = mm(perm, mv[...]).astype(BF16)

    for cb in range(cb_n):
        logits = mm_nt(wp[...], qs[cb]).reshape(9, UPSCALE * UPSCALE, rb_n * BLOCK)
        e = jnp.exp(logits)
        mix[cb] = e / jnp.sum(e, axis=0, keepdims=True)

    for copy in flow_cols:
        copy.wait_recv()
    for side in range(2):

        @pl.when(present(side))
        def _():
            for copy in flow_corners[1 - side] + [flow_rows[1 - side]]:
                copy.wait_recv()

    flows[...] = fb[...]

    for side in range(2):

        @pl.when(present(side))
        def _():
            for band in range(3):
                for copy in lat_sends[band][side] + relays[band][side]:
                    copy.wait_send()
            for copy in lates[side] + [flow_rows[side]] + flow_corners[side]:
                copy.wait_send()

    for copy in strips + mains + earlies + flow_cols:
        copy.wait_send()


def upsample(mix, fb, out_hbm, out, sem):
    cb_n, rb_n = mix.shape[0], mix.shape[3] // BLOCK
    lane = iota((8, BLOCK), 1)
    qr, qc = lane >> 4, lane & 15
    k = iota((BLOCK, BLOCK), 0)
    weave = (iota((BLOCK, BLOCK), 1) == ((k & 15) << 3) + (k >> 4)).astype(F32).astype(BF16)

    copies = []
    for cb in range(cb_n):
        for rb in range(rb_n):
            shifted = {}
            for r in range(rb, rb + 3):
                mid = fb[r, cb + 1]
                shifted[r, 0] = jnp.where(
                    qc == 0, pltpu.roll(fb[r, cb], BLOCK - 15, 1), pltpu.roll(mid, 1, 1)
                )
                shifted[r, 1] = mid
                shifted[r, 2] = jnp.where(
                    qc == 15, pltpu.roll(fb[r, cb + 2], 15, 1), pltpu.roll(mid, BLOCK - 1, 1)
                )
            beside = []
            for a in range(3):
                for b in range(3):
                    here = shifted[rb + 1, b]
                    if a == 0:
                        here = pltpu.roll(jnp.where(qr == 7, shifted[rb, b], here), BLOCK_COLS, 1)
                    if a == 2:
                        here = pltpu.roll(
                            jnp.where(qr == 0, shifted[rb + 2, b], here), BLOCK - BLOCK_COLS, 1
                        )
                    beside.append(here)
            for d in range(2):
                up = jnp.zeros((UPSCALE * UPSCALE, BLOCK), F32)
                for n in range(9):
                    share = mix[cb, n, :, rb * BLOCK : (rb + 1) * BLOCK]
                    up = up + share * beside[n][d : d + 1]
                xs = [up[8 * j : 8 * j + 8] for j in range(8)]
                rowed = jnp.concatenate(swap_groups(xs, qr), axis=0)
                high = rowed.astype(BF16)
                rest = rowed - high.astype(F32)
                mid = rest.astype(BF16)
                low = (rest - mid.astype(F32)).astype(BF16)
                woven = mm(high, weave) + mm(mid, weave) + mm(low, weave)
                out[d, rb * 64 : (rb + 1) * 64, cb * BLOCK : (cb + 1) * BLOCK] = woven
                copies.append(
                    pltpu.make_async_copy(
                        out.at[d, pl.ds(rb * 64, 64), pl.ds(cb * BLOCK, BLOCK)],
                        out_hbm.at[d, pl.ds(rb * 64, 64), pl.ds(cb * BLOCK, BLOCK)],
                        sem.at[len(copies)],
                    )
                )
                copies[-1].start()
    for copy in copies:
        copy.wait()


def body(frame_one, frame_two, enc_weight, mask_weight):
    rows, cols, ch = frame_one.shape
    n_mask = mask_weight.shape[1]
    rb_n, cb_n = rows // BLOCK_ROWS, cols // BLOCK_COLS
    mix, fb = pl.pallas_call(
        kernel,
        out_shape=[
            jax.ShapeDtypeStruct((cb_n, 9, UPSCALE * UPSCALE, rb_n * BLOCK), F32),
            jax.ShapeDtypeStruct((rb_n + 2, cb_n + 2, 8, BLOCK), F32),
        ],
        in_specs=[pl.BlockSpec(memory_space=pltpu.HBM)] * 4,
        out_specs=[pl.BlockSpec(memory_space=pltpu.VMEM)] * 2,
        scratch_shapes=[
            pltpu.VMEM((rows + 2, cols, ch), BF16),
            pltpu.VMEM((rows + 2 * BLOCK_ROWS + 2, cols + 2 * BLOCK_COLS, ch), BF16),
            pltpu.VMEM(enc_weight.shape, BF16),
            pltpu.VMEM((n_mask, ch), BF16),
            pltpu.VMEM((n_mask, ch), BF16),
            pltpu.VMEM((rows, cols, ch), F32),
            pltpu.VMEM((rows + 2 * BLOCK_ROWS, cols + 2 * BLOCK_COLS, ch), F32),
            pltpu.VMEM((2, 2 * rows, ch), BF16),
            pltpu.VMEM((2, 2 * rows, ch), BF16),
            pltpu.VMEM((2, 16, ch), BF16),
            pltpu.VMEM((2, 16, ch), BF16),
            pltpu.VMEM((2, 32, ch), BF16),
            pltpu.VMEM((2, 32, ch), BF16),
            pltpu.VMEM((rows + 2 * BLOCK_ROWS, cols + 2 * BLOCK_COLS, ch), BF16),
            pltpu.VMEM((cb_n, rb_n * BLOCK, ch), BF16),
            pltpu.VMEM((rb_n + 2, cb_n + 2, 8, BLOCK), F32),
            pltpu.SemaphoreType.DMA((4,)),
            pltpu.SemaphoreType.DMA((40,)),
            pltpu.SemaphoreType.DMA((40,)),
            pltpu.SemaphoreType.REGULAR,
        ],
        compiler_params=pltpu.CompilerParams(
            collective_id=0, has_side_effects=True, vmem_limit_bytes=32 * 2**20
        ),
        name="flow",
    )(*[pltpu.with_memory_space_constraint(a, pltpu.HBM) for a in (frame_one, frame_two, enc_weight, mask_weight.T)])
    shape = (2, rows * UPSCALE, cols * UPSCALE)
    return pl.pallas_call(
        upsample,
        out_shape=jax.ShapeDtypeStruct(shape, F32),
        in_specs=[pl.BlockSpec(memory_space=pltpu.VMEM)] * 2,
        out_specs=pl.BlockSpec(memory_space=pl.ANY),
        scratch_shapes=[
            pltpu.VMEM(shape, F32),
            pltpu.SemaphoreType.DMA((2 * rb_n * cb_n,)),
        ],
        compiler_params=pltpu.CompilerParams(vmem_limit_bytes=32 * 2**20),
        name="upsample",
    )(mix, fb)


def solution(mesh):
    in_specs = (P("lat", "lon", None), P("lat", "lon", None), P(), P())
    out_specs = P(None, "lat", "lon")
    return jax.shard_map(body, mesh=mesh, in_specs=in_specs, out_specs=out_specs, check_vma=False)
```

```python
import functools
import math

import jax
import jax.numpy as jnp
from jax import lax
from jax.experimental import pallas as pl
from jax.experimental.pallas import tpu as pltpu
from jax.sharding import PartitionSpec as P

BLOCK_ROWS = 8
BLOCK_COLS = 16
BLOCK = BLOCK_ROWS * BLOCK_COLS
UPSCALE = 8
F32 = jnp.float32
BF16 = jnp.bfloat16
MESH = pl.DeviceIdType.MESH


def iota(shape, axis):
    return lax.broadcasted_iota(jnp.int32, shape, axis)


def mm(a, b):
    return jnp.dot(a, b, preferred_element_type=F32)


def mm_nt(a, b):
    return lax.dot_general(a, b, (((1,), (1,)), ((), ())), preferred_element_type=F32)


def swap_groups(xs, lane_group):
    xs = list(xs)
    for bit in (1, 2, 4):
        mask = (lane_group & bit) != 0
        shift = bit * BLOCK_COLS
        for a in range(8):
            if a & bit:
                continue
            lo, hi = xs[a], xs[a | bit]
            xs[a] = jnp.where(mask, pltpu.roll(hi, shift, 1), lo)
            xs[a | bit] = jnp.where(mask, hi, pltpu.roll(lo, BLOCK - shift, 1))
    return xs


def kernel(
    f1, f2, w_hbm, mw_hbm, mix, flows,
    g1, g2, wv, mv, wp, a1, a2, strip_s, strip_r, early_s, early_r, late_s, late_r, keys, qs, fb, transit,
    lsem, ssem, rsem, ready,
):
    rows, cols, ch = f1.shape
    br, bc = BLOCK_ROWS, BLOCK_COLS
    rb_n, cb_n = rows // br, cols // bc
    n_mask = mw_hbm.shape[0]
    rim = br + 1
    lat, lon = lax.axis_index("lat"), lax.axis_index("lon")
    nlat, nlon = lax.axis_size("lat"), lax.axis_size("lon")
    has_n, has_s = lat > 0, lat < nlat - 1
    left = (lat, lax.rem(lon + nlon - 1, nlon))
    right = (lat, lax.rem(lon + 1, nlon))
    north, south = (lat - 1, lon), (lat + 1, lon)

    barrier = pltpu.get_barrier_semaphore()

    def greet(peer):
        pl.semaphore_signal(barrier, inc=1, device_id=peer, device_id_type=MESH)

    first, last = lon == 0, lon == nlon - 1
    greet(left)
    pl.when(jnp.logical_not(last))(lambda: greet(right))
    pl.when(has_n)(lambda: greet(north))
    pl.when(has_s)(lambda: greet(south))

    odd = (lax.rem(lon, 2) == 1) & (nlat == 4)
    by_way = [odd & (lat == 2), odd & (lat == 1)]
    is_hub = [odd & (lat == 0), odd & (lat == 3)]
    hubs, ends = [(0, lon), (3, lon)], [(1, lon), (2, lon)]
    for side in range(2):
        pl.when(is_hub[side])(lambda: greet(ends[1 - side]))

    own = pl.ds(rim, rows)
    loads = [
        pltpu.make_async_copy(f1, g1.at[pl.ds(1, rows)], lsem.at[0]),
        pltpu.make_async_copy(f2, g2.at[own, pl.ds(bc, cols)], lsem.at[1]),
        pltpu.make_async_copy(w_hbm, wv, lsem.at[2]),
        pltpu.make_async_copy(mw_hbm, mv, lsem.at[3]),
    ]
    for load in loads:
        load.start()

    def absent(side):
        return jnp.logical_not(has_n if side == 0 else has_s)

    def present(side):
        return has_n if side == 0 else has_s

    def send(k, src, dst, peer, arrive_k=None):
        return pltpu.make_async_remote_copy(
            src_ref=src, dst_ref=dst, send_sem=ssem.at[k],
            recv_sem=rsem.at[k if arrive_k is None else arrive_k],
            device_id=peer, device_id_type=MESH,
        )

    bands = [(0, 1), (1, 5), (6, 3)]

    def band_at(side, band):
        off, n = bands[band]
        return (rim - off - n if side == 0 else rim + rows + off), n

    def row_send(k, side, band):
        off, n = bands[band]
        src = off if side == 0 else rows - off - n
        dst, _ = band_at(1 - side, band)
        peer = north if side == 0 else south
        return send(k, f2.at[pl.ds(src, n)], g2.at[pl.ds(dst, n), pl.ds(bc, cols)], peer)

    lat_sends = [
        [
            [
                send(side, f1.at[0 if side == 0 else rows - 1],
                     g1.at[rows + 1 if side == 0 else 0], north if side == 0 else south),
                row_send(2 + side, side, 0),
            ]
            for side in range(2)
        ],
    ]
    for band in range(1, len(bands)):
        lat_sends.append([[row_send(2 + 2 * band + side, side, band)] for side in range(2)])
    def detour(band, side):
        off, n = bands[band]
        k = 46 + 4 * (band - 1) + 2 * side
        src = off if side == 0 else rows - off - n
        at = transit.at[pl.ds(off - 1, n)]
        dst, _ = band_at(1 - side, band)
        into = g2.at[pl.ds(dst, n), pl.ds(bc, cols)]
        return (
            send(k, f2.at[pl.ds(src, n)], at, hubs[side]),
            send(k + 1, at, into, ends[side], 2 + 2 * band + side),
        )

    detours = [[]] + [[detour(band, side) for side in range(2)] for band in range(1, len(bands))]

    def goes_direct(side, band):
        if band == 0:
            return present(side)
        return present(side) & jnp.logical_not(by_way[side])

    mains = [
        send(44, f2.at[:, pl.ds(0, bc)], g2.at[own, pl.ds(bc + cols, bc)], left),
        send(45, f2.at[:, pl.ds(cols - bc, bc)], g2.at[own, pl.ds(0, bc)], right),
    ]
    strips = [
        send(10, strip_s.at[0], strip_r.at[1], left),
        send(11, strip_s.at[1], strip_r.at[0], right),
    ]
    earlies = [
        send(12, early_s.at[0], early_r.at[1], left),
        send(13, early_s.at[1], early_r.at[0], right),
    ]

    def relay(k, side, band):
        at, n = band_at(side, band)
        r = pl.ds(at, n)
        return [
            send(k, g2.at[r, pl.ds(bc, bc)], g2.at[r, pl.ds(bc + cols, bc)], left),
            send(k + 1, g2.at[r, pl.ds(cols, bc)], g2.at[r, pl.ds(0, bc)], right),
        ]

    relays = [[relay(24 + 4 * band + 2 * side, side, band) for side in range(2)] for band in range(len(bands))]
    lates = [
        [
            send(40 + 2 * side, late_s.at[0, pl.ds(16 * side, 16)], late_r.at[1, pl.ds(16 * side, 16)], left),
            send(41 + 2 * side, late_s.at[1, pl.ds(16 * side, 16)], late_r.at[0, pl.ds(16 * side, 16)], right),
        ]
        for side in range(2)
    ]

    for side in range(2):

        @pl.when(absent(side))
        def _():
            g1[0 if side == 0 else rows + 1] = jnp.zeros((cols, ch), BF16)
            lo = 0 if side == 0 else rim + rows
            g2[lo : lo + rim] = jnp.zeros((rim,) + g2.shape[1:], BF16)
            late_r[:, 16 * side : 16 * side + 16] = jnp.zeros((2, 16, ch), BF16)
            at = 0 if side == 0 else rb_n + 1
            fb[at] = jnp.zeros(fb.shape[1:], F32)

    met = [jnp.logical_not(first), has_n, has_s, by_way[0] | by_way[1]]
    pl.semaphore_wait(barrier, 1 + sum(m.astype(jnp.int32) for m in met))

    @pl.when(last)
    def _():
        pl.semaphore_signal(ready, inc=1, device_id=right, device_id_type=MESH)

    for band in range(len(bands)):
        for side, (by, _) in enumerate(detours[band]):
            pl.when(by_way[side])(by.start)
        for side in range(2):

            @pl.when(goes_direct(side, band))
            def _():
                for copy in lat_sends[band][side]:
                    copy.start()

    loads[0].wait()
    loads[1].wait()

    def pick_col(tile, pick):
        return jnp.sum(jnp.where(iota(tile.shape, 1) == pick, tile.astype(F32), 0.0), axis=1)

    for side in range(2):
        lo, pick = (0, 0) if side == 0 else (cols - bc, bc - 1)
        strip_s[side, :rows] = pick_col(g1[1 : rows + 1, lo : lo + bc, :], pick).astype(BF16)
        lo, pick = (2 * bc, 0) if side == 0 else (cols - bc, bc - 1)
        strip_s[side, rows:] = pick_col(g2[rim : rim + rows, lo : lo + bc, :], pick).astype(BF16)
    strips[1].start()
    mains[1].start()

    @pl.when(jnp.logical_not(first))
    def _():
        strips[0].start()
        mains[0].start()

    loads[2].wait()


    def taps(lhs, n, w):
        ys = [mm(lhs, wv[:, b].reshape(3 * ch, ch)) for b in range(3)]
        t0 = pltpu.roll(ys[0], 1, 0).reshape(n, w, ch)
        t2 = pltpu.roll(ys[2], n * w - 1, 0).reshape(n, w, ch)
        at = iota((n, w, ch), 1)
        y = ys[1].reshape(n, w, ch) + jnp.where(at == 0, 0.0, t0) + jnp.where(at == w - 1, 0.0, t2)
        edge = iota((n, 8, ch), 1)
        to_right = jnp.concatenate([t0[1:, :8], t0[:1, :8]], axis=0)
        to_left = jnp.concatenate([t2[n - 1 :, w - 8 :], t2[: n - 1, w - 8 :]], axis=0)
        return y, jnp.where(edge == 0, to_right, 0.0), jnp.where(edge == 7, to_left, 0.0)

    def lhs1(r, n):
        return jnp.concatenate([g1[r + a : r + a + n].reshape(n * cols, ch) for a in range(3)], axis=1)

    def lhs2(r, n, c, w):
        return jnp.concatenate(
            [g2[r + a : r + a + n, c : c + w, :].reshape(n * w, ch) for a in range(3)], axis=1
        )

    east = bc + cols

    def put_center(r, y, to_right, to_left):
        n = y.shape[0]
        a2[r : r + n, bc:east] = y
        a2[r : r + n, east : east + 8] = to_right
        a2[r : r + n, bc - 8 : bc] = to_left

    inner = rows - 2
    y, _, _ = taps(lhs1(1, inner), inner, cols)
    a1[1 : rows - 1] = y
    put_center(br + 1, *taps(lhs2(br + 1, inner, bc, cols), inner, cols))

    @pl.when(first)
    def _():
        pl.semaphore_wait(ready, 1)
        strips[0].start()
        mains[0].start()

    def arrive(band):
        for side in range(2):

            @pl.when(present(side))
            def _():
                for copy in lat_sends[band][1 - side]:
                    copy.wait_recv()

    def pass_on(band):
        for side in range(2):

            @pl.when(present(side))
            def _():
                for copy in relays[band][side]:
                    copy.start()

    def forward(band):
        for side, (by, on) in enumerate(detours[band]):

            @pl.when(is_hub[side])
            def _():
                by.wait_recv()
                on.start()

    arrive(0)
    pass_on(0)
    at_row, at_key = iota((16, 64), 0), iota((16, 64), 1)
    for side in range(2):
        c1, p1 = (0, 0) if side == 0 else (cols - bc, bc - 1)
        c2, p2 = (2 * bc, 0) if side == 0 else (cols - bc, bc - 1)
        tiles = [g1[r, c1 : c1 + bc, :] for r in (0, rows + 1)]
        tiles += [g2[r, c2 : c2 + bc, :] for r in (rim - 1, rim + rows)]
        hit = jnp.where(at_row < 2, p1, p2) + at_row * bc == at_key
        early_s[side] = mm(hit.astype(F32).astype(BF16), jnp.concatenate(tiles, axis=0)).astype(BF16)
    for copy in earlies:
        copy.start()

    forward(1)
    forward(2)
    arrive(1)
    pass_on(1)

    for band in range(2, len(bands)):
        arrive(band)
        pass_on(band)
    at_row, at_key = iota((32, 2 * rim * bc), 0), iota((32, 2 * rim * bc), 1)
    held = jnp.where(at_row < 16, at_row - (16 - rim), at_row - 16 + rim)
    held = jnp.where((at_row < 16 - rim) | (at_row >= 16 + rim), -bc, held)
    for side in range(2):
        c, pick = (2 * bc, 0) if side == 0 else (cols - bc, bc - 1)
        tiles = [g2[r : r + rim, c : c + bc, :].reshape(rim * bc, ch) for r in (0, rim + rows)]
        hit = (held * bc + pick == at_key).astype(F32).astype(BF16)
        late_s[side] = mm(hit, jnp.concatenate(tiles, axis=0)).astype(BF16)
    for side in range(2):

        @pl.when(present(side))
        def _():
            for copy in lates[side]:
                copy.start()

    for copy in strips + mains + earlies:
        copy.wait_recv()

    def relayed(band):
        for side in range(2):

            @pl.when(present(side))
            def _():
                for copy in relays[band][side]:
                    copy.wait_recv()

    relayed(0)

    def put_sides(r, y, to_right, to_left, spread=None):
        n = y.shape[0] // 2
        outer = [y[:n, :8], y[n:, 8:]]
        if spread is not None:
            outer = [o + h for o, h in zip(outer, spread)]
        a2[r : r + n, :8] = outer[0]
        a2[r : r + n, 8:bc] = a2[r : r + n, 8:bc] + y[:n, 8:]
        a2[r : r + n, east : east + 8] = a2[r : r + n, east : east + 8] + y[n:, :8]
        a2[r : r + n, east + 8 :] = outer[1]
        a2[r : r + n, bc : bc + 8] = a2[r : r + n, bc : bc + 8] + to_right[:n]
        a2[r : r + n, east - 8 : east] = a2[r : r + n, east - 8 : east] + to_left[n:]

    near = br // 2
    last_row = br + rows - 1
    lhs = [lhs2(near, near + 1, bc, cols), lhs2(last_row, near + 1, bc, cols), lhs1(0, 1), lhs1(rows - 1, 1)]
    y, to_right, to_left = taps(jnp.concatenate(lhs, axis=0), 2 * near + 4, cols)
    for side in range(2):
        part = slice(side * (near + 1), (side + 1) * (near + 1))
        put_center(near if side == 0 else last_row, y[part], to_right[part], to_left[part])
    a1[0] = y[2 * near + 2]
    a1[rows - 1] = y[2 * near + 3]

    row_id = iota((rows, ch), 0)
    spreads = []
    for side in range(2):
        lhs = jnp.concatenate([strip_r[side], early_r[side]], axis=0)
        z = [mm(lhs, wv[a, 2 * side]) for a in range(3)]
        for f in range(2):
            mid = [z[a][f * rows : (f + 1) * rows] for a in range(3)]
            e = 2 * rows + 2 * f
            h = mid[1] + jnp.where(row_id == 0, z[0][e : e + 1], pltpu.roll(mid[0], 1, 0))
            h = h + jnp.where(row_id == rows - 1, z[2][e + 1 : e + 2], pltpu.roll(mid[2], rows - 1, 0))
            lo, pick = (0, 0) if side == 0 else (cols - 8, 7)
            spread = jnp.where(iota((rows, 8, ch), 1) == pick, h[:, None, :], 0.0)
            if f == 0:
                a1[:, lo : lo + 8, :] = a1[:, lo : lo + 8, :] + spread
            else:
                spreads.append(spread)

    for cb in range(cb_n):
        for rb in range(rb_n):
            block = a1[rb * br : (rb + 1) * br, cb * bc : (cb + 1) * bc, :]
            qs[cb, rb * BLOCK : (rb + 1) * BLOCK] = block.astype(BF16).reshape(BLOCK, ch)

    lhs = [lhs2(br, rows, 0, bc), lhs2(br, rows, east, bc)]
    put_sides(br, *taps(jnp.concatenate(lhs, axis=0), 2 * rows, bc), spreads)
    keys[br : br + rows] = a2[br : br + rows].astype(BF16)

    scale = 1.0 / math.sqrt(ch)
    inside = [has_n.astype(F32), has_s.astype(F32)]
    zero = jnp.zeros((8, BLOCK), F32)
    totals = {(rb, cb): [zero, zero, zero] for rb in range(rb_n) for cb in range(cb_n)}
    sub = iota((8, BLOCK), 0).astype(F32)

    def correlate(kbs, kc):
        part = keys[kbs[0] * br : (kbs[-1] + 1) * br, kc * bc : (kc + 1) * bc, :]
        part = part.reshape(len(kbs) * BLOCK, ch)
        for cb in range(max(0, kc - 2), min(cb_n, kc + 1)):
            rbs = [rb for rb in range(rb_n) if any(0 <= kb - rb <= 2 for kb in kbs)]
            r0 = rbs[0]
            s = mm_nt(part, qs[cb, r0 * BLOCK : (rbs[-1] + 1) * BLOCK])
            for at, kb in enumerate(kbs):
                for rb in rbs:
                    if not 0 <= kb - rb <= 2:
                        continue
                    e = s[at * BLOCK : (at + 1) * BLOCK, (rb - r0) * BLOCK : (rb - r0 + 1) * BLOCK]
                    e = jnp.exp(e * scale).reshape(br, 2, 8, BLOCK)
                    lanes = [e[:, h] for h in range(2)]
                    by_row = lanes[0] + lanes[1]
                    y = by_row[0] * float(br * (kb - rb - 1))
                    for kr in range(1, br):
                        y = y + by_row[kr] * float(br * (kb - rb - 1) + kr)
                    by_col = [jnp.sum(h, axis=0) for h in lanes]
                    m = by_col[0] + by_col[1]
                    off = float(bc * (kc - cb - 1))
                    x = by_col[0] * (sub + off) + by_col[1] * (sub + (off + 8.0))
                    if kb == 0 or kb == rb_n + 1:
                        gate = inside[0] if kb == 0 else inside[1]
                        m, y, x = m * gate, y * gate, x * gate
                    old = totals[rb, cb]
                    totals[rb, cb] = [old[0] + m, old[1] + y, old[2] + x]

    own_kbs = list(range(1, rb_n + 1))
    for kc in range(cb_n + 2):
        correlate(own_kbs, kc)

    relayed(1)
    far = br + rows + near
    lhs = [lhs2(0, near, bc, cols), lhs2(far, near, bc, cols)]
    y, to_right, to_left = taps(jnp.concatenate(lhs, axis=0), 2 * near, cols)
    for side in range(2):
        part = slice(side * near, (side + 1) * near)
        put_center(0 if side == 0 else far, y[part], to_right[part], to_left[part])

    def corners(starts):
        lhs = [lhs2(r, near, c, bc) for r in starts for c in (0, east)]
        y, to_right, to_left = taps(jnp.concatenate(lhs, axis=0), 4 * near, bc)
        for end, r in enumerate(starts):
            part = slice(2 * end * near, 2 * (end + 1) * near)
            put_sides(r, y[part], to_right[part], to_left[part])

    corners([near, br + rows])

    for band in range(2, len(bands)):
        relayed(band)
    for side in range(2):

        @pl.when(present(side))
        def _():
            for copy in lates[side]:
                copy.wait_recv()

    corners([0, far])
    total = 32 + rows
    for side in range(2):
        lhs = jnp.concatenate([late_r[side, :16], strip_r[side, rows:], late_r[side, 16:]], axis=0)
        z = [mm(lhs, wv[a, 2 * side]) for a in range(3)]
        h = z[1] + pltpu.roll(z[0], 1, 0) + pltpu.roll(z[2], total - 1, 0)
        lo, pick = (0, 0) if side == 0 else (east + 8, 7)
        for end in range(2):
            part = h[8:16] if end == 0 else h[16 + rows : 24 + rows]
            r = end * (br + rows)
            a2[r : r + br, lo : lo + 8] = a2[r : r + br, lo : lo + 8] + jnp.where(
                iota((br, 8, ch), 1) == pick, part[:, None, :], 0.0
            )
    for end in range(2):
        r = end * (br + rows)
        keys[r : r + br] = (a2[r : r + br] * inside[end]).astype(BF16)
    for kc in range(cb_n + 2):
        correlate([0], kc)
        correlate([rb_n + 1], kc)

    lane = iota((8, BLOCK), 1)
    sublane = iota((8, BLOCK), 0)
    qr, qc = lane >> 4, lane & 15
    for (rb, cb), (m, y, x) in totals.items():
        m, y, x = [jnp.sum(t, axis=0, keepdims=True) for t in (m, y, x)]
        fy = y / m - qr.astype(F32)
        fx = x / m - qc.astype(F32)
        both = jnp.where(sublane == 0, fy, fx) * float(UPSCALE)
        fb[rb + 1, cb + 1] = both

    flow_rows = [
        send(16, fb.at[1, pl.ds(1, cb_n)], fb.at[rb_n + 1, pl.ds(1, cb_n)], north),
        send(17, fb.at[rb_n, pl.ds(1, cb_n)], fb.at[0, pl.ds(1, cb_n)], south),
    ]
    flow_cols = [
        send(18, fb.at[pl.ds(1, rb_n), 1], fb.at[pl.ds(1, rb_n), cb_n + 1], left),
        send(19, fb.at[pl.ds(1, rb_n), cb_n], fb.at[pl.ds(1, rb_n), 0], right),
    ]
    flow_corners = {}
    for side in range(2):
        src_r, dst_r = (1, rb_n + 1) if side == 0 else (rb_n, 0)
        to = lat - 1 if side == 0 else lat + 1
        flow_corners[side] = [
            send(20 + 2 * side, fb.at[src_r, 1], fb.at[dst_r, cb_n + 1], (to, left[1])),
            send(21 + 2 * side, fb.at[src_r, cb_n], fb.at[dst_r, 0], (to, right[1])),
        ]
    for side in range(2):

        @pl.when(present(side))
        def _():
            for copy in flow_corners[side] + [flow_rows[side]]:
                copy.start()

    for copy in flow_cols:
        copy.start()
    loads[3].wait()
    p = iota((n_mask, n_mask), 0)
    want = (p - (p & 63)) + ((p & 7) << 3) + ((p >> 3) & 7)
    perm = (iota((n_mask, n_mask), 1) == want).astype(F32).astype(BF16)
    wp[...] = mm(perm, mv[...]).astype(BF16)

    for cb in range(cb_n):
        logits = mm_nt(wp[...], qs[cb]).reshape(9, UPSCALE * UPSCALE, rb_n * BLOCK)
        e = jnp.exp(logits)
        mix[cb] = e / jnp.sum(e, axis=0, keepdims=True)

    for copy in flow_cols:
        copy.wait_recv()
    for side in range(2):

        @pl.when(present(side))
        def _():
            for copy in flow_corners[1 - side] + [flow_rows[1 - side]]:
                copy.wait_recv()

    flows[...] = fb[...]

    for side in range(2):

        @pl.when(present(side))
        def _():
            for copy in lates[side] + [flow_rows[side]] + flow_corners[side]:
                copy.wait_send()
            for band in range(len(bands)):
                for copy in relays[band][side]:
                    copy.wait_send()

    for band in range(len(bands)):
        for side in range(2):

            @pl.when(goes_direct(side, band))
            def _():
                for copy in lat_sends[band][side]:
                    copy.wait_send()

        for side, (by, on) in enumerate(detours[band]):
            pl.when(by_way[side])(by.wait_send)
            pl.when(is_hub[side])(on.wait_send)

    for copy in strips + mains + earlies + flow_cols:
        copy.wait_send()


def upsample(mix, fb, out_hbm, out, sem):
    cb_n, rb_n = mix.shape[0], mix.shape[3] // BLOCK
    lane = iota((8, BLOCK), 1)
    qr, qc = lane >> 4, lane & 15
    k = iota((BLOCK, BLOCK), 0)
    weave = (iota((BLOCK, BLOCK), 1) == ((k & 15) << 3) + (k >> 4)).astype(F32).astype(BF16)

    copies = []
    for cb in range(cb_n):
        for rb in range(rb_n):
            shifted = {}
            for r in range(rb, rb + 3):
                mid = fb[r, cb + 1]
                shifted[r, 0] = jnp.where(
                    qc == 0, pltpu.roll(fb[r, cb], BLOCK - 15, 1), pltpu.roll(mid, 1, 1)
                )
                shifted[r, 1] = mid
                shifted[r, 2] = jnp.where(
                    qc == 15, pltpu.roll(fb[r, cb + 2], 15, 1), pltpu.roll(mid, BLOCK - 1, 1)
                )
            beside = []
            for a in range(3):
                for b in range(3):
                    here = shifted[rb + 1, b]
                    if a == 0:
                        here = pltpu.roll(jnp.where(qr == 7, shifted[rb, b], here), BLOCK_COLS, 1)
                    if a == 2:
                        here = pltpu.roll(
                            jnp.where(qr == 0, shifted[rb + 2, b], here), BLOCK - BLOCK_COLS, 1
                        )
                    beside.append(here)
            for d in range(2):
                up = jnp.zeros((UPSCALE * UPSCALE, BLOCK), F32)
                for n in range(9):
                    share = mix[cb, n, :, rb * BLOCK : (rb + 1) * BLOCK]
                    up = up + share * beside[n][d : d + 1]
                xs = [up[8 * j : 8 * j + 8] for j in range(8)]
                rowed = jnp.concatenate(swap_groups(xs, qr), axis=0)
                high = rowed.astype(BF16)
                rest = rowed - high.astype(F32)
                mid = rest.astype(BF16)
                low = (rest - mid.astype(F32)).astype(BF16)
                woven = mm(high, weave) + mm(mid, weave) + mm(low, weave)
                out[d, rb * 64 : (rb + 1) * 64, cb * BLOCK : (cb + 1) * BLOCK] = woven
                copies.append(
                    pltpu.make_async_copy(
                        out.at[d, pl.ds(rb * 64, 64), pl.ds(cb * BLOCK, BLOCK)],
                        out_hbm.at[d, pl.ds(rb * 64, 64), pl.ds(cb * BLOCK, BLOCK)],
                        sem.at[len(copies)],
                    )
                )
                copies[-1].start()
    for copy in copies:
        copy.wait()


def body(frame_one, frame_two, enc_weight, mask_weight):
    rows, cols, ch = frame_one.shape
    n_mask = mask_weight.shape[1]
    rb_n, cb_n = rows // BLOCK_ROWS, cols // BLOCK_COLS
    mix, fb = pl.pallas_call(
        kernel,
        out_shape=[
            jax.ShapeDtypeStruct((cb_n, 9, UPSCALE * UPSCALE, rb_n * BLOCK), F32),
            jax.ShapeDtypeStruct((rb_n + 2, cb_n + 2, 8, BLOCK), F32),
        ],
        in_specs=[pl.BlockSpec(memory_space=pltpu.HBM)] * 4,
        out_specs=[pl.BlockSpec(memory_space=pltpu.VMEM)] * 2,
        scratch_shapes=[
            pltpu.VMEM((rows + 2, cols, ch), BF16),
            pltpu.VMEM((rows + 2 * BLOCK_ROWS + 2, cols + 2 * BLOCK_COLS, ch), BF16),
            pltpu.VMEM(enc_weight.shape, BF16),
            pltpu.VMEM((n_mask, ch), BF16),
            pltpu.VMEM((n_mask, ch), BF16),
            pltpu.VMEM((rows, cols, ch), F32),
            pltpu.VMEM((rows + 2 * BLOCK_ROWS, cols + 2 * BLOCK_COLS, ch), F32),
            pltpu.VMEM((2, 2 * rows, ch), BF16),
            pltpu.VMEM((2, 2 * rows, ch), BF16),
            pltpu.VMEM((2, 16, ch), BF16),
            pltpu.VMEM((2, 16, ch), BF16),
            pltpu.VMEM((2, 32, ch), BF16),
            pltpu.VMEM((2, 32, ch), BF16),
            pltpu.VMEM((rows + 2 * BLOCK_ROWS, cols + 2 * BLOCK_COLS, ch), BF16),
            pltpu.VMEM((cb_n, rb_n * BLOCK, ch), BF16),
            pltpu.VMEM((rb_n + 2, cb_n + 2, 8, BLOCK), F32),
            pltpu.VMEM((BLOCK_ROWS, cols, ch), BF16),
            pltpu.SemaphoreType.DMA((4,)),
            pltpu.SemaphoreType.DMA((56,)),
            pltpu.SemaphoreType.DMA((56,)),
            pltpu.SemaphoreType.REGULAR,
        ],
        compiler_params=pltpu.CompilerParams(
            collective_id=0, has_side_effects=True, vmem_limit_bytes=32 * 2**20
        ),
        name="flow",
    )(*[pltpu.with_memory_space_constraint(a, pltpu.HBM) for a in (frame_one, frame_two, enc_weight, mask_weight.T)])
    shape = (2, rows * UPSCALE, cols * UPSCALE)
    return pl.pallas_call(
        upsample,
        out_shape=jax.ShapeDtypeStruct(shape, F32),
        in_specs=[pl.BlockSpec(memory_space=pltpu.VMEM)] * 2,
        out_specs=pl.BlockSpec(memory_space=pl.ANY),
        scratch_shapes=[
            pltpu.VMEM(shape, F32),
            pltpu.SemaphoreType.DMA((2 * rb_n * cb_n,)),
        ],
        compiler_params=pltpu.CompilerParams(vmem_limit_bytes=32 * 2**20),
        name="upsample",
    )(mix, fb)


def solution(mesh):
    in_specs = (P("lat", "lon", None), P("lat", "lon", None), P(), P())
    out_specs = P(None, "lat", "lon")
    return jax.shard_map(body, mesh=mesh, in_specs=in_specs, out_specs=out_specs, check_vma=False)
```

```python
import functools
import math

import jax
import jax.numpy as jnp
from jax import lax
from jax.experimental import pallas as pl
from jax.experimental.pallas import tpu as pltpu
from jax.sharding import PartitionSpec as P

BLOCK_ROWS = 8
BLOCK_COLS = 16
BLOCK = BLOCK_ROWS * BLOCK_COLS
UPSCALE = 8
F32 = jnp.float32
BF16 = jnp.bfloat16
MESH = pl.DeviceIdType.MESH


def iota(shape, axis):
    return lax.broadcasted_iota(jnp.int32, shape, axis)


def mm(a, b):
    return jnp.dot(a, b, preferred_element_type=F32)


def mm_nt(a, b):
    return lax.dot_general(a, b, (((1,), (1,)), ((), ())), preferred_element_type=F32)


def swap_groups(xs, lane_group):
    xs = list(xs)
    for bit in (1, 2, 4):
        mask = (lane_group & bit) != 0
        shift = bit * BLOCK_COLS
        for a in range(8):
            if a & bit:
                continue
            lo, hi = xs[a], xs[a | bit]
            xs[a] = jnp.where(mask, pltpu.roll(hi, shift, 1), lo)
            xs[a | bit] = jnp.where(mask, hi, pltpu.roll(lo, BLOCK - shift, 1))
    return xs


def parts(x):
    high = x.astype(BF16)
    rest = x - high.astype(F32)
    mid = rest.astype(BF16)
    return high, mid, (rest - mid.astype(F32)).astype(BF16)


def weaving():
    k = iota((BLOCK, BLOCK), 0)
    hit = iota((BLOCK, BLOCK), 1) == ((k & (BLOCK_COLS - 1)) << 3) + (k >> 4)
    return hit.astype(F32).astype(BF16)


def by_rows(x, qr):
    return jnp.concatenate(swap_groups([x[8 * j : 8 * j + 8] for j in range(8)], qr), axis=0)


def beside_cols(west, mid, east, qc):
    return [
        jnp.where(qc == 0, pltpu.roll(west, BLOCK - (BLOCK_COLS - 1), 1), pltpu.roll(mid, 1, 1)),
        mid,
        jnp.where(qc == BLOCK_COLS - 1, pltpu.roll(east, BLOCK_COLS - 1, 1), pltpu.roll(mid, BLOCK - 1, 1)),
    ]


def kernel(
    f1, f2, w_hbm, mw_hbm, base, rim_corner, flows,
    g1, g2, wv, mv, wp, a1, a2, strip_s, strip_r, early_s, early_r, late_s, late_r, keys, qs, fb, transit, mix, rim_ns, rim_we, widen, hits,
    lsem, ssem, rsem, ready,
):
    rows, cols, ch = f1.shape
    br, bc = BLOCK_ROWS, BLOCK_COLS
    rb_n, cb_n = rows // br, cols // bc
    n_mask = mw_hbm.shape[0]
    rim = br + 1
    lat, lon = lax.axis_index("lat"), lax.axis_index("lon")
    nlat, nlon = lax.axis_size("lat"), lax.axis_size("lon")
    has_n, has_s = lat > 0, lat < nlat - 1
    left = (lat, lax.rem(lon + nlon - 1, nlon))
    right = (lat, lax.rem(lon + 1, nlon))
    north, south = (lat - 1, lon), (lat + 1, lon)

    barrier = pltpu.get_barrier_semaphore()

    def greet(peer):
        pl.semaphore_signal(barrier, inc=1, device_id=peer, device_id_type=MESH)

    first, last = lon == 0, lon == nlon - 1
    greet(left)
    pl.when(jnp.logical_not(last))(lambda: greet(right))
    pl.when(has_n)(lambda: greet(north))
    pl.when(has_s)(lambda: greet(south))

    odd = (lax.rem(lon, 2) == 1) & (nlat == 4)
    by_way = [odd & (lat == 2), odd & (lat == 1)]
    is_hub = [odd & (lat == 0), odd & (lat == 3)]
    hubs, ends = [(0, lon), (3, lon)], [(1, lon), (2, lon)]
    for side in range(2):
        pl.when(is_hub[side])(lambda: greet(ends[1 - side]))

    own = pl.ds(rim, rows)
    loads = [
        pltpu.make_async_copy(f1, g1.at[pl.ds(1, rows)], lsem.at[0]),
        pltpu.make_async_copy(f2, g2.at[own, pl.ds(bc, cols)], lsem.at[1]),
        pltpu.make_async_copy(w_hbm, wv, lsem.at[2]),
        pltpu.make_async_copy(mw_hbm, mv, lsem.at[3]),
    ]
    for load in loads:
        load.start()

    def absent(side):
        return jnp.logical_not(has_n if side == 0 else has_s)

    def present(side):
        return has_n if side == 0 else has_s

    def send(k, src, dst, peer, arrive_k=None):
        return pltpu.make_async_remote_copy(
            src_ref=src, dst_ref=dst, send_sem=ssem.at[k],
            recv_sem=rsem.at[k if arrive_k is None else arrive_k],
            device_id=peer, device_id_type=MESH,
        )

    bands = [(0, 1), (1, 4), (5, 2), (7, 2)]

    def band_at(side, band):
        off, n = bands[band]
        return (rim - off - n if side == 0 else rim + rows + off), n

    def row_send(k, side, band):
        off, n = bands[band]
        src = off if side == 0 else rows - off - n
        dst, _ = band_at(1 - side, band)
        peer = north if side == 0 else south
        return send(k, f2.at[pl.ds(src, n)], g2.at[pl.ds(dst, n), pl.ds(bc, cols)], peer)

    lat_sends = [
        [
            [
                send(side, f1.at[0 if side == 0 else rows - 1],
                     g1.at[rows + 1 if side == 0 else 0], north if side == 0 else south),
                row_send(2 + side, side, 0),
            ]
            for side in range(2)
        ],
    ]
    for band in range(1, len(bands)):
        lat_sends.append([[row_send(2 + 2 * band + side, side, band)] for side in range(2)])
    def detour(band, side):
        off, n = bands[band]
        k = 46 + 4 * (band - 1) + 2 * side
        src = off if side == 0 else rows - off - n
        at = transit.at[pl.ds(off - 1, n)]
        dst, _ = band_at(1 - side, band)
        into = g2.at[pl.ds(dst, n), pl.ds(bc, cols)]
        return (
            send(k, f2.at[pl.ds(src, n)], at, hubs[side]),
            send(k + 1, at, into, ends[side], 2 + 2 * band + side),
        )

    detours = [[]] + [[detour(band, side) for side in range(2)] for band in range(1, len(bands))]

    def goes_direct(side, band):
        if band == 0:
            return present(side)
        return present(side) & jnp.logical_not(by_way[side])

    mains = [
        send(44, f2.at[:, pl.ds(0, bc)], g2.at[own, pl.ds(bc + cols, bc)], left),
        send(45, f2.at[:, pl.ds(cols - bc, bc)], g2.at[own, pl.ds(0, bc)], right),
    ]
    strips = [
        send(10, strip_s.at[0], strip_r.at[1], left),
        send(11, strip_s.at[1], strip_r.at[0], right),
    ]
    earlies = [
        send(12, early_s.at[0], early_r.at[1], left),
        send(13, early_s.at[1], early_r.at[0], right),
    ]

    def relay(k, side, band):
        at, n = band_at(side, band)
        r = pl.ds(at, n)
        return [
            send(k, g2.at[r, pl.ds(bc, bc)], g2.at[r, pl.ds(bc + cols, bc)], left),
            send(k + 1, g2.at[r, pl.ds(cols, bc)], g2.at[r, pl.ds(0, bc)], right),
        ]

    relays = [[relay(24 + 4 * band + 2 * side, side, band) for side in range(2)] for band in range(len(bands))]
    lates = [
        send(40, late_s.at[0], late_r.at[1], left),
        send(41, late_s.at[1], late_r.at[0], right),
    ]

    for side in range(2):

        @pl.when(absent(side))
        def _():
            g1[0 if side == 0 else rows + 1] = jnp.zeros((cols, ch), BF16)
            lo = 0 if side == 0 else rim + rows
            g2[lo : lo + rim] = jnp.zeros((rim,) + g2.shape[1:], BF16)
            at = 0 if side == 0 else rb_n + 1
            fb[at] = jnp.zeros(fb.shape[1:], F32)

    met = [jnp.logical_not(first), has_n, has_s, by_way[0] | by_way[1]]
    pl.semaphore_wait(barrier, 1 + sum(m.astype(jnp.int32) for m in met))

    @pl.when(last)
    def _():
        pl.semaphore_signal(ready, inc=1, device_id=right, device_id_type=MESH)

    for band in range(len(bands)):
        for side, (by, _) in enumerate(detours[band]):
            pl.when(by_way[side])(by.start)
        for side in range(2):

            @pl.when(goes_direct(side, band))
            def _():
                for copy in lat_sends[band][side]:
                    copy.start()

    mains[1].start()
    pl.when(jnp.logical_not(first))(mains[0].start)
    loads[0].wait()
    loads[1].wait()

    def pick_col(tile, pick):
        return jnp.sum(jnp.where(iota(tile.shape, 1) == pick, tile.astype(F32), 0.0), axis=1)

    for side in range(2):
        lo, pick = (0, 0) if side == 0 else (cols - bc, bc - 1)
        strip_s[side, :rows] = pick_col(g1[1 : rows + 1, lo : lo + bc, :], pick).astype(BF16)
        lo, pick = (2 * bc, 0) if side == 0 else (cols - bc, bc - 1)
        strip_s[side, rows:] = pick_col(g2[rim : rim + rows, lo : lo + bc, :], pick).astype(BF16)
    strips[1].start()
    pl.when(jnp.logical_not(first))(strips[0].start)

    loads[2].wait()


    def taps(lhs, n, w):
        ys = [mm(lhs, wv[:, b].reshape(3 * ch, ch)) for b in range(3)]
        t0 = pltpu.roll(ys[0], 1, 0).reshape(n, w, ch)
        t2 = pltpu.roll(ys[2], n * w - 1, 0).reshape(n, w, ch)
        at = iota((n, w, ch), 1)
        y = ys[1].reshape(n, w, ch) + jnp.where(at == 0, 0.0, t0) + jnp.where(at == w - 1, 0.0, t2)
        edge = iota((n, 8, ch), 1)
        to_right = jnp.concatenate([t0[1:, :8], t0[:1, :8]], axis=0)
        to_left = jnp.concatenate([t2[n - 1 :, w - 8 :], t2[: n - 1, w - 8 :]], axis=0)
        return y, jnp.where(edge == 0, to_right, 0.0), jnp.where(edge == 7, to_left, 0.0)

    def lhs1(r, n):
        return jnp.concatenate([g1[r + a : r + a + n].reshape(n * cols, ch) for a in range(3)], axis=1)

    def lhs2(r, n, c, w):
        return jnp.concatenate(
            [g2[r + a : r + a + n, c : c + w, :].reshape(n * w, ch) for a in range(3)], axis=1
        )

    east = bc + cols

    def put_center(r, y, to_right, to_left):
        n = y.shape[0]
        a2[r : r + n, bc:east] = y
        a2[r : r + n, east : east + 8] = to_right
        a2[r : r + n, bc - 8 : bc] = to_left

    inner = rows - 2
    y, _, _ = taps(lhs1(1, inner), inner, cols)
    a1[1 : rows - 1] = y
    put_center(br + 1, *taps(lhs2(br + 1, inner, bc, cols), inner, cols))

    @pl.when(first)
    def _():
        pl.semaphore_wait(ready, 1)
        strips[0].start()
        mains[0].start()

    def arrive(band):
        for side in range(2):

            @pl.when(present(side))
            def _():
                for copy in lat_sends[band][1 - side]:
                    copy.wait_recv()

    def pass_on(band):
        for side in range(2):

            @pl.when(present(side))
            def _():
                for copy in relays[band][side]:
                    copy.start()

    def forward(band):
        for side, (by, on) in enumerate(detours[band]):

            @pl.when(is_hub[side])
            def _():
                by.wait_recv()
                on.start()

    arrive(0)
    pass_on(0)
    at_row, at_key = iota((16, 64), 0), iota((16, 64), 1)
    for side in range(2):
        c1, p1 = (0, 0) if side == 0 else (cols - bc, bc - 1)
        c2, p2 = (2 * bc, 0) if side == 0 else (cols - bc, bc - 1)
        tiles = [g1[r, c1 : c1 + bc, :] for r in (0, rows + 1)]
        tiles += [g2[r, c2 : c2 + bc, :] for r in (rim - 1, rim + rows)]
        hit = jnp.where(at_row < 2, p1, p2) + at_row * bc == at_key
        early_s[side] = mm(hit.astype(F32).astype(BF16), jnp.concatenate(tiles, axis=0)).astype(BF16)
    for copy in earlies:
        copy.start()

    for band in range(1, len(bands)):
        forward(band)
    arrive(1)
    pass_on(1)

    near = br // 2
    last_row = br + rows - 1
    lhs = [lhs2(near, near + 1, bc, cols), lhs2(last_row, near + 1, bc, cols), lhs1(0, 1), lhs1(rows - 1, 1)]
    y, to_right, to_left = taps(jnp.concatenate(lhs, axis=0), 2 * near + 4, cols)
    for side in range(2):
        part = slice(side * (near + 1), (side + 1) * (near + 1))
        put_center(near if side == 0 else last_row, y[part], to_right[part], to_left[part])
    a1[0] = y[2 * near + 2]
    a1[rows - 1] = y[2 * near + 3]

    for band in range(2, len(bands)):
        arrive(band)
        pass_on(band)
    at_row, at_key = iota((2 * br, 2 * rim * bc), 0), iota((2 * br, 2 * rim * bc), 1)
    held = jnp.where(at_row < br, at_row, at_row + 2)
    for side in range(2):
        c, pick = (2 * bc, 0) if side == 0 else (cols - bc, bc - 1)
        tiles = [g2[r : r + rim, c : c + bc, :].reshape(rim * bc, ch) for r in (0, rim + rows)]
        hit = (held * bc + pick == at_key).astype(F32).astype(BF16)
        late_s[side] = mm(hit, jnp.concatenate(tiles, axis=0)).astype(BF16)
    for copy in lates:
        copy.start()

    for copy in strips + mains + earlies:
        copy.wait_recv()

    def relayed(band):
        for side in range(2):

            @pl.when(present(side))
            def _():
                for copy in relays[band][side]:
                    copy.wait_recv()

    relayed(0)

    def put_sides(r, y, to_right, to_left, spread=None):
        n = y.shape[0] // 2
        outer = [y[:n, :8], y[n:, 8:]]
        if spread is not None:
            outer = [o + h for o, h in zip(outer, spread)]
        a2[r : r + n, :8] = outer[0]
        a2[r : r + n, 8:bc] = a2[r : r + n, 8:bc] + y[:n, 8:]
        a2[r : r + n, east : east + 8] = a2[r : r + n, east : east + 8] + y[n:, :8]
        a2[r : r + n, east + 8 :] = outer[1]
        a2[r : r + n, bc : bc + 8] = a2[r : r + n, bc : bc + 8] + to_right[:n]
        a2[r : r + n, east - 8 : east] = a2[r : r + n, east - 8 : east] + to_left[n:]

    row_id = iota((rows, ch), 0)
    spreads = []
    for side in range(2):
        lhs = jnp.concatenate([strip_r[side], early_r[side]], axis=0)
        z = [mm(lhs, wv[a, 2 * side]) for a in range(3)]
        for f in range(2):
            mid = [z[a][f * rows : (f + 1) * rows] for a in range(3)]
            e = 2 * rows + 2 * f
            h = mid[1] + jnp.where(row_id == 0, z[0][e : e + 1], pltpu.roll(mid[0], 1, 0))
            h = h + jnp.where(row_id == rows - 1, z[2][e + 1 : e + 2], pltpu.roll(mid[2], rows - 1, 0))
            lo, pick = (0, 0) if side == 0 else (cols - 8, 7)
            spread = jnp.where(iota((rows, 8, ch), 1) == pick, h[:, None, :], 0.0)
            if f == 0:
                a1[:, lo : lo + 8, :] = a1[:, lo : lo + 8, :] + spread
            else:
                spreads.append(spread)

    for cb in range(cb_n):
        for rb in range(rb_n):
            block = a1[rb * br : (rb + 1) * br, cb * bc : (cb + 1) * bc, :]
            qs[cb, rb * BLOCK : (rb + 1) * BLOCK] = block.astype(BF16).reshape(BLOCK, ch)

    lhs = [lhs2(br, rows, 0, bc), lhs2(br, rows, east, bc)]
    put_sides(br, *taps(jnp.concatenate(lhs, axis=0), 2 * rows, bc), spreads)
    keys[br : br + rows] = a2[br : br + rows].astype(BF16)

    scale = 1.0 / math.sqrt(ch)
    inside = [has_n.astype(F32), has_s.astype(F32)]
    zero = jnp.zeros((8, BLOCK), F32)
    totals = {(rb, cb): [zero, zero, zero] for rb in range(rb_n) for cb in range(cb_n)}
    sub = iota((8, BLOCK), 0).astype(F32)

    def correlate(kbs, kc):
        part = keys[kbs[0] * br : (kbs[-1] + 1) * br, kc * bc : (kc + 1) * bc, :]
        part = part.reshape(len(kbs) * BLOCK, ch)
        for cb in range(max(0, kc - 2), min(cb_n, kc + 1)):
            rbs = [rb for rb in range(rb_n) if any(0 <= kb - rb <= 2 for kb in kbs)]
            r0 = rbs[0]
            s = mm_nt(part, qs[cb, r0 * BLOCK : (rbs[-1] + 1) * BLOCK])
            for at, kb in enumerate(kbs):
                for rb in rbs:
                    if not 0 <= kb - rb <= 2:
                        continue
                    e = s[at * BLOCK : (at + 1) * BLOCK, (rb - r0) * BLOCK : (rb - r0 + 1) * BLOCK]
                    e = jnp.exp(e * scale).reshape(br, 2, 8, BLOCK)
                    lanes = [e[:, h] for h in range(2)]
                    by_row = lanes[0] + lanes[1]
                    y = by_row[0] * float(br * (kb - rb - 1))
                    for kr in range(1, br):
                        y = y + by_row[kr] * float(br * (kb - rb - 1) + kr)
                    by_col = [jnp.sum(h, axis=0) for h in lanes]
                    m = by_col[0] + by_col[1]
                    off = float(bc * (kc - cb - 1))
                    x = by_col[0] * (sub + off) + by_col[1] * (sub + (off + 8.0))
                    if kb == 0 or kb == rb_n + 1:
                        gate = inside[0] if kb == 0 else inside[1]
                        m, y, x = m * gate, y * gate, x * gate
                    old = totals[rb, cb]
                    totals[rb, cb] = [old[0] + m, old[1] + y, old[2] + x]

    own_kbs = list(range(1, rb_n + 1))
    for kc in range(cb_n + 2):
        correlate(own_kbs, kc)

    relayed(1)
    far = br + rows + near
    lhs = [lhs2(0, near, bc, cols), lhs2(far, near, bc, cols)]
    y, to_right, to_left = taps(jnp.concatenate(lhs, axis=0), 2 * near, cols)
    for side in range(2):
        part = slice(side * near, (side + 1) * near)
        put_center(0 if side == 0 else far, y[part], to_right[part], to_left[part])

    def corners(starts):
        lhs = [lhs2(r, near, c, bc) for r in starts for c in (0, east)]
        y, to_right, to_left = taps(jnp.concatenate(lhs, axis=0), 4 * near, bc)
        for end, r in enumerate(starts):
            part = slice(2 * end * near, 2 * (end + 1) * near)
            put_sides(r, y[part], to_right[part], to_left[part])

    corners([near, br + rows])

    for band in range(2, len(bands)):
        relayed(band)
    for copy in lates:
        copy.wait_recv()

    corners([0, far])
    at8 = iota((br, ch), 0)
    for side in range(2):
        lhs = jnp.concatenate([late_r[side], early_r[side], strip_r[side, rows:]], axis=0)
        z = [mm(lhs, wv[a, 2 * side]) for a in range(3)]
        far_n, far_s = [x[:br] for x in z], [x[br : 2 * br] for x in z]
        by_n, by_s = [x[2 * br + 2 : 2 * br + 3] for x in z], [x[2 * br + 3 : 2 * br + 4] for x in z]
        own_n, own_s = z[2][4 * br : 4 * br + 1], z[0][4 * br + rows - 1 : 4 * br + rows]
        h_n = far_n[0] + jnp.where(at8 == br - 1, by_n[1], pltpu.roll(far_n[1], br - 1, 0))
        nxt = jnp.where(at8 == br - 2, by_n[2], pltpu.roll(far_n[2], br - 2, 0))
        h_n = h_n + jnp.where(at8 == br - 1, own_n, nxt)
        h_s = far_s[2] + jnp.where(at8 == 0, by_s[1], pltpu.roll(far_s[1], 1, 0))
        nxt = jnp.where(at8 == 1, by_s[0], pltpu.roll(far_s[0], 2, 0))
        h_s = h_s + jnp.where(at8 == 0, own_s, nxt)
        lo, pick = (0, 0) if side == 0 else (east + 8, 7)
        for end in range(2):
            part = h_n if end == 0 else h_s
            r = end * (br + rows)
            a2[r : r + br, lo : lo + 8] = a2[r : r + br, lo : lo + 8] + jnp.where(
                iota((br, 8, ch), 1) == pick, part[:, None, :], 0.0
            )
    for end in range(2):
        r = end * (br + rows)
        keys[r : r + br] = (a2[r : r + br] * inside[end]).astype(BF16)
    for kc in range(cb_n + 2):
        correlate([0], kc)
        correlate([rb_n + 1], kc)

    lane = iota((8, BLOCK), 1)
    sublane = iota((8, BLOCK), 0)
    qr, qc = lane >> 4, lane & 15
    for (rb, cb), (m, y, x) in totals.items():
        m, y, x = [jnp.sum(t, axis=0, keepdims=True) for t in (m, y, x)]
        fy = y / m - qr.astype(F32)
        fx = x / m - qc.astype(F32)
        both = jnp.where(sublane == 0, fy, fx) * float(UPSCALE)
        fb[rb + 1, cb + 1] = both

    flow_rows = [
        send(16, fb.at[1, pl.ds(1, cb_n)], fb.at[rb_n + 1, pl.ds(1, cb_n)], north),
        send(17, fb.at[rb_n, pl.ds(1, cb_n)], fb.at[0, pl.ds(1, cb_n)], south),
    ]
    flow_cols = [
        send(18, fb.at[pl.ds(1, rb_n), 1], fb.at[pl.ds(1, rb_n), cb_n + 1], left),
        send(19, fb.at[pl.ds(1, rb_n), cb_n], fb.at[pl.ds(1, rb_n), 0], right),
    ]
    flow_corners = {}
    for side in range(2):
        src_r, dst_r = (1, rb_n + 1) if side == 0 else (rb_n, 0)
        to = lat - 1 if side == 0 else lat + 1
        flow_corners[side] = [
            send(20 + 2 * side, fb.at[src_r, 1], fb.at[dst_r, cb_n + 1], (to, left[1])),
            send(21 + 2 * side, fb.at[src_r, cb_n], fb.at[dst_r, 0], (to, right[1])),
        ]
    for side in range(2):

        @pl.when(present(side))
        def _():
            for copy in flow_corners[side] + [flow_rows[side]]:
                copy.start()

    for copy in flow_cols:
        copy.start()
    loads[3].wait()
    p = iota((n_mask, n_mask), 0)
    want = (p - (p & 63)) + ((p & 7) << 3) + ((p >> 3) & 7)
    perm = (iota((n_mask, n_mask), 1) == want).astype(F32).astype(BF16)
    wp[...] = mm(perm, mv[...]).astype(BF16)

    for cb in range(cb_n):
        logits = mm_nt(wp[...], qs[cb]).reshape(9, UPSCALE * UPSCALE, rb_n * BLOCK)
        e = jnp.exp(logits)
        mix[cb] = e / jnp.sum(e, axis=0, keepdims=True)

    weave = weaving()

    def woven(x):
        return sum(mm(p, weave) for p in parts(x))

    none = jnp.zeros((8, BLOCK), F32)
    own_fb = {(r, c): fb[r, c] for r in range(1, rb_n + 1) for c in range(1, cb_n + 1)}

    def at_block(r, c):
        return own_fb.get((r, c), none)

    for cb in range(cb_n):
        for rb in range(rb_n):
            shifted = {
                r: beside_cols(at_block(r, cb), at_block(r, cb + 1), at_block(r, cb + 2), qc)
                for r in range(rb, rb + 3)
            }
            beside = []
            for a in range(3):
                for b in range(3):
                    here = shifted[rb + 1][b]
                    if a == 0:
                        here = pltpu.roll(jnp.where(qr == br - 1, shifted[rb][b], here), bc, 1)
                    if a == 2:
                        here = pltpu.roll(jnp.where(qr == 0, shifted[rb + 2][b], here), BLOCK - bc, 1)
                    beside.append(here)
            for d in range(2):
                up = jnp.zeros((UPSCALE * UPSCALE, BLOCK), F32)
                for n in range(9):
                    up = up + mix[cb, n, :, rb * BLOCK : (rb + 1) * BLOCK] * beside[n][d : d + 1]
                base[d, rb * 64 : (rb + 1) * 64, cb * BLOCK : (cb + 1) * BLOCK] = woven(by_rows(up, qr))

    def share(rb, cb, n):
        return by_rows(mix[cb, n, :, rb * BLOCK : (rb + 1) * BLOCK], qr)

    tops = [share(0, cb, b)[:8] for b in range(3) for cb in range(cb_n)]
    tops += [share(rb_n - 1, cb, 6 + b)[56:] for b in range(3) for cb in range(cb_n)]
    tops = woven(jnp.concatenate(tops, axis=0))
    for side in range(2):
        for b in range(3):
            for cb in range(cb_n):
                k = 8 * ((side * 3 + b) * cb_n + cb)
                rim_ns[side, b, :, cb * BLOCK : (cb + 1) * BLOCK] = tops[k : k + 8]
    lanes = iota((64, BLOCK), 1)
    for side in range(2):
        keep = lanes < UPSCALE if side == 0 else lanes >= BLOCK - UPSCALE
        for a in range(3):
            for rb in range(rb_n):
                x = woven(share(rb, 0 if side == 0 else cb_n - 1, 3 * a + 2 * side))
                rim_we[side, a, rb * 64 : (rb + 1) * 64] = jnp.where(keep, x, 0.0)
        at = 0 if side == 0 else cb_n - 1
        for end in range(2):
            k = 8 * ((end * 3 + 2 * side) * cb_n + at)
            rim_corner[end, side] = jnp.where(keep[:8], tops[k : k + 8], 0.0)

    k = iota((BLOCK, BLOCK), 0)
    widen[...] = (k == BLOCK - bc + (iota((BLOCK, BLOCK), 1) >> 3)).astype(F32).astype(BF16)
    high = rows * UPSCALE
    for a in range(3):
        want = ((iota((high, rb_n * BLOCK), 0) >> 3) + (a - 1)) * bc + (bc - 1)
        hit = iota((high, rb_n * BLOCK), 1) == want
        hits[a * high : (a + 1) * high] = hit.astype(F32).astype(BF16)

    for copy in flow_cols:
        copy.wait_recv()
    west = [fb[r, 0] for r in range(1, rb_n + 1)]
    eastern = [pltpu.roll(fb[r, cb_n + 1], bc - 1, 1) for r in range(1, rb_n + 1)]
    sides = jnp.concatenate([jnp.concatenate(x, axis=1) for x in (west, eastern)], axis=0)
    tall = sum(mm_nt(hits[...], p) for p in parts(sides))
    for side in range(2):
        cc = slice(0, BLOCK) if side == 0 else slice((cb_n - 1) * BLOCK, cb_n * BLOCK)
        for d in range(2):
            y = base[d, :, cc]
            for a in range(3):
                y = y + rim_we[side, a] * tall[a * high : (a + 1) * high, 8 * side + d : 8 * side + d + 1]
            base[d, :, cc] = y

    for side in range(2):
        pl.when(present(side))(flow_rows[1 - side].wait_recv)
    cells = []
    for side in range(2):
        r = 0 if side == 0 else rb_n + 1
        at_c = [none] + [fb[r, c] for c in range(1, cb_n + 1)] + [none]
        near_by = [beside_cols(*at_c[cb : cb + 3], qc) for cb in range(cb_n)]
        if side == 1:
            near_by = [[pltpu.roll(x, BLOCK - bc, 1) for x in xs] for xs in near_by]
        cells += [near_by[cb][b] for b in range(3) for cb in range(cb_n)]
    wide = sum(mm(p, widen[...]) for p in parts(jnp.concatenate(cells, axis=0)))
    for d in range(2):
        for side in range(2):
            edge = slice(0, 8) if side == 0 else slice(high - 8, high)
            for cb in range(cb_n):
                cc = slice(cb * BLOCK, (cb + 1) * BLOCK)
                y = base[d, edge, cc]
                for b in range(3):
                    k = 8 * ((side * 3 + b) * cb_n + cb) + d
                    y = y + rim_ns[side, b, :, cc] * wide[k : k + 1]
                base[d, edge, cc] = y

    for side in range(2):

        @pl.when(present(side))
        def _():
            for copy in flow_corners[1 - side]:
                copy.wait_recv()

    flows[...] = fb[...]

    for side in range(2):

        @pl.when(present(side))
        def _():
            for copy in [flow_rows[side]] + flow_corners[side]:
                copy.wait_send()
            for band in range(len(bands)):
                for copy in relays[band][side]:
                    copy.wait_send()

    for band in range(len(bands)):
        for side in range(2):

            @pl.when(goes_direct(side, band))
            def _():
                for copy in lat_sends[band][side]:
                    copy.wait_send()

        for side, (by, on) in enumerate(detours[band]):
            pl.when(by_way[side])(by.wait_send)
            pl.when(is_hub[side])(on.wait_send)

    for copy in strips + mains + earlies + lates + flow_cols:
        copy.wait_send()


def add_corners(base, rim_corner, fb, out_hbm, out, sem):
    rb_n, cb_n = fb.shape[0] - 2, fb.shape[1] - 2
    high = base.shape[1]
    edges = [slice(0, 8), slice(high - 8, high)]
    copies = [
        pltpu.make_async_copy(
            base.at[:, pl.ds(8, high - 16)], out_hbm.at[:, pl.ds(8, high - 16)], sem.at[2]
        )
    ]
    copies[0].start()
    for end in range(2):
        for d in range(2):
            out[end, d] = base[d, edges[end], :]
            for side in range(2):
                at = slice(0, BLOCK) if side == 0 else slice((cb_n - 1) * BLOCK, cb_n * BLOCK)
                lane = (BLOCK - BLOCK_COLS) * (1 - end) + (BLOCK_COLS - 1) * (1 - side)
                x = fb[end * (rb_n + 1), side * (cb_n + 1)][d : d + 1, lane : lane + 1]
                out[end, d, :, at] = out[end, d, :, at] + rim_corner[end, side] * x
        copies.append(
            pltpu.make_async_copy(out.at[end], out_hbm.at[:, pl.ds(end * (high - 8), 8)], sem.at[end])
        )
        copies[-1].start()
    for copy in copies:
        copy.wait()


def body(frame_one, frame_two, enc_weight, mask_weight):
    rows, cols, ch = frame_one.shape
    n_mask = mask_weight.shape[1]
    rb_n, cb_n = rows // BLOCK_ROWS, cols // BLOCK_COLS
    shape = (2, rows * UPSCALE, cols * UPSCALE)
    held = pl.pallas_call(
        kernel,
        out_shape=[
            jax.ShapeDtypeStruct(shape, F32),
            jax.ShapeDtypeStruct((2, 2, UPSCALE, BLOCK), F32),
            jax.ShapeDtypeStruct((rb_n + 2, cb_n + 2, 8, BLOCK), F32),
        ],
        in_specs=[pl.BlockSpec(memory_space=pltpu.HBM)] * 4,
        out_specs=[pl.BlockSpec(memory_space=pltpu.VMEM)] * 3,
        scratch_shapes=[
            pltpu.VMEM((rows + 2, cols, ch), BF16),
            pltpu.VMEM((rows + 2 * BLOCK_ROWS + 2, cols + 2 * BLOCK_COLS, ch), BF16),
            pltpu.VMEM(enc_weight.shape, BF16),
            pltpu.VMEM((n_mask, ch), BF16),
            pltpu.VMEM((n_mask, ch), BF16),
            pltpu.VMEM((rows, cols, ch), F32),
            pltpu.VMEM((rows + 2 * BLOCK_ROWS, cols + 2 * BLOCK_COLS, ch), F32),
            pltpu.VMEM((2, 2 * rows, ch), BF16),
            pltpu.VMEM((2, 2 * rows, ch), BF16),
            pltpu.VMEM((2, 16, ch), BF16),
            pltpu.VMEM((2, 16, ch), BF16),
            pltpu.VMEM((2, 2 * BLOCK_ROWS, ch), BF16),
            pltpu.VMEM((2, 2 * BLOCK_ROWS, ch), BF16),
            pltpu.VMEM((rows + 2 * BLOCK_ROWS, cols + 2 * BLOCK_COLS, ch), BF16),
            pltpu.VMEM((cb_n, rb_n * BLOCK, ch), BF16),
            pltpu.VMEM((rb_n + 2, cb_n + 2, 8, BLOCK), F32),
            pltpu.VMEM((BLOCK_ROWS, cols, ch), BF16),
            pltpu.VMEM((cb_n, 9, UPSCALE * UPSCALE, rb_n * BLOCK), F32),
            pltpu.VMEM((2, 3, UPSCALE, cols * UPSCALE), F32),
            pltpu.VMEM((2, 3, rows * UPSCALE, BLOCK), F32),
            pltpu.VMEM((BLOCK, BLOCK), BF16),
            pltpu.VMEM((3 * rows * UPSCALE, rb_n * BLOCK), BF16),
            pltpu.SemaphoreType.DMA((4,)),
            pltpu.SemaphoreType.DMA((64,)),
            pltpu.SemaphoreType.DMA((64,)),
            pltpu.SemaphoreType.REGULAR,
        ],
        compiler_params=pltpu.CompilerParams(
            collective_id=0, has_side_effects=True, vmem_limit_bytes=32 * 2**20
        ),
        name="flow",
    )(*[pltpu.with_memory_space_constraint(a, pltpu.HBM) for a in (frame_one, frame_two, enc_weight, mask_weight.T)])
    return pl.pallas_call(
        add_corners,
        out_shape=jax.ShapeDtypeStruct(shape, F32),
        in_specs=[pl.BlockSpec(memory_space=pltpu.VMEM)] * 3,
        out_specs=pl.BlockSpec(memory_space=pl.ANY),
        scratch_shapes=[
            pltpu.VMEM((2, 2, UPSCALE, cols * UPSCALE), F32),
            pltpu.SemaphoreType.DMA((3,)),
        ],
        compiler_params=pltpu.CompilerParams(vmem_limit_bytes=32 * 2**20),
        name="add_corners",
    )(*held)


def solution(mesh):
    in_specs = (P("lat", "lon", None), P("lat", "lon", None), P(), P())
    out_specs = P(None, "lat", "lon")
    return jax.shard_map(body, mesh=mesh, in_specs=in_specs, out_specs=out_specs, check_vma=False)
```

```python
import functools
import math

import jax
import jax.numpy as jnp
from jax import lax
from jax.experimental import pallas as pl
from jax.experimental.pallas import tpu as pltpu
from jax.sharding import PartitionSpec as P

BLOCK_ROWS = 8
BLOCK_COLS = 16
BLOCK = BLOCK_ROWS * BLOCK_COLS
UPSCALE = 8
F32 = jnp.float32
BF16 = jnp.bfloat16
MESH = pl.DeviceIdType.MESH


def iota(shape, axis):
    return lax.broadcasted_iota(jnp.int32, shape, axis)


def mm(a, b):
    return jnp.dot(a, b, preferred_element_type=F32)


def mm_nt(a, b):
    return lax.dot_general(a, b, (((1,), (1,)), ((), ())), preferred_element_type=F32)


def swap_groups(xs, lane_group):
    xs = list(xs)
    for bit in (1, 2, 4):
        mask = (lane_group & bit) != 0
        shift = bit * BLOCK_COLS
        for a in range(8):
            if a & bit:
                continue
            lo, hi = xs[a], xs[a | bit]
            xs[a] = jnp.where(mask, pltpu.roll(hi, shift, 1), lo)
            xs[a | bit] = jnp.where(mask, hi, pltpu.roll(lo, BLOCK - shift, 1))
    return xs


def parts(x):
    high = x.astype(BF16)
    rest = x - high.astype(F32)
    mid = rest.astype(BF16)
    return high, mid, (rest - mid.astype(F32)).astype(BF16)


def weaving():
    k = iota((BLOCK, BLOCK), 0)
    hit = iota((BLOCK, BLOCK), 1) == ((k & (BLOCK_COLS - 1)) << 3) + (k >> 4)
    return hit.astype(F32).astype(BF16)


def by_rows(x, qr):
    return jnp.concatenate(swap_groups([x[8 * j : 8 * j + 8] for j in range(8)], qr), axis=0)


def beside_cols(west, mid, east, qc):
    return [
        jnp.where(qc == 0, pltpu.roll(west, BLOCK - (BLOCK_COLS - 1), 1), pltpu.roll(mid, 1, 1)),
        mid,
        jnp.where(qc == BLOCK_COLS - 1, pltpu.roll(east, BLOCK_COLS - 1, 1), pltpu.roll(mid, BLOCK - 1, 1)),
    ]


def kernel(
    f1, f2, w_hbm, mw_hbm, base, rim_corner, flows,
    g1, g2, wv, mv, wp, a1, a2, strip_s, strip_r, early_s, early_r, late_s, late_r, keys, qs, fb, transit, mix, rim_ns, rim_we, widen, hits,
    lsem, ssem, rsem, ready,
):
    rows, cols, ch = f1.shape
    br, bc = BLOCK_ROWS, BLOCK_COLS
    rb_n, cb_n = rows // br, cols // bc
    n_mask = mw_hbm.shape[0]
    rim = br + 1
    lat, lon = lax.axis_index("lat"), lax.axis_index("lon")
    nlat, nlon = lax.axis_size("lat"), lax.axis_size("lon")
    has_n, has_s = lat > 0, lat < nlat - 1
    left = (lat, lax.rem(lon + nlon - 1, nlon))
    right = (lat, lax.rem(lon + 1, nlon))
    north, south = (lat - 1, lon), (lat + 1, lon)

    barrier = pltpu.get_barrier_semaphore()

    def greet(peer):
        pl.semaphore_signal(barrier, inc=1, device_id=peer, device_id_type=MESH)

    first, last = lon == 0, lon == nlon - 1
    greet(left)
    pl.when(jnp.logical_not(last))(lambda: greet(right))
    pl.when(has_n)(lambda: greet(north))
    pl.when(has_s)(lambda: greet(south))

    odd = (lax.rem(lon, 2) == 1) & (nlat == 4)
    by_way = [odd & (lat == 2), odd & (lat == 1)]
    is_hub = [odd & (lat == 0), odd & (lat == 3)]
    hubs, ends = [(0, lon), (3, lon)], [(1, lon), (2, lon)]
    for side in range(2):
        pl.when(is_hub[side])(lambda: greet(ends[1 - side]))

    own = pl.ds(rim, rows)
    loads = [
        pltpu.make_async_copy(f1, g1.at[pl.ds(1, rows)], lsem.at[0]),
        pltpu.make_async_copy(f2, g2.at[own, pl.ds(bc, cols)], lsem.at[1]),
        pltpu.make_async_copy(w_hbm, wv, lsem.at[2]),
        pltpu.make_async_copy(mw_hbm, mv, lsem.at[3]),
    ]
    for load in loads:
        load.start()

    def absent(side):
        return jnp.logical_not(has_n if side == 0 else has_s)

    def present(side):
        return has_n if side == 0 else has_s

    def send(k, src, dst, peer, arrive_k=None):
        return pltpu.make_async_remote_copy(
            src_ref=src, dst_ref=dst, send_sem=ssem.at[k],
            recv_sem=rsem.at[k if arrive_k is None else arrive_k],
            device_id=peer, device_id_type=MESH,
        )

    bands = [(0, 1), (1, 4), (5, 2), (7, 2)]

    def band_at(side, band):
        off, n = bands[band]
        return (rim - off - n if side == 0 else rim + rows + off), n

    def row_send(k, side, band):
        off, n = bands[band]
        src = off if side == 0 else rows - off - n
        dst, _ = band_at(1 - side, band)
        peer = north if side == 0 else south
        return send(k, f2.at[pl.ds(src, n)], g2.at[pl.ds(dst, n), pl.ds(bc, cols)], peer)

    lat_sends = [
        [
            [
                send(side, f1.at[0 if side == 0 else rows - 1],
                     g1.at[rows + 1 if side == 0 else 0], north if side == 0 else south),
                row_send(2 + side, side, 0),
            ]
            for side in range(2)
        ],
    ]
    for band in range(1, len(bands)):
        lat_sends.append([[row_send(2 + 2 * band + side, side, band)] for side in range(2)])
    def detour(band, side):
        off, n = bands[band]
        k = 46 + 4 * (band - 1) + 2 * side
        src = off if side == 0 else rows - off - n
        at = transit.at[pl.ds(off - 1, n)]
        dst, _ = band_at(1 - side, band)
        into = g2.at[pl.ds(dst, n), pl.ds(bc, cols)]
        return (
            send(k, f2.at[pl.ds(src, n)], at, hubs[side]),
            send(k + 1, at, into, ends[side], 2 + 2 * band + side),
        )

    detours = [[]] + [[detour(band, side) for side in range(2)] for band in range(1, len(bands))]

    def goes_direct(side, band):
        if band == 0:
            return present(side)
        return present(side) & jnp.logical_not(by_way[side])

    mains = [
        send(44, f2.at[:, pl.ds(0, bc)], g2.at[own, pl.ds(bc + cols, bc)], left),
        send(45, f2.at[:, pl.ds(cols - bc, bc)], g2.at[own, pl.ds(0, bc)], right),
    ]
    strips = [
        send(10, strip_s.at[0], strip_r.at[1], left),
        send(11, strip_s.at[1], strip_r.at[0], right),
    ]
    earlies = [
        send(12, early_s.at[0], early_r.at[1], left),
        send(13, early_s.at[1], early_r.at[0], right),
    ]

    def relay(k, side, band):
        at, n = band_at(side, band)
        r = pl.ds(at, n)
        return [
            send(k, g2.at[r, pl.ds(bc, bc)], g2.at[r, pl.ds(bc + cols, bc)], left),
            send(k + 1, g2.at[r, pl.ds(cols, bc)], g2.at[r, pl.ds(0, bc)], right),
        ]

    relays = [[relay(24 + 4 * band + 2 * side, side, band) for side in range(2)] for band in range(len(bands))]
    lates = [
        send(40, late_s.at[0], late_r.at[1], left),
        send(41, late_s.at[1], late_r.at[0], right),
    ]

    for side in range(2):

        @pl.when(absent(side))
        def _():
            g1[0 if side == 0 else rows + 1] = jnp.zeros((cols, ch), BF16)
            lo = 0 if side == 0 else rim + rows
            g2[lo : lo + rim] = jnp.zeros((rim,) + g2.shape[1:], BF16)
            at = 0 if side == 0 else rb_n + 1
            fb[at] = jnp.zeros(fb.shape[1:], F32)

    met = [jnp.logical_not(first), has_n, has_s, by_way[0] | by_way[1]]
    pl.semaphore_wait(barrier, 1 + sum(m.astype(jnp.int32) for m in met))

    @pl.when(last)
    def _():
        pl.semaphore_signal(ready, inc=1, device_id=right, device_id_type=MESH)

    for band in range(len(bands)):
        for side, (by, _) in enumerate(detours[band]):
            pl.when(by_way[side])(by.start)
        for side in range(2):

            @pl.when(goes_direct(side, band))
            def _():
                for copy in lat_sends[band][side]:
                    copy.start()

    mains[1].start()
    pl.when(jnp.logical_not(first))(mains[0].start)
    loads[0].wait()
    loads[1].wait()

    def pick_col(tile, pick):
        return jnp.sum(jnp.where(iota(tile.shape, 1) == pick, tile.astype(F32), 0.0), axis=1)

    for side in range(2):
        lo, pick = (0, 0) if side == 0 else (cols - bc, bc - 1)
        strip_s[side, :rows] = pick_col(g1[1 : rows + 1, lo : lo + bc, :], pick).astype(BF16)
        lo, pick = (2 * bc, 0) if side == 0 else (cols - bc, bc - 1)
        strip_s[side, rows:] = pick_col(g2[rim : rim + rows, lo : lo + bc, :], pick).astype(BF16)
    strips[1].start()
    pl.when(jnp.logical_not(first))(strips[0].start)

    loads[2].wait()


    def taps(lhs, n, w):
        ys = [mm(lhs, wv[:, b].reshape(3 * ch, ch)) for b in range(3)]
        t0 = pltpu.roll(ys[0], 1, 0).reshape(n, w, ch)
        t2 = pltpu.roll(ys[2], n * w - 1, 0).reshape(n, w, ch)
        at = iota((n, w, ch), 1)
        y = ys[1].reshape(n, w, ch) + jnp.where(at == 0, 0.0, t0) + jnp.where(at == w - 1, 0.0, t2)
        edge = iota((n, 8, ch), 1)
        to_right = jnp.concatenate([t0[1:, :8], t0[:1, :8]], axis=0)
        to_left = jnp.concatenate([t2[n - 1 :, w - 8 :], t2[: n - 1, w - 8 :]], axis=0)
        return y, jnp.where(edge == 0, to_right, 0.0), jnp.where(edge == 7, to_left, 0.0)

    def lhs1(r, n):
        return jnp.concatenate([g1[r + a : r + a + n].reshape(n * cols, ch) for a in range(3)], axis=1)

    def lhs2(r, n, c, w):
        return jnp.concatenate(
            [g2[r + a : r + a + n, c : c + w, :].reshape(n * w, ch) for a in range(3)], axis=1
        )

    east = bc + cols

    def put_center(r, y, to_right, to_left):
        n = y.shape[0]
        a2[r : r + n, bc:east] = y
        a2[r : r + n, east : east + 8] = to_right
        a2[r : r + n, bc - 8 : bc] = to_left

    inner = rows - 2
    y, _, _ = taps(lhs1(1, inner), inner, cols)
    a1[1 : rows - 1] = y
    put_center(br + 1, *taps(lhs2(br + 1, inner, bc, cols), inner, cols))

    @pl.when(first)
    def _():
        pl.semaphore_wait(ready, 1)
        strips[0].start()
        mains[0].start()

    def arrive(band):
        for side in range(2):

            @pl.when(present(side))
            def _():
                for copy in lat_sends[band][1 - side]:
                    copy.wait_recv()

    def pass_on(band):
        for side in range(2):

            @pl.when(present(side))
            def _():
                for copy in relays[band][side]:
                    copy.start()

    def forward(band):
        for side, (by, on) in enumerate(detours[band]):

            @pl.when(is_hub[side])
            def _():
                by.wait_recv()
                on.start()

    arrive(0)
    pass_on(0)
    at_row, at_key = iota((16, 64), 0), iota((16, 64), 1)
    for side in range(2):
        c1, p1 = (0, 0) if side == 0 else (cols - bc, bc - 1)
        c2, p2 = (2 * bc, 0) if side == 0 else (cols - bc, bc - 1)
        tiles = [g1[r, c1 : c1 + bc, :] for r in (0, rows + 1)]
        tiles += [g2[r, c2 : c2 + bc, :] for r in (rim - 1, rim + rows)]
        hit = jnp.where(at_row < 2, p1, p2) + at_row * bc == at_key
        early_s[side] = mm(hit.astype(F32).astype(BF16), jnp.concatenate(tiles, axis=0)).astype(BF16)
    for copy in earlies:
        copy.start()

    for band in range(1, len(bands)):
        forward(band)
    arrive(1)
    pass_on(1)

    for band in range(2, len(bands)):
        arrive(band)
        pass_on(band)
    at_row, at_key = iota((2 * br, 2 * rim * bc), 0), iota((2 * br, 2 * rim * bc), 1)
    held = jnp.where(at_row < br, at_row, at_row + 2)
    for side in range(2):
        c, pick = (2 * bc, 0) if side == 0 else (cols - bc, bc - 1)
        tiles = [g2[r : r + rim, c : c + bc, :].reshape(rim * bc, ch) for r in (0, rim + rows)]
        hit = (held * bc + pick == at_key).astype(F32).astype(BF16)
        late_s[side] = mm(hit, jnp.concatenate(tiles, axis=0)).astype(BF16)
    for copy in lates:
        copy.start()

    for copy in strips + mains + earlies:
        copy.wait_recv()

    def relayed(band):
        for side in range(2):

            @pl.when(present(side))
            def _():
                for copy in relays[band][side]:
                    copy.wait_recv()

    relayed(0)

    near = br // 2
    last_row = br + rows - 1
    lhs = [lhs2(0, rim, bc, cols), lhs2(last_row, rim, bc, cols), lhs1(0, 1), lhs1(rows - 1, 1)]
    y, to_right, to_left = taps(jnp.concatenate(lhs, axis=0), 2 * rim + 2, cols)
    for side in range(2):
        part = slice(side * rim, (side + 1) * rim)
        put_center(side * last_row, y[part], to_right[part], to_left[part])
    a1[0] = y[2 * rim]
    a1[rows - 1] = y[2 * rim + 1]

    def put_sides(r, y, to_right, to_left, spread=None):
        n = y.shape[0] // 2
        outer = [y[:n, :8], y[n:, 8:]]
        if spread is not None:
            outer = [o + h for o, h in zip(outer, spread)]
        a2[r : r + n, :8] = outer[0]
        a2[r : r + n, 8:bc] = a2[r : r + n, 8:bc] + y[:n, 8:]
        a2[r : r + n, east : east + 8] = a2[r : r + n, east : east + 8] + y[n:, :8]
        a2[r : r + n, east + 8 :] = outer[1]
        a2[r : r + n, bc : bc + 8] = a2[r : r + n, bc : bc + 8] + to_right[:n]
        a2[r : r + n, east - 8 : east] = a2[r : r + n, east - 8 : east] + to_left[n:]

    row_id = iota((rows, ch), 0)
    spreads = []
    for side in range(2):
        lhs = jnp.concatenate([strip_r[side], early_r[side]], axis=0)
        z = [mm(lhs, wv[a, 2 * side]) for a in range(3)]
        for f in range(2):
            mid = [z[a][f * rows : (f + 1) * rows] for a in range(3)]
            e = 2 * rows + 2 * f
            h = mid[1] + jnp.where(row_id == 0, z[0][e : e + 1], pltpu.roll(mid[0], 1, 0))
            h = h + jnp.where(row_id == rows - 1, z[2][e + 1 : e + 2], pltpu.roll(mid[2], rows - 1, 0))
            lo, pick = (0, 0) if side == 0 else (cols - 8, 7)
            spread = jnp.where(iota((rows, 8, ch), 1) == pick, h[:, None, :], 0.0)
            if f == 0:
                a1[:, lo : lo + 8, :] = a1[:, lo : lo + 8, :] + spread
            else:
                spreads.append(spread)

    for cb in range(cb_n):
        for rb in range(rb_n):
            block = a1[rb * br : (rb + 1) * br, cb * bc : (cb + 1) * bc, :]
            qs[cb, rb * BLOCK : (rb + 1) * BLOCK] = block.astype(BF16).reshape(BLOCK, ch)

    lhs = [lhs2(br, rows, 0, bc), lhs2(br, rows, east, bc)]
    put_sides(br, *taps(jnp.concatenate(lhs, axis=0), 2 * rows, bc), spreads)
    keys[br : br + rows] = a2[br : br + rows].astype(BF16)

    scale = 1.0 / math.sqrt(ch)
    inside = [has_n.astype(F32), has_s.astype(F32)]
    zero = jnp.zeros((8, BLOCK), F32)
    totals = {(rb, cb): [zero, zero, zero] for rb in range(rb_n) for cb in range(cb_n)}
    sub = iota((8, BLOCK), 0).astype(F32)

    def correlate(kbs, kc):
        part = keys[kbs[0] * br : (kbs[-1] + 1) * br, kc * bc : (kc + 1) * bc, :]
        part = part.reshape(len(kbs) * BLOCK, ch)
        for cb in range(max(0, kc - 2), min(cb_n, kc + 1)):
            rbs = [rb for rb in range(rb_n) if any(0 <= kb - rb <= 2 for kb in kbs)]
            r0 = rbs[0]
            s = mm_nt(part, qs[cb, r0 * BLOCK : (rbs[-1] + 1) * BLOCK])
            for at, kb in enumerate(kbs):
                for rb in rbs:
                    if not 0 <= kb - rb <= 2:
                        continue
                    e = s[at * BLOCK : (at + 1) * BLOCK, (rb - r0) * BLOCK : (rb - r0 + 1) * BLOCK]
                    e = jnp.exp(e * scale).reshape(br, 2, 8, BLOCK)
                    lanes = [e[:, h] for h in range(2)]
                    by_row = lanes[0] + lanes[1]
                    y = by_row[0] * float(br * (kb - rb - 1))
                    for kr in range(1, br):
                        y = y + by_row[kr] * float(br * (kb - rb - 1) + kr)
                    by_col = [jnp.sum(h, axis=0) for h in lanes]
                    m = by_col[0] + by_col[1]
                    off = float(bc * (kc - cb - 1))
                    x = by_col[0] * (sub + off) + by_col[1] * (sub + (off + 8.0))
                    if kb == 0 or kb == rb_n + 1:
                        gate = inside[0] if kb == 0 else inside[1]
                        m, y, x = m * gate, y * gate, x * gate
                    old = totals[rb, cb]
                    totals[rb, cb] = [old[0] + m, old[1] + y, old[2] + x]

    own_kbs = list(range(1, rb_n + 1))
    for kc in range(cb_n + 2):
        correlate(own_kbs, kc)

    relayed(1)
    far = br + rows + near

    def corners(starts):
        lhs = [lhs2(r, near, c, bc) for r in starts for c in (0, east)]
        y, to_right, to_left = taps(jnp.concatenate(lhs, axis=0), 4 * near, bc)
        for end, r in enumerate(starts):
            part = slice(2 * end * near, 2 * (end + 1) * near)
            put_sides(r, y[part], to_right[part], to_left[part])

    corners([near, br + rows])

    for band in range(2, len(bands)):
        relayed(band)
    for copy in lates:
        copy.wait_recv()

    corners([0, far])
    at8 = iota((br, ch), 0)
    for side in range(2):
        lhs = jnp.concatenate([late_r[side], early_r[side], strip_r[side, rows:]], axis=0)
        z = [mm(lhs, wv[a, 2 * side]) for a in range(3)]
        far_n, far_s = [x[:br] for x in z], [x[br : 2 * br] for x in z]
        by_n, by_s = [x[2 * br + 2 : 2 * br + 3] for x in z], [x[2 * br + 3 : 2 * br + 4] for x in z]
        own_n, own_s = z[2][4 * br : 4 * br + 1], z[0][4 * br + rows - 1 : 4 * br + rows]
        h_n = far_n[0] + jnp.where(at8 == br - 1, by_n[1], pltpu.roll(far_n[1], br - 1, 0))
        nxt = jnp.where(at8 == br - 2, by_n[2], pltpu.roll(far_n[2], br - 2, 0))
        h_n = h_n + jnp.where(at8 == br - 1, own_n, nxt)
        h_s = far_s[2] + jnp.where(at8 == 0, by_s[1], pltpu.roll(far_s[1], 1, 0))
        nxt = jnp.where(at8 == 1, by_s[0], pltpu.roll(far_s[0], 2, 0))
        h_s = h_s + jnp.where(at8 == 0, own_s, nxt)
        lo, pick = (0, 0) if side == 0 else (east + 8, 7)
        for end in range(2):
            part = h_n if end == 0 else h_s
            r = end * (br + rows)
            a2[r : r + br, lo : lo + 8] = a2[r : r + br, lo : lo + 8] + jnp.where(
                iota((br, 8, ch), 1) == pick, part[:, None, :], 0.0
            )
    for end in range(2):
        r = end * (br + rows)
        keys[r : r + br] = (a2[r : r + br] * inside[end]).astype(BF16)
    for kc in range(cb_n + 2):
        correlate([0], kc)
        correlate([rb_n + 1], kc)

    lane = iota((8, BLOCK), 1)
    sublane = iota((8, BLOCK), 0)
    qr, qc = lane >> 4, lane & 15
    for (rb, cb), (m, y, x) in totals.items():
        m, y, x = [jnp.sum(t, axis=0, keepdims=True) for t in (m, y, x)]
        fy = y / m - qr.astype(F32)
        fx = x / m - qc.astype(F32)
        both = jnp.where(sublane == 0, fy, fx) * float(UPSCALE)
        fb[rb + 1, cb + 1] = both

    flow_rows = [
        send(16, fb.at[1, pl.ds(1, cb_n)], fb.at[rb_n + 1, pl.ds(1, cb_n)], north),
        send(17, fb.at[rb_n, pl.ds(1, cb_n)], fb.at[0, pl.ds(1, cb_n)], south),
    ]
    flow_cols = [
        send(18, fb.at[pl.ds(1, rb_n), 1], fb.at[pl.ds(1, rb_n), cb_n + 1], left),
        send(19, fb.at[pl.ds(1, rb_n), cb_n], fb.at[pl.ds(1, rb_n), 0], right),
    ]
    flow_corners = {}
    for side in range(2):
        src_r, dst_r = (1, rb_n + 1) if side == 0 else (rb_n, 0)
        to = lat - 1 if side == 0 else lat + 1
        flow_corners[side] = [
            send(20 + 2 * side, fb.at[src_r, 1], fb.at[dst_r, cb_n + 1], (to, left[1])),
            send(21 + 2 * side, fb.at[src_r, cb_n], fb.at[dst_r, 0], (to, right[1])),
        ]
    for side in range(2):

        @pl.when(present(side))
        def _():
            for copy in flow_corners[side] + [flow_rows[side]]:
                copy.start()

    for copy in flow_cols:
        copy.start()
    loads[3].wait()
    p = iota((n_mask, n_mask), 0)
    want = (p - (p & 63)) + ((p & 7) << 3) + ((p >> 3) & 7)
    perm = (iota((n_mask, n_mask), 1) == want).astype(F32).astype(BF16)
    wp[...] = mm(perm, mv[...]).astype(BF16)

    for cb in range(cb_n):
        logits = mm_nt(wp[...], qs[cb]).reshape(9, UPSCALE * UPSCALE, rb_n * BLOCK)
        e = jnp.exp(logits)
        mix[cb] = e / jnp.sum(e, axis=0, keepdims=True)

    weave = weaving()

    def woven(x):
        return sum(mm(p, weave) for p in parts(x))

    none = jnp.zeros((8, BLOCK), F32)
    own_fb = {(r, c): fb[r, c] for r in range(1, rb_n + 1) for c in range(1, cb_n + 1)}

    def at_block(r, c):
        return own_fb.get((r, c), none)

    for cb in range(cb_n):
        for rb in range(rb_n):
            shifted = {
                r: beside_cols(at_block(r, cb), at_block(r, cb + 1), at_block(r, cb + 2), qc)
                for r in range(rb, rb + 3)
            }
            beside = []
            for a in range(3):
                for b in range(3):
                    here = shifted[rb + 1][b]
                    if a == 0:
                        here = pltpu.roll(jnp.where(qr == br - 1, shifted[rb][b], here), bc, 1)
                    if a == 2:
                        here = pltpu.roll(jnp.where(qr == 0, shifted[rb + 2][b], here), BLOCK - bc, 1)
                    beside.append(here)
            for d in range(2):
                up = jnp.zeros((UPSCALE * UPSCALE, BLOCK), F32)
                for n in range(9):
                    up = up + mix[cb, n, :, rb * BLOCK : (rb + 1) * BLOCK] * beside[n][d : d + 1]
                base[d, rb * 64 : (rb + 1) * 64, cb * BLOCK : (cb + 1) * BLOCK] = woven(by_rows(up, qr))

    def share(rb, cb, n):
        return by_rows(mix[cb, n, :, rb * BLOCK : (rb + 1) * BLOCK], qr)

    tops = [share(0, cb, b)[:8] for b in range(3) for cb in range(cb_n)]
    tops += [share(rb_n - 1, cb, 6 + b)[56:] for b in range(3) for cb in range(cb_n)]
    tops = woven(jnp.concatenate(tops, axis=0))
    for side in range(2):
        for b in range(3):
            for cb in range(cb_n):
                k = 8 * ((side * 3 + b) * cb_n + cb)
                rim_ns[side, b, :, cb * BLOCK : (cb + 1) * BLOCK] = tops[k : k + 8]
    lanes = iota((64, BLOCK), 1)
    for side in range(2):
        keep = lanes < UPSCALE if side == 0 else lanes >= BLOCK - UPSCALE
        for a in range(3):
            for rb in range(rb_n):
                x = woven(share(rb, 0 if side == 0 else cb_n - 1, 3 * a + 2 * side))
                rim_we[side, a, rb * 64 : (rb + 1) * 64] = jnp.where(keep, x, 0.0)
        at = 0 if side == 0 else cb_n - 1
        for end in range(2):
            k = 8 * ((end * 3 + 2 * side) * cb_n + at)
            rim_corner[end, side] = jnp.where(keep[:8], tops[k : k + 8], 0.0)

    k = iota((BLOCK, BLOCK), 0)
    widen[...] = (k == BLOCK - bc + (iota((BLOCK, BLOCK), 1) >> 3)).astype(F32).astype(BF16)
    high = rows * UPSCALE
    for a in range(3):
        want = ((iota((high, rb_n * BLOCK), 0) >> 3) + (a - 1)) * bc + (bc - 1)
        hit = iota((high, rb_n * BLOCK), 1) == want
        hits[a * high : (a + 1) * high] = hit.astype(F32).astype(BF16)

    for copy in flow_cols:
        copy.wait_recv()
    west = [fb[r, 0] for r in range(1, rb_n + 1)]
    eastern = [pltpu.roll(fb[r, cb_n + 1], bc - 1, 1) for r in range(1, rb_n + 1)]
    sides = jnp.concatenate([jnp.concatenate(x, axis=1) for x in (west, eastern)], axis=0)
    tall = sum(mm_nt(hits[...], p) for p in parts(sides))
    for side in range(2):
        cc = slice(0, BLOCK) if side == 0 else slice((cb_n - 1) * BLOCK, cb_n * BLOCK)
        for d in range(2):
            y = base[d, :, cc]
            for a in range(3):
                y = y + rim_we[side, a] * tall[a * high : (a + 1) * high, 8 * side + d : 8 * side + d + 1]
            base[d, :, cc] = y

    for side in range(2):
        pl.when(present(side))(flow_rows[1 - side].wait_recv)
    cells = []
    for side in range(2):
        r = 0 if side == 0 else rb_n + 1
        at_c = [none] + [fb[r, c] for c in range(1, cb_n + 1)] + [none]
        near_by = [beside_cols(*at_c[cb : cb + 3], qc) for cb in range(cb_n)]
        if side == 1:
            near_by = [[pltpu.roll(x, BLOCK - bc, 1) for x in xs] for xs in near_by]
        cells += [near_by[cb][b] for b in range(3) for cb in range(cb_n)]
    wide = sum(mm(p, widen[...]) for p in parts(jnp.concatenate(cells, axis=0)))
    for d in range(2):
        for side in range(2):
            edge = slice(0, 8) if side == 0 else slice(high - 8, high)
            for cb in range(cb_n):
                cc = slice(cb * BLOCK, (cb + 1) * BLOCK)
                y = base[d, edge, cc]
                for b in range(3):
                    k = 8 * ((side * 3 + b) * cb_n + cb) + d
                    y = y + rim_ns[side, b, :, cc] * wide[k : k + 1]
                base[d, edge, cc] = y

    for side in range(2):

        @pl.when(present(side))
        def _():
            for copy in flow_corners[1 - side]:
                copy.wait_recv()

    flows[...] = fb[...]

    for side in range(2):

        @pl.when(present(side))
        def _():
            for copy in [flow_rows[side]] + flow_corners[side]:
                copy.wait_send()
            for band in range(len(bands)):
                for copy in relays[band][side]:
                    copy.wait_send()

    for band in range(len(bands)):
        for side in range(2):

            @pl.when(goes_direct(side, band))
            def _():
                for copy in lat_sends[band][side]:
                    copy.wait_send()

        for side, (by, on) in enumerate(detours[band]):
            pl.when(by_way[side])(by.wait_send)
            pl.when(is_hub[side])(on.wait_send)

    for copy in strips + mains + earlies + lates + flow_cols:
        copy.wait_send()


def add_corners(base, rim_corner, fb, out_hbm, out, sem):
    rb_n, cb_n = fb.shape[0] - 2, fb.shape[1] - 2
    high = base.shape[1]
    edges = [slice(0, 8), slice(high - 8, high)]
    copies = [
        pltpu.make_async_copy(
            base.at[:, pl.ds(8, high - 16)], out_hbm.at[:, pl.ds(8, high - 16)], sem.at[2]
        )
    ]
    copies[0].start()
    for end in range(2):
        for d in range(2):
            out[end, d] = base[d, edges[end], :]
            for side in range(2):
                at = slice(0, BLOCK) if side == 0 else slice((cb_n - 1) * BLOCK, cb_n * BLOCK)
                lane = (BLOCK - BLOCK_COLS) * (1 - end) + (BLOCK_COLS - 1) * (1 - side)
                x = fb[end * (rb_n + 1), side * (cb_n + 1)][d : d + 1, lane : lane + 1]
                out[end, d, :, at] = out[end, d, :, at] + rim_corner[end, side] * x
        copies.append(
            pltpu.make_async_copy(out.at[end], out_hbm.at[:, pl.ds(end * (high - 8), 8)], sem.at[end])
        )
        copies[-1].start()
    for copy in copies:
        copy.wait()


def body(frame_one, frame_two, enc_weight, mask_weight):
    rows, cols, ch = frame_one.shape
    n_mask = mask_weight.shape[1]
    rb_n, cb_n = rows // BLOCK_ROWS, cols // BLOCK_COLS
    shape = (2, rows * UPSCALE, cols * UPSCALE)
    held = pl.pallas_call(
        kernel,
        out_shape=[
            jax.ShapeDtypeStruct(shape, F32),
            jax.ShapeDtypeStruct((2, 2, UPSCALE, BLOCK), F32),
            jax.ShapeDtypeStruct((rb_n + 2, cb_n + 2, 8, BLOCK), F32),
        ],
        in_specs=[pl.BlockSpec(memory_space=pltpu.HBM)] * 4,
        out_specs=[pl.BlockSpec(memory_space=pltpu.VMEM)] * 3,
        scratch_shapes=[
            pltpu.VMEM((rows + 2, cols, ch), BF16),
            pltpu.VMEM((rows + 2 * BLOCK_ROWS + 2, cols + 2 * BLOCK_COLS, ch), BF16),
            pltpu.VMEM(enc_weight.shape, BF16),
            pltpu.VMEM((n_mask, ch), BF16),
            pltpu.VMEM((n_mask, ch), BF16),
            pltpu.VMEM((rows, cols, ch), F32),
            pltpu.VMEM((rows + 2 * BLOCK_ROWS, cols + 2 * BLOCK_COLS, ch), F32),
            pltpu.VMEM((2, 2 * rows, ch), BF16),
            pltpu.VMEM((2, 2 * rows, ch), BF16),
            pltpu.VMEM((2, 16, ch), BF16),
            pltpu.VMEM((2, 16, ch), BF16),
            pltpu.VMEM((2, 2 * BLOCK_ROWS, ch), BF16),
            pltpu.VMEM((2, 2 * BLOCK_ROWS, ch), BF16),
            pltpu.VMEM((rows + 2 * BLOCK_ROWS, cols + 2 * BLOCK_COLS, ch), BF16),
            pltpu.VMEM((cb_n, rb_n * BLOCK, ch), BF16),
            pltpu.VMEM((rb_n + 2, cb_n + 2, 8, BLOCK), F32),
            pltpu.VMEM((BLOCK_ROWS, cols, ch), BF16),
            pltpu.VMEM((cb_n, 9, UPSCALE * UPSCALE, rb_n * BLOCK), F32),
            pltpu.VMEM((2, 3, UPSCALE, cols * UPSCALE), F32),
            pltpu.VMEM((2, 3, rows * UPSCALE, BLOCK), F32),
            pltpu.VMEM((BLOCK, BLOCK), BF16),
            pltpu.VMEM((3 * rows * UPSCALE, rb_n * BLOCK), BF16),
            pltpu.SemaphoreType.DMA((4,)),
            pltpu.SemaphoreType.DMA((64,)),
            pltpu.SemaphoreType.DMA((64,)),
            pltpu.SemaphoreType.REGULAR,
        ],
        compiler_params=pltpu.CompilerParams(
            collective_id=0, has_side_effects=True, vmem_limit_bytes=32 * 2**20
        ),
        name="flow",
    )(*[pltpu.with_memory_space_constraint(a, pltpu.HBM) for a in (frame_one, frame_two, enc_weight, mask_weight.T)])
    return pl.pallas_call(
        add_corners,
        out_shape=jax.ShapeDtypeStruct(shape, F32),
        in_specs=[pl.BlockSpec(memory_space=pltpu.VMEM)] * 3,
        out_specs=pl.BlockSpec(memory_space=pl.ANY),
        scratch_shapes=[
            pltpu.VMEM((2, 2, UPSCALE, cols * UPSCALE), F32),
            pltpu.SemaphoreType.DMA((3,)),
        ],
        compiler_params=pltpu.CompilerParams(vmem_limit_bytes=32 * 2**20),
        name="add_corners",
    )(*held)


def solution(mesh):
    in_specs = (P("lat", "lon", None), P("lat", "lon", None), P(), P())
    out_specs = P(None, "lat", "lon")
    return jax.shard_map(body, mesh=mesh, in_specs=in_specs, out_specs=out_specs, check_vma=False)
```

```python
import functools
import math

import jax
import jax.numpy as jnp
from jax import lax
from jax.experimental import pallas as pl
from jax.experimental.pallas import tpu as pltpu
from jax.sharding import PartitionSpec as P

BLOCK_ROWS = 8
BLOCK_COLS = 16
BLOCK = BLOCK_ROWS * BLOCK_COLS
UPSCALE = 8
F32 = jnp.float32
BF16 = jnp.bfloat16
MESH = pl.DeviceIdType.MESH


def iota(shape, axis):
    return lax.broadcasted_iota(jnp.int32, shape, axis)


def mm(a, b):
    return jnp.dot(a, b, preferred_element_type=F32)


def mm_nt(a, b):
    return lax.dot_general(a, b, (((1,), (1,)), ((), ())), preferred_element_type=F32)


def swap_groups(xs, lane_group):
    xs = list(xs)
    for bit in (1, 2, 4):
        mask = (lane_group & bit) != 0
        shift = bit * BLOCK_COLS
        for a in range(8):
            if a & bit:
                continue
            lo, hi = xs[a], xs[a | bit]
            xs[a] = jnp.where(mask, pltpu.roll(hi, shift, 1), lo)
            xs[a | bit] = jnp.where(mask, hi, pltpu.roll(lo, BLOCK - shift, 1))
    return xs


def parts(x):
    high = x.astype(BF16)
    rest = x - high.astype(F32)
    mid = rest.astype(BF16)
    return high, mid, (rest - mid.astype(F32)).astype(BF16)


def weaving():
    k = iota((BLOCK, BLOCK), 0)
    hit = iota((BLOCK, BLOCK), 1) == ((k & (BLOCK_COLS - 1)) << 3) + (k >> 4)
    return hit.astype(F32).astype(BF16)


def by_rows(x, qr):
    return jnp.concatenate(swap_groups([x[8 * j : 8 * j + 8] for j in range(8)], qr), axis=0)


def beside_cols(west, mid, east, qc):
    return [
        jnp.where(qc == 0, pltpu.roll(west, BLOCK - (BLOCK_COLS - 1), 1), pltpu.roll(mid, 1, 1)),
        mid,
        jnp.where(qc == BLOCK_COLS - 1, pltpu.roll(east, BLOCK_COLS - 1, 1), pltpu.roll(mid, BLOCK - 1, 1)),
    ]


def kernel(
    f1, f2, w_hbm, mw_hbm, base, rim_corner, flows,
    g1, g2, wv, mv, wp, a1, a2, strip_s, strip_r, early_s, early_r, late_s, late_r, keys, qs, fb, transit, mix, rim_ns, rim_we, widen, hits,
    lsem, ssem, rsem, ready,
):
    rows, cols, ch = f1.shape
    br, bc = BLOCK_ROWS, BLOCK_COLS
    rb_n, cb_n = rows // br, cols // bc
    n_mask = mw_hbm.shape[0]
    rim = br + 1
    lat, lon = lax.axis_index("lat"), lax.axis_index("lon")
    nlat, nlon = lax.axis_size("lat"), lax.axis_size("lon")
    has_n, has_s = lat > 0, lat < nlat - 1
    left = (lat, lax.rem(lon + nlon - 1, nlon))
    right = (lat, lax.rem(lon + 1, nlon))
    north, south = (lat - 1, lon), (lat + 1, lon)

    barrier = pltpu.get_barrier_semaphore()

    def greet(peer):
        pl.semaphore_signal(barrier, inc=1, device_id=peer, device_id_type=MESH)

    first, last = lon == 0, lon == nlon - 1
    greet(left)
    pl.when(jnp.logical_not(last))(lambda: greet(right))
    pl.when(has_n)(lambda: greet(north))
    pl.when(has_s)(lambda: greet(south))

    odd = (lax.rem(lon, 2) == 1) & (nlat == 4)
    by_way = [odd & (lat == 2), odd & (lat == 1)]
    is_hub = [odd & (lat == 0), odd & (lat == 3)]
    hubs, ends = [(0, lon), (3, lon)], [(1, lon), (2, lon)]
    for side in range(2):
        pl.when(is_hub[side])(lambda: greet(ends[1 - side]))

    own = pl.ds(rim, rows)
    loads = [
        pltpu.make_async_copy(f1, g1.at[pl.ds(1, rows)], lsem.at[0]),
        pltpu.make_async_copy(f2, g2.at[own, pl.ds(bc, cols)], lsem.at[1]),
        pltpu.make_async_copy(w_hbm, wv, lsem.at[2]),
        pltpu.make_async_copy(mw_hbm, mv, lsem.at[3]),
    ]
    for load in loads:
        load.start()

    def absent(side):
        return jnp.logical_not(has_n if side == 0 else has_s)

    def present(side):
        return has_n if side == 0 else has_s

    def send(k, src, dst, peer, arrive_k=None):
        return pltpu.make_async_remote_copy(
            src_ref=src, dst_ref=dst, send_sem=ssem.at[k],
            recv_sem=rsem.at[k if arrive_k is None else arrive_k],
            device_id=peer, device_id_type=MESH,
        )

    bands = [(0, 1), (1, 4), (5, 2), (7, 2)]

    def band_at(side, band):
        off, n = bands[band]
        return (rim - off - n if side == 0 else rim + rows + off), n

    def row_send(k, side, band):
        off, n = bands[band]
        src = off if side == 0 else rows - off - n
        dst, _ = band_at(1 - side, band)
        peer = north if side == 0 else south
        return send(k, f2.at[pl.ds(src, n)], g2.at[pl.ds(dst, n), pl.ds(bc, cols)], peer)

    lat_sends = [
        [
            [
                send(side, f1.at[0 if side == 0 else rows - 1],
                     g1.at[rows + 1 if side == 0 else 0], north if side == 0 else south),
                row_send(2 + side, side, 0),
            ]
            for side in range(2)
        ],
    ]
    for band in range(1, len(bands)):
        lat_sends.append([[row_send(2 + 2 * band + side, side, band)] for side in range(2)])
    def detour(band, side):
        off, n = bands[band]
        k = 46 + 4 * (band - 1) + 2 * side
        src = off if side == 0 else rows - off - n
        at = transit.at[pl.ds(off - 1, n)]
        dst, _ = band_at(1 - side, band)
        into = g2.at[pl.ds(dst, n), pl.ds(bc, cols)]
        return (
            send(k, f2.at[pl.ds(src, n)], at, hubs[side]),
            send(k + 1, at, into, ends[side], 2 + 2 * band + side),
        )

    detours = [[]] + [[detour(band, side) for side in range(2)] for band in range(1, len(bands))]

    def goes_direct(side, band):
        if band == 0:
            return present(side)
        return present(side) & jnp.logical_not(by_way[side])

    mains = [
        send(44, f2.at[:, pl.ds(0, bc)], g2.at[own, pl.ds(bc + cols, bc)], left),
        send(45, f2.at[:, pl.ds(cols - bc, bc)], g2.at[own, pl.ds(0, bc)], right),
    ]
    strips = [
        send(10, strip_s.at[0], strip_r.at[1], left),
        send(11, strip_s.at[1], strip_r.at[0], right),
    ]
    earlies = [
        send(12, early_s.at[0], early_r.at[1], left),
        send(13, early_s.at[1], early_r.at[0], right),
    ]

    def relay(k, side, band):
        at, n = band_at(side, band)
        r = pl.ds(at, n)
        return [
            send(k, g2.at[r, pl.ds(bc, bc)], g2.at[r, pl.ds(bc + cols, bc)], left),
            send(k + 1, g2.at[r, pl.ds(cols, bc)], g2.at[r, pl.ds(0, bc)], right),
        ]

    relays = [[relay(24 + 4 * band + 2 * side, side, band) for side in range(2)] for band in range(len(bands))]
    lates = [
        send(40, late_s.at[0], late_r.at[1], left),
        send(41, late_s.at[1], late_r.at[0], right),
    ]

    for side in range(2):

        @pl.when(absent(side))
        def _():
            g1[0 if side == 0 else rows + 1] = jnp.zeros((cols, ch), BF16)
            lo = 0 if side == 0 else rim + rows
            g2[lo : lo + rim] = jnp.zeros((rim,) + g2.shape[1:], BF16)
            at = 0 if side == 0 else rb_n + 1
            fb[at] = jnp.zeros(fb.shape[1:], F32)

    met = [jnp.logical_not(first), has_n, has_s, by_way[0] | by_way[1]]
    pl.semaphore_wait(barrier, 1 + sum(m.astype(jnp.int32) for m in met))

    @pl.when(last)
    def _():
        pl.semaphore_signal(ready, inc=1, device_id=right, device_id_type=MESH)

    for band in range(len(bands)):
        for side, (by, _) in enumerate(detours[band]):
            pl.when(by_way[side])(by.start)
        for side in range(2):

            @pl.when(goes_direct(side, band))
            def _():
                for copy in lat_sends[band][side]:
                    copy.start()

    mains[1].start()
    pl.when(jnp.logical_not(first))(mains[0].start)
    loads[0].wait()
    loads[1].wait()

    def pick_col(tile, pick):
        return jnp.sum(jnp.where(iota(tile.shape, 1) == pick, tile.astype(F32), 0.0), axis=1)

    for side in range(2):
        lo, pick = (0, 0) if side == 0 else (cols - bc, bc - 1)
        strip_s[side, :rows] = pick_col(g1[1 : rows + 1, lo : lo + bc, :], pick).astype(BF16)
        lo, pick = (2 * bc, 0) if side == 0 else (cols - bc, bc - 1)
        strip_s[side, rows:] = pick_col(g2[rim : rim + rows, lo : lo + bc, :], pick).astype(BF16)
    strips[1].start()
    pl.when(jnp.logical_not(first))(strips[0].start)

    loads[2].wait()


    def taps(lhs, n, w):
        ys = [mm(lhs, wv[:, b].reshape(3 * ch, ch)) for b in range(3)]
        t0 = pltpu.roll(ys[0], 1, 0).reshape(n, w, ch)
        t2 = pltpu.roll(ys[2], n * w - 1, 0).reshape(n, w, ch)
        at = iota((n, w, ch), 1)
        y = ys[1].reshape(n, w, ch) + jnp.where(at == 0, 0.0, t0) + jnp.where(at == w - 1, 0.0, t2)
        edge = iota((n, 8, ch), 1)
        to_right = jnp.concatenate([t0[1:, :8], t0[:1, :8]], axis=0)
        to_left = jnp.concatenate([t2[n - 1 :, w - 8 :], t2[: n - 1, w - 8 :]], axis=0)
        return y, jnp.where(edge == 0, to_right, 0.0), jnp.where(edge == 7, to_left, 0.0)

    def lhs1(r, n):
        return jnp.concatenate([g1[r + a : r + a + n].reshape(n * cols, ch) for a in range(3)], axis=1)

    def lhs2(r, n, c, w):
        return jnp.concatenate(
            [g2[r + a : r + a + n, c : c + w, :].reshape(n * w, ch) for a in range(3)], axis=1
        )

    east = bc + cols

    def put_center(r, y, to_right, to_left):
        n = y.shape[0]
        a2[r : r + n, bc:east] = y
        a2[r : r + n, east : east + 8] = to_right
        a2[r : r + n, bc - 8 : bc] = to_left

    inner = rows - 2
    y, _, _ = taps(lhs1(1, inner), inner, cols)
    a1[1 : rows - 1] = y
    put_center(br + 1, *taps(lhs2(br + 1, inner, bc, cols), inner, cols))

    @pl.when(first)
    def _():
        pl.semaphore_wait(ready, 1)
        strips[0].start()
        mains[0].start()

    def arrive(band):
        for side in range(2):

            @pl.when(present(side))
            def _():
                for copy in lat_sends[band][1 - side]:
                    copy.wait_recv()

    def pass_on(band):
        for side in range(2):

            @pl.when(present(side))
            def _():
                for copy in relays[band][side]:
                    copy.start()

    def forward(band):
        for side, (by, on) in enumerate(detours[band]):

            @pl.when(is_hub[side])
            def _():
                by.wait_recv()
                on.start()

    arrive(0)
    pass_on(0)
    at_row, at_key = iota((16, 64), 0), iota((16, 64), 1)
    for side in range(2):
        c1, p1 = (0, 0) if side == 0 else (cols - bc, bc - 1)
        c2, p2 = (2 * bc, 0) if side == 0 else (cols - bc, bc - 1)
        tiles = [g1[r, c1 : c1 + bc, :] for r in (0, rows + 1)]
        tiles += [g2[r, c2 : c2 + bc, :] for r in (rim - 1, rim + rows)]
        hit = jnp.where(at_row < 2, p1, p2) + at_row * bc == at_key
        early_s[side] = mm(hit.astype(F32).astype(BF16), jnp.concatenate(tiles, axis=0)).astype(BF16)
    for copy in earlies:
        copy.start()

    for band in range(1, len(bands)):
        forward(band)
    arrive(1)
    pass_on(1)

    for band in range(2, len(bands)):
        arrive(band)
        pass_on(band)
    at_row, at_key = iota((2 * br, 2 * rim * bc), 0), iota((2 * br, 2 * rim * bc), 1)
    held = jnp.where(at_row < br, at_row, at_row + 2)
    for side in range(2):
        c, pick = (2 * bc, 0) if side == 0 else (cols - bc, bc - 1)
        tiles = [g2[r : r + rim, c : c + bc, :].reshape(rim * bc, ch) for r in (0, rim + rows)]
        hit = (held * bc + pick == at_key).astype(F32).astype(BF16)
        late_s[side] = mm(hit, jnp.concatenate(tiles, axis=0)).astype(BF16)
    for copy in lates:
        copy.start()

    for copy in strips + mains + earlies:
        copy.wait_recv()

    def relayed(band):
        for side in range(2):

            @pl.when(present(side))
            def _():
                for copy in relays[band][side]:
                    copy.wait_recv()

    relayed(0)

    near = br // 2
    last_row = br + rows - 1
    lhs = [lhs2(0, rim, bc, cols), lhs2(last_row, rim, bc, cols), lhs1(0, 1), lhs1(rows - 1, 1)]
    y, to_right, to_left = taps(jnp.concatenate(lhs, axis=0), 2 * rim + 2, cols)
    for side in range(2):
        part = slice(side * rim, (side + 1) * rim)
        put_center(side * last_row, y[part], to_right[part], to_left[part])
    a1[0] = y[2 * rim]
    a1[rows - 1] = y[2 * rim + 1]

    def put_sides(r, y, to_right, to_left, spread=None):
        n = y.shape[0] // 2
        outer = [y[:n, :8], y[n:, 8:]]
        if spread is not None:
            outer = [o + h for o, h in zip(outer, spread)]
        a2[r : r + n, :8] = outer[0]
        a2[r : r + n, 8:bc] = a2[r : r + n, 8:bc] + y[:n, 8:]
        a2[r : r + n, east : east + 8] = a2[r : r + n, east : east + 8] + y[n:, :8]
        a2[r : r + n, east + 8 :] = outer[1]
        a2[r : r + n, bc : bc + 8] = a2[r : r + n, bc : bc + 8] + to_right[:n]
        a2[r : r + n, east - 8 : east] = a2[r : r + n, east - 8 : east] + to_left[n:]

    row_id = iota((rows, ch), 0)
    spreads = []
    for side in range(2):
        lhs = jnp.concatenate([strip_r[side], early_r[side]], axis=0)
        z = [mm(lhs, wv[a, 2 * side]) for a in range(3)]
        for f in range(2):
            mid = [z[a][f * rows : (f + 1) * rows] for a in range(3)]
            e = 2 * rows + 2 * f
            h = mid[1] + jnp.where(row_id == 0, z[0][e : e + 1], pltpu.roll(mid[0], 1, 0))
            h = h + jnp.where(row_id == rows - 1, z[2][e + 1 : e + 2], pltpu.roll(mid[2], rows - 1, 0))
            lo, pick = (0, 0) if side == 0 else (cols - 8, 7)
            spread = jnp.where(iota((rows, 8, ch), 1) == pick, h[:, None, :], 0.0)
            if f == 0:
                a1[:, lo : lo + 8, :] = a1[:, lo : lo + 8, :] + spread
            else:
                spreads.append(spread)

    for cb in range(cb_n):
        for rb in range(rb_n):
            block = a1[rb * br : (rb + 1) * br, cb * bc : (cb + 1) * bc, :]
            qs[cb, rb * BLOCK : (rb + 1) * BLOCK] = block.astype(BF16).reshape(BLOCK, ch)

    lhs = [lhs2(br, rows, 0, bc), lhs2(br, rows, east, bc)]
    put_sides(br, *taps(jnp.concatenate(lhs, axis=0), 2 * rows, bc), spreads)
    keys[br : br + rows] = a2[br : br + rows].astype(BF16)

    scale = 1.0 / math.sqrt(ch)
    inside = [has_n.astype(F32), has_s.astype(F32)]
    zero = jnp.zeros((8, BLOCK), F32)
    totals = {(rb, cb): [zero, zero, zero] for rb in range(rb_n) for cb in range(cb_n)}
    sub = iota((8, BLOCK), 0).astype(F32)

    def correlate(kbs, kc):
        part = keys[kbs[0] * br : (kbs[-1] + 1) * br, kc * bc : (kc + 1) * bc, :]
        part = part.reshape(len(kbs) * BLOCK, ch)
        for cb in range(max(0, kc - 2), min(cb_n, kc + 1)):
            rbs = [rb for rb in range(rb_n) if any(0 <= kb - rb <= 2 for kb in kbs)]
            r0 = rbs[0]
            s = mm_nt(part, qs[cb, r0 * BLOCK : (rbs[-1] + 1) * BLOCK])
            for at, kb in enumerate(kbs):
                for rb in rbs:
                    if not 0 <= kb - rb <= 2:
                        continue
                    e = s[at * BLOCK : (at + 1) * BLOCK, (rb - r0) * BLOCK : (rb - r0 + 1) * BLOCK]
                    e = jnp.exp(e * scale).reshape(br, 2, 8, BLOCK)
                    lanes = [e[:, h] for h in range(2)]
                    by_row = lanes[0] + lanes[1]
                    y = by_row[0] * float(br * (kb - rb - 1))
                    for kr in range(1, br):
                        y = y + by_row[kr] * float(br * (kb - rb - 1) + kr)
                    by_col = [jnp.sum(h, axis=0) for h in lanes]
                    m = by_col[0] + by_col[1]
                    off = float(bc * (kc - cb - 1))
                    x = by_col[0] * (sub + off) + by_col[1] * (sub + (off + 8.0))
                    if kb == 0 or kb == rb_n + 1:
                        gate = inside[0] if kb == 0 else inside[1]
                        m, y, x = m * gate, y * gate, x * gate
                    old = totals[rb, cb]
                    totals[rb, cb] = [old[0] + m, old[1] + y, old[2] + x]

    own_kbs = list(range(1, rb_n + 1))
    for kc in range(cb_n + 2):
        correlate(own_kbs, kc)

    relayed(1)
    def correlate_rows(end, groups):
        rb = 0 if end == 0 else rb_n - 1
        off_r = -br if end == 0 else br
        r = end * (br + rows)
        part = [a2[r : r + br, bc + c : bc + c + 8] * inside[end] for c in groups]
        part = jnp.concatenate(part, axis=1).astype(BF16).reshape(BLOCK, ch)
        for cb in range(cb_n):
            took = [h for h, c in enumerate(groups) if bc * (cb - 1) <= c < bc * (cb + 2)]
            if not took:
                continue
            s = mm_nt(part, qs[cb, rb * BLOCK : (rb + 1) * BLOCK])
            e = jnp.exp(s * scale).reshape(br, 2, 8, BLOCK)
            by_row = sum(e[:, h] for h in took)
            y = by_row[0] * float(off_r)
            for kr in range(1, br):
                y = y + by_row[kr] * float(off_r + kr)
            by_col = [jnp.sum(e[:, h], axis=0) for h in took]
            m = sum(by_col)
            x = sum(t * (sub + float(groups[h] - bc * cb)) for t, h in zip(by_col, took))
            old = totals[rb, cb]
            totals[rb, cb] = [o + t * inside[end] for o, t in zip(old, (m, y, x))]

    for c in range(8, cols - 8, bc):
        for end in range(2):
            correlate_rows(end, (c, c + 8))
    far = br + rows + near

    def corners(starts):
        lhs = [lhs2(r, near, c, bc) for r in starts for c in (0, east)]
        y, to_right, to_left = taps(jnp.concatenate(lhs, axis=0), 4 * near, bc)
        for end, r in enumerate(starts):
            part = slice(2 * end * near, 2 * (end + 1) * near)
            put_sides(r, y[part], to_right[part], to_left[part])

    corners([near, br + rows])

    for band in range(2, len(bands)):
        relayed(band)
    for copy in lates:
        copy.wait_recv()

    corners([0, far])
    at8 = iota((br, ch), 0)
    for side in range(2):
        lhs = jnp.concatenate([late_r[side], early_r[side], strip_r[side, rows:]], axis=0)
        z = [mm(lhs, wv[a, 2 * side]) for a in range(3)]
        far_n, far_s = [x[:br] for x in z], [x[br : 2 * br] for x in z]
        by_n, by_s = [x[2 * br + 2 : 2 * br + 3] for x in z], [x[2 * br + 3 : 2 * br + 4] for x in z]
        own_n, own_s = z[2][4 * br : 4 * br + 1], z[0][4 * br + rows - 1 : 4 * br + rows]
        h_n = far_n[0] + jnp.where(at8 == br - 1, by_n[1], pltpu.roll(far_n[1], br - 1, 0))
        nxt = jnp.where(at8 == br - 2, by_n[2], pltpu.roll(far_n[2], br - 2, 0))
        h_n = h_n + jnp.where(at8 == br - 1, own_n, nxt)
        h_s = far_s[2] + jnp.where(at8 == 0, by_s[1], pltpu.roll(far_s[1], 1, 0))
        nxt = jnp.where(at8 == 1, by_s[0], pltpu.roll(far_s[0], 2, 0))
        h_s = h_s + jnp.where(at8 == 0, own_s, nxt)
        lo, pick = (0, 0) if side == 0 else (east + 8, 7)
        for end in range(2):
            part = h_n if end == 0 else h_s
            r = end * (br + rows)
            a2[r : r + br, lo : lo + 8] = a2[r : r + br, lo : lo + 8] + jnp.where(
                iota((br, 8, ch), 1) == pick, part[:, None, :], 0.0
            )
    for end in range(2):
        for groups in ((-bc, 8 - bc), (0, cols - 8), (cols, cols + 8)):
            correlate_rows(end, groups)

    lane = iota((8, BLOCK), 1)
    sublane = iota((8, BLOCK), 0)
    qr, qc = lane >> 4, lane & 15
    for (rb, cb), (m, y, x) in totals.items():
        m, y, x = [jnp.sum(t, axis=0, keepdims=True) for t in (m, y, x)]
        fy = y / m - qr.astype(F32)
        fx = x / m - qc.astype(F32)
        both = jnp.where(sublane == 0, fy, fx) * float(UPSCALE)
        fb[rb + 1, cb + 1] = both

    flow_rows = [
        send(16, fb.at[1, pl.ds(1, cb_n)], fb.at[rb_n + 1, pl.ds(1, cb_n)], north),
        send(17, fb.at[rb_n, pl.ds(1, cb_n)], fb.at[0, pl.ds(1, cb_n)], south),
    ]
    flow_cols = [
        send(18, fb.at[pl.ds(1, rb_n), 1], fb.at[pl.ds(1, rb_n), cb_n + 1], left),
        send(19, fb.at[pl.ds(1, rb_n), cb_n], fb.at[pl.ds(1, rb_n), 0], right),
    ]
    flow_corners = {}
    for side in range(2):
        src_r, dst_r = (1, rb_n + 1) if side == 0 else (rb_n, 0)
        to = lat - 1 if side == 0 else lat + 1
        flow_corners[side] = [
            send(20 + 2 * side, fb.at[src_r, 1], fb.at[dst_r, cb_n + 1], (to, left[1])),
            send(21 + 2 * side, fb.at[src_r, cb_n], fb.at[dst_r, 0], (to, right[1])),
        ]
    for side in range(2):

        @pl.when(present(side))
        def _():
            for copy in flow_corners[side] + [flow_rows[side]]:
                copy.start()

    for copy in flow_cols:
        copy.start()
    loads[3].wait()
    p = iota((n_mask, n_mask), 0)
    want = (p - (p & 63)) + ((p & 7) << 3) + ((p >> 3) & 7)
    perm = (iota((n_mask, n_mask), 1) == want).astype(F32).astype(BF16)
    wp[...] = mm(perm, mv[...]).astype(BF16)

    for cb in range(cb_n):
        logits = mm_nt(wp[...], qs[cb]).reshape(9, UPSCALE * UPSCALE, rb_n * BLOCK)
        e = jnp.exp(logits)
        mix[cb] = e / jnp.sum(e, axis=0, keepdims=True)

    weave = weaving()

    def woven(x):
        return sum(mm(p, weave) for p in parts(x))

    none = jnp.zeros((8, BLOCK), F32)
    own_fb = {(r, c): fb[r, c] for r in range(1, rb_n + 1) for c in range(1, cb_n + 1)}

    def at_block(r, c):
        return own_fb.get((r, c), none)

    for cb in range(cb_n):
        for rb in range(rb_n):
            shifted = {
                r: beside_cols(at_block(r, cb), at_block(r, cb + 1), at_block(r, cb + 2), qc)
                for r in range(rb, rb + 3)
            }
            beside = []
            for a in range(3):
                for b in range(3):
                    here = shifted[rb + 1][b]
                    if a == 0:
                        here = pltpu.roll(jnp.where(qr == br - 1, shifted[rb][b], here), bc, 1)
                    if a == 2:
                        here = pltpu.roll(jnp.where(qr == 0, shifted[rb + 2][b], here), BLOCK - bc, 1)
                    beside.append(here)
            for d in range(2):
                up = jnp.zeros((UPSCALE * UPSCALE, BLOCK), F32)
                for n in range(9):
                    up = up + mix[cb, n, :, rb * BLOCK : (rb + 1) * BLOCK] * beside[n][d : d + 1]
                base[d, rb * 64 : (rb + 1) * 64, cb * BLOCK : (cb + 1) * BLOCK] = woven(by_rows(up, qr))

    def share(rb, cb, n):
        return by_rows(mix[cb, n, :, rb * BLOCK : (rb + 1) * BLOCK], qr)

    tops = [share(0, cb, b)[:8] for b in range(3) for cb in range(cb_n)]
    tops += [share(rb_n - 1, cb, 6 + b)[56:] for b in range(3) for cb in range(cb_n)]
    tops = woven(jnp.concatenate(tops, axis=0))
    for side in range(2):
        for b in range(3):
            for cb in range(cb_n):
                k = 8 * ((side * 3 + b) * cb_n + cb)
                rim_ns[side, b, :, cb * BLOCK : (cb + 1) * BLOCK] = tops[k : k + 8]
    lanes = iota((64, BLOCK), 1)
    for side in range(2):
        keep = lanes < UPSCALE if side == 0 else lanes >= BLOCK - UPSCALE
        for a in range(3):
            for rb in range(rb_n):
                x = woven(share(rb, 0 if side == 0 else cb_n - 1, 3 * a + 2 * side))
                rim_we[side, a, rb * 64 : (rb + 1) * 64] = jnp.where(keep, x, 0.0)
        at = 0 if side == 0 else cb_n - 1
        for end in range(2):
            k = 8 * ((end * 3 + 2 * side) * cb_n + at)
            rim_corner[end, side] = jnp.where(keep[:8], tops[k : k + 8], 0.0)

    k = iota((BLOCK, BLOCK), 0)
    widen[...] = (k == BLOCK - bc + (iota((BLOCK, BLOCK), 1) >> 3)).astype(F32).astype(BF16)
    high = rows * UPSCALE
    for a in range(3):
        want = ((iota((high, rb_n * BLOCK), 0) >> 3) + (a - 1)) * bc + (bc - 1)
        hit = iota((high, rb_n * BLOCK), 1) == want
        hits[a * high : (a + 1) * high] = hit.astype(F32).astype(BF16)

    for copy in flow_cols:
        copy.wait_recv()
    west = [fb[r, 0] for r in range(1, rb_n + 1)]
    eastern = [pltpu.roll(fb[r, cb_n + 1], bc - 1, 1) for r in range(1, rb_n + 1)]
    sides = jnp.concatenate([jnp.concatenate(x, axis=1) for x in (west, eastern)], axis=0)
    tall = sum(mm_nt(hits[...], p) for p in parts(sides))
    for side in range(2):
        cc = slice(0, BLOCK) if side == 0 else slice((cb_n - 1) * BLOCK, cb_n * BLOCK)
        for d in range(2):
            y = base[d, :, cc]
            for a in range(3):
                y = y + rim_we[side, a] * tall[a * high : (a + 1) * high, 8 * side + d : 8 * side + d + 1]
            base[d, :, cc] = y

    for side in range(2):
        pl.when(present(side))(flow_rows[1 - side].wait_recv)
    cells = []
    for side in range(2):
        r = 0 if side == 0 else rb_n + 1
        at_c = [none] + [fb[r, c] for c in range(1, cb_n + 1)] + [none]
        near_by = [beside_cols(*at_c[cb : cb + 3], qc) for cb in range(cb_n)]
        if side == 1:
            near_by = [[pltpu.roll(x, BLOCK - bc, 1) for x in xs] for xs in near_by]
        cells += [near_by[cb][b] for b in range(3) for cb in range(cb_n)]
    wide = sum(mm(p, widen[...]) for p in parts(jnp.concatenate(cells, axis=0)))
    for d in range(2):
        for side in range(2):
            edge = slice(0, 8) if side == 0 else slice(high - 8, high)
            for cb in range(cb_n):
                cc = slice(cb * BLOCK, (cb + 1) * BLOCK)
                y = base[d, edge, cc]
                for b in range(3):
                    k = 8 * ((side * 3 + b) * cb_n + cb) + d
                    y = y + rim_ns[side, b, :, cc] * wide[k : k + 1]
                base[d, edge, cc] = y

    for side in range(2):

        @pl.when(present(side))
        def _():
            for copy in flow_corners[1 - side]:
                copy.wait_recv()

    flows[...] = fb[...]

    for side in range(2):

        @pl.when(present(side))
        def _():
            for copy in [flow_rows[side]] + flow_corners[side]:
                copy.wait_send()
            for band in range(len(bands)):
                for copy in relays[band][side]:
                    copy.wait_send()

    for band in range(len(bands)):
        for side in range(2):

            @pl.when(goes_direct(side, band))
            def _():
                for copy in lat_sends[band][side]:
                    copy.wait_send()

        for side, (by, on) in enumerate(detours[band]):
            pl.when(by_way[side])(by.wait_send)
            pl.when(is_hub[side])(on.wait_send)

    for copy in strips + mains + earlies + lates + flow_cols:
        copy.wait_send()


def add_corners(base, rim_corner, fb, out_hbm, out, sem):
    rb_n, cb_n = fb.shape[0] - 2, fb.shape[1] - 2
    high = base.shape[1]
    edges = [slice(0, 8), slice(high - 8, high)]
    copies = [
        pltpu.make_async_copy(
            base.at[:, pl.ds(8, high - 16)], out_hbm.at[:, pl.ds(8, high - 16)], sem.at[2]
        )
    ]
    copies[0].start()
    for end in range(2):
        for d in range(2):
            out[end, d] = base[d, edges[end], :]
            for side in range(2):
                at = slice(0, BLOCK) if side == 0 else slice((cb_n - 1) * BLOCK, cb_n * BLOCK)
                lane = (BLOCK - BLOCK_COLS) * (1 - end) + (BLOCK_COLS - 1) * (1 - side)
                x = fb[end * (rb_n + 1), side * (cb_n + 1)][d : d + 1, lane : lane + 1]
                out[end, d, :, at] = out[end, d, :, at] + rim_corner[end, side] * x
        copies.append(
            pltpu.make_async_copy(out.at[end], out_hbm.at[:, pl.ds(end * (high - 8), 8)], sem.at[end])
        )
        copies[-1].start()
    for copy in copies:
        copy.wait()


def body(frame_one, frame_two, enc_weight, mask_weight):
    rows, cols, ch = frame_one.shape
    n_mask = mask_weight.shape[1]
    rb_n, cb_n = rows // BLOCK_ROWS, cols // BLOCK_COLS
    shape = (2, rows * UPSCALE, cols * UPSCALE)
    held = pl.pallas_call(
        kernel,
        out_shape=[
            jax.ShapeDtypeStruct(shape, F32),
            jax.ShapeDtypeStruct((2, 2, UPSCALE, BLOCK), F32),
            jax.ShapeDtypeStruct((rb_n + 2, cb_n + 2, 8, BLOCK), F32),
        ],
        in_specs=[pl.BlockSpec(memory_space=pltpu.HBM)] * 4,
        out_specs=[pl.BlockSpec(memory_space=pltpu.VMEM)] * 3,
        scratch_shapes=[
            pltpu.VMEM((rows + 2, cols, ch), BF16),
            pltpu.VMEM((rows + 2 * BLOCK_ROWS + 2, cols + 2 * BLOCK_COLS, ch), BF16),
            pltpu.VMEM(enc_weight.shape, BF16),
            pltpu.VMEM((n_mask, ch), BF16),
            pltpu.VMEM((n_mask, ch), BF16),
            pltpu.VMEM((rows, cols, ch), F32),
            pltpu.VMEM((rows + 2 * BLOCK_ROWS, cols + 2 * BLOCK_COLS, ch), F32),
            pltpu.VMEM((2, 2 * rows, ch), BF16),
            pltpu.VMEM((2, 2 * rows, ch), BF16),
            pltpu.VMEM((2, 16, ch), BF16),
            pltpu.VMEM((2, 16, ch), BF16),
            pltpu.VMEM((2, 2 * BLOCK_ROWS, ch), BF16),
            pltpu.VMEM((2, 2 * BLOCK_ROWS, ch), BF16),
            pltpu.VMEM((rows + 2 * BLOCK_ROWS, cols + 2 * BLOCK_COLS, ch), BF16),
            pltpu.VMEM((cb_n, rb_n * BLOCK, ch), BF16),
            pltpu.VMEM((rb_n + 2, cb_n + 2, 8, BLOCK), F32),
            pltpu.VMEM((BLOCK_ROWS, cols, ch), BF16),
            pltpu.VMEM((cb_n, 9, UPSCALE * UPSCALE, rb_n * BLOCK), F32),
            pltpu.VMEM((2, 3, UPSCALE, cols * UPSCALE), F32),
            pltpu.VMEM((2, 3, rows * UPSCALE, BLOCK), F32),
            pltpu.VMEM((BLOCK, BLOCK), BF16),
            pltpu.VMEM((3 * rows * UPSCALE, rb_n * BLOCK), BF16),
            pltpu.SemaphoreType.DMA((4,)),
            pltpu.SemaphoreType.DMA((64,)),
            pltpu.SemaphoreType.DMA((64,)),
            pltpu.SemaphoreType.REGULAR,
        ],
        compiler_params=pltpu.CompilerParams(
            collective_id=0, has_side_effects=True, vmem_limit_bytes=32 * 2**20
        ),
        name="flow",
    )(*[pltpu.with_memory_space_constraint(a, pltpu.HBM) for a in (frame_one, frame_two, enc_weight, mask_weight.T)])
    return pl.pallas_call(
        add_corners,
        out_shape=jax.ShapeDtypeStruct(shape, F32),
        in_specs=[pl.BlockSpec(memory_space=pltpu.VMEM)] * 3,
        out_specs=pl.BlockSpec(memory_space=pl.ANY),
        scratch_shapes=[
            pltpu.VMEM((2, 2, UPSCALE, cols * UPSCALE), F32),
            pltpu.SemaphoreType.DMA((3,)),
        ],
        compiler_params=pltpu.CompilerParams(vmem_limit_bytes=32 * 2**20),
        name="add_corners",
    )(*held)


def solution(mesh):
    in_specs = (P("lat", "lon", None), P("lat", "lon", None), P(), P())
    out_specs = P(None, "lat", "lon")
    return jax.shard_map(body, mesh=mesh, in_specs=in_specs, out_specs=out_specs, check_vma=False)
```

```python
import functools
import math

import jax
import jax.numpy as jnp
from jax import lax
from jax.experimental import pallas as pl
from jax.experimental.pallas import tpu as pltpu
from jax.sharding import PartitionSpec as P

BLOCK_ROWS = 8
BLOCK_COLS = 16
BLOCK = BLOCK_ROWS * BLOCK_COLS
UPSCALE = 8
F32 = jnp.float32
BF16 = jnp.bfloat16
MESH = pl.DeviceIdType.MESH


def iota(shape, axis):
    return lax.broadcasted_iota(jnp.int32, shape, axis)


def mm(a, b):
    return jnp.dot(a, b, preferred_element_type=F32)


def mm_nt(a, b):
    return lax.dot_general(a, b, (((1,), (1,)), ((), ())), preferred_element_type=F32)


def swap_groups(xs, lane_group):
    xs = list(xs)
    for bit in (1, 2, 4):
        mask = (lane_group & bit) != 0
        shift = bit * BLOCK_COLS
        for a in range(8):
            if a & bit:
                continue
            lo, hi = xs[a], xs[a | bit]
            xs[a] = jnp.where(mask, pltpu.roll(hi, shift, 1), lo)
            xs[a | bit] = jnp.where(mask, hi, pltpu.roll(lo, BLOCK - shift, 1))
    return xs


def parts(x):
    high = x.astype(BF16)
    rest = x - high.astype(F32)
    mid = rest.astype(BF16)
    return high, mid, (rest - mid.astype(F32)).astype(BF16)


def weaving():
    k = iota((BLOCK, BLOCK), 0)
    hit = iota((BLOCK, BLOCK), 1) == ((k & (BLOCK_COLS - 1)) << 3) + (k >> 4)
    return hit.astype(F32).astype(BF16)


def by_rows(x, qr):
    return jnp.concatenate(swap_groups([x[8 * j : 8 * j + 8] for j in range(8)], qr), axis=0)


def beside_cols(west, mid, east, qc):
    return [
        jnp.where(qc == 0, pltpu.roll(west, BLOCK - (BLOCK_COLS - 1), 1), pltpu.roll(mid, 1, 1)),
        mid,
        jnp.where(qc == BLOCK_COLS - 1, pltpu.roll(east, BLOCK_COLS - 1, 1), pltpu.roll(mid, BLOCK - 1, 1)),
    ]


def kernel(
    f1, f2, w_hbm, mw_hbm, base, rim_corner, flows,
    g1, g2, wv, mv, wp, a1, a2, strip_s, strip_r, early_s, early_r, late_s, late_r, keys, qs, fb, transit, mix, rim_ns, rim_we, widen, hits,
    lsem, ssem, rsem, ready,
):
    rows, cols, ch = f1.shape
    br, bc = BLOCK_ROWS, BLOCK_COLS
    rb_n, cb_n = rows // br, cols // bc
    n_mask = mw_hbm.shape[0]
    rim = br + 1
    lat, lon = lax.axis_index("lat"), lax.axis_index("lon")
    nlat, nlon = lax.axis_size("lat"), lax.axis_size("lon")
    has_n, has_s = lat > 0, lat < nlat - 1
    left = (lat, lax.rem(lon + nlon - 1, nlon))
    right = (lat, lax.rem(lon + 1, nlon))
    north, south = (lat - 1, lon), (lat + 1, lon)

    barrier = pltpu.get_barrier_semaphore()

    def greet(peer):
        pl.semaphore_signal(barrier, inc=1, device_id=peer, device_id_type=MESH)

    first, last = lon == 0, lon == nlon - 1
    greet(left)
    pl.when(jnp.logical_not(last))(lambda: greet(right))
    pl.when(has_n)(lambda: greet(north))
    pl.when(has_s)(lambda: greet(south))

    odd = (lax.rem(lon, 2) == 1) & (nlat == 4)
    by_way = [odd & (lat == 2), odd & (lat == 1)]
    is_hub = [odd & (lat == 0), odd & (lat == 3)]
    hubs, ends = [(0, lon), (3, lon)], [(1, lon), (2, lon)]
    for side in range(2):
        pl.when(is_hub[side])(lambda: greet(ends[1 - side]))

    own = pl.ds(rim, rows)
    loads = [
        pltpu.make_async_copy(f1, g1.at[pl.ds(1, rows)], lsem.at[0]),
        pltpu.make_async_copy(f2, g2.at[own, pl.ds(bc, cols)], lsem.at[1]),
        pltpu.make_async_copy(w_hbm, wv, lsem.at[2]),
        pltpu.make_async_copy(mw_hbm, mv, lsem.at[3]),
    ]
    for load in loads:
        load.start()

    def absent(side):
        return jnp.logical_not(has_n if side == 0 else has_s)

    def present(side):
        return has_n if side == 0 else has_s

    def send(k, src, dst, peer, arrive_k=None):
        return pltpu.make_async_remote_copy(
            src_ref=src, dst_ref=dst, send_sem=ssem.at[k],
            recv_sem=rsem.at[k if arrive_k is None else arrive_k],
            device_id=peer, device_id_type=MESH,
        )

    bands = [(0, 1), (1, 4), (5, 2), (7, 2)]

    def band_at(side, band):
        off, n = bands[band]
        return (rim - off - n if side == 0 else rim + rows + off), n

    def row_send(k, side, band):
        off, n = bands[band]
        src = off if side == 0 else rows - off - n
        dst, _ = band_at(1 - side, band)
        peer = north if side == 0 else south
        return send(k, f2.at[pl.ds(src, n)], g2.at[pl.ds(dst, n), pl.ds(bc, cols)], peer)

    lat_sends = [
        [
            [
                send(side, f1.at[0 if side == 0 else rows - 1],
                     g1.at[rows + 1 if side == 0 else 0], north if side == 0 else south),
                row_send(2 + side, side, 0),
            ]
            for side in range(2)
        ],
    ]
    for band in range(1, len(bands)):
        lat_sends.append([[row_send(2 + 2 * band + side, side, band)] for side in range(2)])
    def detour(band, side):
        off, n = bands[band]
        k = 46 + 4 * (band - 1) + 2 * side
        src = off if side == 0 else rows - off - n
        at = transit.at[pl.ds(off - 1, n)]
        dst, _ = band_at(1 - side, band)
        into = g2.at[pl.ds(dst, n), pl.ds(bc, cols)]
        return (
            send(k, f2.at[pl.ds(src, n)], at, hubs[side]),
            send(k + 1, at, into, ends[side], 2 + 2 * band + side),
        )

    detours = [[]] + [[detour(band, side) for side in range(2)] for band in range(1, len(bands))]

    def goes_direct(side, band):
        if band == 0:
            return present(side)
        return present(side) & jnp.logical_not(by_way[side])

    mains = [
        send(44, f2.at[:, pl.ds(0, bc)], g2.at[own, pl.ds(bc + cols, bc)], left),
        send(45, f2.at[:, pl.ds(cols - bc, bc)], g2.at[own, pl.ds(0, bc)], right),
    ]
    strips = [
        send(10, strip_s.at[0], strip_r.at[1], left),
        send(11, strip_s.at[1], strip_r.at[0], right),
    ]
    earlies = [
        send(12, early_s.at[0], early_r.at[1], left),
        send(13, early_s.at[1], early_r.at[0], right),
    ]

    def relay(k, side, band):
        at, n = band_at(side, band)
        r = pl.ds(at, n)
        return [
            send(k, g2.at[r, pl.ds(bc, bc)], g2.at[r, pl.ds(bc + cols, bc)], left),
            send(k + 1, g2.at[r, pl.ds(cols, bc)], g2.at[r, pl.ds(0, bc)], right),
        ]

    relays = [[relay(24 + 4 * band + 2 * side, side, band) for side in range(2)] for band in range(len(bands))]
    lates = [
        send(40, late_s.at[0], late_r.at[1], left),
        send(41, late_s.at[1], late_r.at[0], right),
    ]

    for side in range(2):

        @pl.when(absent(side))
        def _():
            g1[0 if side == 0 else rows + 1] = jnp.zeros((cols, ch), BF16)
            lo = 0 if side == 0 else rim + rows
            g2[lo : lo + rim] = jnp.zeros((rim,) + g2.shape[1:], BF16)
            at = 0 if side == 0 else rb_n + 1
            fb[at] = jnp.zeros(fb.shape[1:], F32)

    met = [jnp.logical_not(first), has_n, has_s, by_way[0] | by_way[1]]
    pl.semaphore_wait(barrier, 1 + sum(m.astype(jnp.int32) for m in met))

    @pl.when(last)
    def _():
        pl.semaphore_signal(ready, inc=1, device_id=right, device_id_type=MESH)

    for band in range(len(bands)):
        for side, (by, _) in enumerate(detours[band]):
            pl.when(by_way[side])(by.start)
        for side in range(2):

            @pl.when(goes_direct(side, band))
            def _():
                for copy in lat_sends[band][side]:
                    copy.start()

    mains[1].start()
    pl.when(jnp.logical_not(first))(mains[0].start)
    loads[0].wait()
    loads[1].wait()

    def pick_col(tile, pick):
        return jnp.sum(jnp.where(iota(tile.shape, 1) == pick, tile.astype(F32), 0.0), axis=1)

    for side in range(2):
        lo, pick = (0, 0) if side == 0 else (cols - bc, bc - 1)
        strip_s[side, :rows] = pick_col(g1[1 : rows + 1, lo : lo + bc, :], pick).astype(BF16)
        lo, pick = (2 * bc, 0) if side == 0 else (cols - bc, bc - 1)
        strip_s[side, rows:] = pick_col(g2[rim : rim + rows, lo : lo + bc, :], pick).astype(BF16)
    strips[1].start()
    pl.when(jnp.logical_not(first))(strips[0].start)

    loads[2].wait()


    def taps(lhs, n, w):
        ys = [mm(lhs, wv[:, b].reshape(3 * ch, ch)) for b in range(3)]
        t0 = pltpu.roll(ys[0], 1, 0).reshape(n, w, ch)
        t2 = pltpu.roll(ys[2], n * w - 1, 0).reshape(n, w, ch)
        at = iota((n, w, ch), 1)
        y = ys[1].reshape(n, w, ch) + jnp.where(at == 0, 0.0, t0) + jnp.where(at == w - 1, 0.0, t2)
        edge = iota((n, 8, ch), 1)
        to_right = jnp.concatenate([t0[1:, :8], t0[:1, :8]], axis=0)
        to_left = jnp.concatenate([t2[n - 1 :, w - 8 :], t2[: n - 1, w - 8 :]], axis=0)
        return y, jnp.where(edge == 0, to_right, 0.0), jnp.where(edge == 7, to_left, 0.0)

    def lhs1(r, n):
        return jnp.concatenate([g1[r + a : r + a + n].reshape(n * cols, ch) for a in range(3)], axis=1)

    def lhs2(r, n, c, w):
        return jnp.concatenate(
            [g2[r + a : r + a + n, c : c + w, :].reshape(n * w, ch) for a in range(3)], axis=1
        )

    east = bc + cols

    def put_center(r, y, to_right, to_left):
        n = y.shape[0]
        a2[r : r + n, bc:east] = y
        a2[r : r + n, east : east + 8] = to_right
        a2[r : r + n, bc - 8 : bc] = to_left

    inner = rows - 2
    y, _, _ = taps(lhs1(1, inner), inner, cols)
    a1[1 : rows - 1] = y
    put_center(br + 1, *taps(lhs2(br + 1, inner, bc, cols), inner, cols))

    @pl.when(first)
    def _():
        pl.semaphore_wait(ready, 1)
        strips[0].start()
        mains[0].start()

    def arrive(band):
        for side in range(2):

            @pl.when(present(side))
            def _():
                for copy in lat_sends[band][1 - side]:
                    copy.wait_recv()

    def pass_on(band):
        for side in range(2):

            @pl.when(present(side))
            def _():
                for copy in relays[band][side]:
                    copy.start()

    def forward(band):
        for side, (by, on) in enumerate(detours[band]):

            @pl.when(is_hub[side])
            def _():
                by.wait_recv()
                on.start()

    arrive(0)
    pass_on(0)
    at_row, at_key = iota((16, 64), 0), iota((16, 64), 1)
    for side in range(2):
        c1, p1 = (0, 0) if side == 0 else (cols - bc, bc - 1)
        c2, p2 = (2 * bc, 0) if side == 0 else (cols - bc, bc - 1)
        tiles = [g1[r, c1 : c1 + bc, :] for r in (0, rows + 1)]
        tiles += [g2[r, c2 : c2 + bc, :] for r in (rim - 1, rim + rows)]
        hit = jnp.where(at_row < 2, p1, p2) + at_row * bc == at_key
        early_s[side] = mm(hit.astype(F32).astype(BF16), jnp.concatenate(tiles, axis=0)).astype(BF16)
    for copy in earlies:
        copy.start()

    for band in range(1, len(bands)):
        forward(band)
    arrive(1)
    pass_on(1)

    for band in range(2, len(bands)):
        arrive(band)
        pass_on(band)
    at_row, at_key = iota((2 * br, 2 * rim * bc), 0), iota((2 * br, 2 * rim * bc), 1)
    held = jnp.where(at_row < br, at_row, at_row + 2)
    for side in range(2):
        c, pick = (2 * bc, 0) if side == 0 else (cols - bc, bc - 1)
        tiles = [g2[r : r + rim, c : c + bc, :].reshape(rim * bc, ch) for r in (0, rim + rows)]
        hit = (held * bc + pick == at_key).astype(F32).astype(BF16)
        late_s[side] = mm(hit, jnp.concatenate(tiles, axis=0)).astype(BF16)
    for copy in lates:
        copy.start()

    for copy in strips + mains + earlies:
        copy.wait_recv()

    def relayed(band):
        for side in range(2):

            @pl.when(present(side))
            def _():
                for copy in relays[band][side]:
                    copy.wait_recv()

    relayed(0)

    near = br // 2
    last_row = br + rows - 1
    lhs = [lhs2(0, rim, bc, cols), lhs2(last_row, rim, bc, cols), lhs1(0, 1), lhs1(rows - 1, 1)]
    y, to_right, to_left = taps(jnp.concatenate(lhs, axis=0), 2 * rim + 2, cols)
    for side in range(2):
        part = slice(side * rim, (side + 1) * rim)
        put_center(side * last_row, y[part], to_right[part], to_left[part])
    a1[0] = y[2 * rim]
    a1[rows - 1] = y[2 * rim + 1]

    def put_sides(r, y, to_right, to_left, spread=None):
        n = y.shape[0] // 2
        outer = [y[:n, :8], y[n:, 8:]]
        if spread is not None:
            outer = [o + h for o, h in zip(outer, spread)]
        a2[r : r + n, :8] = outer[0]
        a2[r : r + n, 8:bc] = a2[r : r + n, 8:bc] + y[:n, 8:]
        a2[r : r + n, east : east + 8] = a2[r : r + n, east : east + 8] + y[n:, :8]
        a2[r : r + n, east + 8 :] = outer[1]
        a2[r : r + n, bc : bc + 8] = a2[r : r + n, bc : bc + 8] + to_right[:n]
        a2[r : r + n, east - 8 : east] = a2[r : r + n, east - 8 : east] + to_left[n:]

    row_id = iota((rows, ch), 0)
    spreads = []
    for side in range(2):
        lhs = jnp.concatenate([strip_r[side], early_r[side]], axis=0)
        z = [mm(lhs, wv[a, 2 * side]) for a in range(3)]
        for f in range(2):
            mid = [z[a][f * rows : (f + 1) * rows] for a in range(3)]
            e = 2 * rows + 2 * f
            h = mid[1] + jnp.where(row_id == 0, z[0][e : e + 1], pltpu.roll(mid[0], 1, 0))
            h = h + jnp.where(row_id == rows - 1, z[2][e + 1 : e + 2], pltpu.roll(mid[2], rows - 1, 0))
            lo, pick = (0, 0) if side == 0 else (cols - 8, 7)
            spread = jnp.where(iota((rows, 8, ch), 1) == pick, h[:, None, :], 0.0)
            if f == 0:
                a1[:, lo : lo + 8, :] = a1[:, lo : lo + 8, :] + spread
            else:
                spreads.append(spread)

    for cb in range(cb_n):
        for rb in range(rb_n):
            block = a1[rb * br : (rb + 1) * br, cb * bc : (cb + 1) * bc, :]
            qs[cb, rb * BLOCK : (rb + 1) * BLOCK] = block.astype(BF16).reshape(BLOCK, ch)

    lhs = [lhs2(br, rows, 0, bc), lhs2(br, rows, east, bc)]
    put_sides(br, *taps(jnp.concatenate(lhs, axis=0), 2 * rows, bc), spreads)
    keys[br : br + rows] = a2[br : br + rows].astype(BF16)

    scale = 1.0 / math.sqrt(ch)
    inside = [has_n.astype(F32), has_s.astype(F32)]
    zero = jnp.zeros((8, BLOCK), F32)
    totals = {(rb, cb): [zero, zero, zero] for rb in range(rb_n) for cb in range(cb_n)}
    sub = iota((8, BLOCK), 0).astype(F32)

    def correlate(kbs, kc):
        part = keys[kbs[0] * br : (kbs[-1] + 1) * br, kc * bc : (kc + 1) * bc, :]
        part = part.reshape(len(kbs) * BLOCK, ch)
        for cb in range(max(0, kc - 2), min(cb_n, kc + 1)):
            rbs = [rb for rb in range(rb_n) if any(0 <= kb - rb <= 2 for kb in kbs)]
            r0 = rbs[0]
            s = mm_nt(part, qs[cb, r0 * BLOCK : (rbs[-1] + 1) * BLOCK])
            for at, kb in enumerate(kbs):
                for rb in rbs:
                    if not 0 <= kb - rb <= 2:
                        continue
                    e = s[at * BLOCK : (at + 1) * BLOCK, (rb - r0) * BLOCK : (rb - r0 + 1) * BLOCK]
                    e = jnp.exp(e * scale).reshape(br, 2, 8, BLOCK)
                    lanes = [e[:, h] for h in range(2)]
                    by_row = lanes[0] + lanes[1]
                    y = by_row[0] * float(br * (kb - rb - 1))
                    for kr in range(1, br):
                        y = y + by_row[kr] * float(br * (kb - rb - 1) + kr)
                    by_col = [jnp.sum(h, axis=0) for h in lanes]
                    m = by_col[0] + by_col[1]
                    off = float(bc * (kc - cb - 1))
                    x = by_col[0] * (sub + off) + by_col[1] * (sub + (off + 8.0))
                    if kb == 0 or kb == rb_n + 1:
                        gate = inside[0] if kb == 0 else inside[1]
                        m, y, x = m * gate, y * gate, x * gate
                    old = totals[rb, cb]
                    totals[rb, cb] = [old[0] + m, old[1] + y, old[2] + x]

    own_kbs = list(range(1, rb_n + 1))
    for kc in range(cb_n + 2):
        correlate(own_kbs, kc)

    relayed(1)
    def correlate_rows(end, groups):
        rb = 0 if end == 0 else rb_n - 1
        off_r = -br if end == 0 else br
        r = end * (br + rows)
        part = [a2[r : r + br, bc + c : bc + c + 8] * inside[end] for c in groups]
        part = jnp.concatenate(part, axis=1).astype(BF16).reshape(BLOCK, ch)
        for cb in range(cb_n):
            took = [h for h, c in enumerate(groups) if bc * (cb - 1) <= c < bc * (cb + 2)]
            if not took:
                continue
            s = mm_nt(part, qs[cb, rb * BLOCK : (rb + 1) * BLOCK])
            e = jnp.exp(s * scale).reshape(br, 2, 8, BLOCK)
            by_row = sum(e[:, h] for h in took)
            y = by_row[0] * float(off_r)
            for kr in range(1, br):
                y = y + by_row[kr] * float(off_r + kr)
            by_col = [jnp.sum(e[:, h], axis=0) for h in took]
            m = sum(by_col)
            x = sum(t * (sub + float(groups[h] - bc * cb)) for t, h in zip(by_col, took))
            old = totals[rb, cb]
            totals[rb, cb] = [o + t * inside[end] for o, t in zip(old, (m, y, x))]

    for c in range(8, cols - 8, bc):
        for end in range(2):
            correlate_rows(end, (c, c + 8))
    far = br + rows + near

    def corners(starts):
        lhs = [lhs2(r, near, c, bc) for r in starts for c in (0, east)]
        y, to_right, to_left = taps(jnp.concatenate(lhs, axis=0), 4 * near, bc)
        for end, r in enumerate(starts):
            part = slice(2 * end * near, 2 * (end + 1) * near)
            put_sides(r, y[part], to_right[part], to_left[part])

    corners([near, br + rows])

    for band in range(2, len(bands)):
        relayed(band)
    for copy in lates:
        copy.wait_recv()

    corners([0, far])
    at8 = iota((br, ch), 0)
    for side in range(2):
        lhs = jnp.concatenate([late_r[side], early_r[side], strip_r[side, rows:]], axis=0)
        z = [mm(lhs, wv[a, 2 * side]) for a in range(3)]
        far_n, far_s = [x[:br] for x in z], [x[br : 2 * br] for x in z]
        by_n, by_s = [x[2 * br + 2 : 2 * br + 3] for x in z], [x[2 * br + 3 : 2 * br + 4] for x in z]
        own_n, own_s = z[2][4 * br : 4 * br + 1], z[0][4 * br + rows - 1 : 4 * br + rows]
        h_n = far_n[0] + jnp.where(at8 == br - 1, by_n[1], pltpu.roll(far_n[1], br - 1, 0))
        nxt = jnp.where(at8 == br - 2, by_n[2], pltpu.roll(far_n[2], br - 2, 0))
        h_n = h_n + jnp.where(at8 == br - 1, own_n, nxt)
        h_s = far_s[2] + jnp.where(at8 == 0, by_s[1], pltpu.roll(far_s[1], 1, 0))
        nxt = jnp.where(at8 == 1, by_s[0], pltpu.roll(far_s[0], 2, 0))
        h_s = h_s + jnp.where(at8 == 0, own_s, nxt)
        lo, pick = (0, 0) if side == 0 else (east + 8, 7)
        for end in range(2):
            part = h_n if end == 0 else h_s
            r = end * (br + rows)
            a2[r : r + br, lo : lo + 8] = a2[r : r + br, lo : lo + 8] + jnp.where(
                iota((br, 8, ch), 1) == pick, part[:, None, :], 0.0
            )
    for end in range(2):
        for groups in ((-bc, 8 - bc), (0, cols - 8), (cols, cols + 8)):
            correlate_rows(end, groups)

    lane = iota((8, BLOCK), 1)
    sublane = iota((8, BLOCK), 0)
    qr, qc = lane >> 4, lane & 15
    for (rb, cb), (m, y, x) in totals.items():
        m, y, x = [jnp.sum(t, axis=0, keepdims=True) for t in (m, y, x)]
        fy = y / m - qr.astype(F32)
        fx = x / m - qc.astype(F32)
        both = jnp.where(sublane == 0, fy, fx) * float(UPSCALE)
        fb[rb + 1, cb + 1] = both

    flow_rows = [
        send(16, fb.at[1, pl.ds(1, cb_n)], fb.at[rb_n + 1, pl.ds(1, cb_n)], north),
        send(17, fb.at[rb_n, pl.ds(1, cb_n)], fb.at[0, pl.ds(1, cb_n)], south),
    ]
    flow_cols = [
        send(18, fb.at[pl.ds(1, rb_n), 1], fb.at[pl.ds(1, rb_n), cb_n + 1], left),
        send(19, fb.at[pl.ds(1, rb_n), cb_n], fb.at[pl.ds(1, rb_n), 0], right),
    ]
    flow_corners = {}
    for side in range(2):
        src_r, dst_r = (1, rb_n + 1) if side == 0 else (rb_n, 0)
        to = lat - 1 if side == 0 else lat + 1
        flow_corners[side] = [
            send(20 + 2 * side, fb.at[src_r, 1], fb.at[dst_r, cb_n + 1], (to, left[1])),
            send(21 + 2 * side, fb.at[src_r, cb_n], fb.at[dst_r, 0], (to, right[1])),
        ]
    for side in range(2):

        @pl.when(present(side))
        def _():
            for copy in flow_corners[side] + [flow_rows[side]]:
                copy.start()

    for copy in flow_cols:
        copy.start()
    loads[3].wait()
    p = iota((n_mask, n_mask), 0)
    want = (p - (p & 63)) + ((p & 7) << 3) + ((p >> 3) & 7)
    perm = (iota((n_mask, n_mask), 1) == want).astype(F32).astype(BF16)
    wp[...] = mm(perm, mv[...]).astype(BF16)

    for cb in range(cb_n):
        logits = mm_nt(wp[...], qs[cb]).reshape(9, UPSCALE * UPSCALE, rb_n * BLOCK)
        e = jnp.exp(logits)
        mix[cb] = e / jnp.sum(e, axis=0, keepdims=True)

    weave = weaving()

    def woven(x):
        return sum(mm(p, weave) for p in parts(x))

    none = jnp.zeros((8, BLOCK), F32)
    own_fb = {(r, c): fb[r, c] for r in range(1, rb_n + 1) for c in range(1, cb_n + 1)}

    def at_block(r, c):
        return own_fb.get((r, c), none)

    for cb in range(cb_n):
        for rb in range(rb_n):
            shifted = {
                r: beside_cols(at_block(r, cb), at_block(r, cb + 1), at_block(r, cb + 2), qc)
                for r in range(rb, rb + 3)
            }
            beside = []
            for a in range(3):
                for b in range(3):
                    here = shifted[rb + 1][b]
                    if a == 0:
                        here = pltpu.roll(jnp.where(qr == br - 1, shifted[rb][b], here), bc, 1)
                    if a == 2:
                        here = pltpu.roll(jnp.where(qr == 0, shifted[rb + 2][b], here), BLOCK - bc, 1)
                    beside.append(here)
            for d in range(2):
                up = jnp.zeros((UPSCALE * UPSCALE, BLOCK), F32)
                for n in range(9):
                    up = up + mix[cb, n, :, rb * BLOCK : (rb + 1) * BLOCK] * beside[n][d : d + 1]
                base[d, rb * 64 : (rb + 1) * 64, cb * BLOCK : (cb + 1) * BLOCK] = woven(by_rows(up, qr))

    def share(rb, cb, n):
        return by_rows(mix[cb, n, :, rb * BLOCK : (rb + 1) * BLOCK], qr)

    tops = [share(0, cb, b)[:8] for b in range(3) for cb in range(cb_n)]
    tops += [share(rb_n - 1, cb, 6 + b)[56:] for b in range(3) for cb in range(cb_n)]
    tops = woven(jnp.concatenate(tops, axis=0))
    for side in range(2):
        for b in range(3):
            for cb in range(cb_n):
                k = 8 * ((side * 3 + b) * cb_n + cb)
                rim_ns[side, b, :, cb * BLOCK : (cb + 1) * BLOCK] = tops[k : k + 8]
    lanes = iota((64, BLOCK), 1)
    for side in range(2):
        keep = lanes < UPSCALE if side == 0 else lanes >= BLOCK - UPSCALE
        for a in range(3):
            for rb in range(rb_n):
                x = woven(share(rb, 0 if side == 0 else cb_n - 1, 3 * a + 2 * side))
                rim_we[side, a, rb * 64 : (rb + 1) * 64] = jnp.where(keep, x, 0.0)
        at = 0 if side == 0 else cb_n - 1
        for end in range(2):
            k = 8 * ((end * 3 + 2 * side) * cb_n + at)
            rim_corner[end, side] = jnp.where(keep[:8], tops[k : k + 8], 0.0)

    k = iota((BLOCK, BLOCK), 0)
    widen[...] = (k == BLOCK - bc + (iota((BLOCK, BLOCK), 1) >> 3)).astype(F32).astype(BF16)
    high = rows * UPSCALE
    want = (iota((high, rb_n * BLOCK), 0) >> 3) * bc + (bc - 1)
    hits[...] = (iota((high, rb_n * BLOCK), 1) == want).astype(F32).astype(BF16)

    for copy in flow_cols:
        copy.wait_recv()
    west = [fb[r, 0] for r in range(1, rb_n + 1)]
    eastern = [pltpu.roll(fb[r, cb_n + 1], bc - 1, 1) for r in range(1, rb_n + 1)]
    sides = jnp.concatenate([jnp.concatenate(x, axis=1) for x in (west, eastern)], axis=0)
    tall = sum(mm_nt(hits[...], p) for p in parts(sides))
    for side in range(2):
        cc = slice(0, BLOCK) if side == 0 else slice((cb_n - 1) * BLOCK, cb_n * BLOCK)
        for d in range(2):
            k = 8 * side + d
            one = jnp.broadcast_to(tall[:, k : k + 1], (high, BLOCK))
            void = jnp.zeros((UPSCALE, BLOCK), F32)
            above = jnp.concatenate([void, one[: high - UPSCALE]], axis=0)
            below = jnp.concatenate([one[UPSCALE:], void], axis=0)
            y = base[d, :, cc] + rim_we[side, 0] * above
            base[d, :, cc] = y + rim_we[side, 1] * one + rim_we[side, 2] * below

    for side in range(2):
        pl.when(present(side))(flow_rows[1 - side].wait_recv)
    cells = []
    for side in range(2):
        r = 0 if side == 0 else rb_n + 1
        at_c = [none] + [fb[r, c] for c in range(1, cb_n + 1)] + [none]
        near_by = [beside_cols(*at_c[cb : cb + 3], qc) for cb in range(cb_n)]
        if side == 1:
            near_by = [[pltpu.roll(x, BLOCK - bc, 1) for x in xs] for xs in near_by]
        cells += [near_by[cb][b] for b in range(3) for cb in range(cb_n)]
    wide = sum(mm(p, widen[...]) for p in parts(jnp.concatenate(cells, axis=0)))
    for d in range(2):
        for side in range(2):
            edge = slice(0, 8) if side == 0 else slice(high - 8, high)
            for cb in range(cb_n):
                cc = slice(cb * BLOCK, (cb + 1) * BLOCK)
                y = base[d, edge, cc]
                for b in range(3):
                    k = 8 * ((side * 3 + b) * cb_n + cb) + d
                    y = y + rim_ns[side, b, :, cc] * wide[k : k + 1]
                base[d, edge, cc] = y

    for side in range(2):

        @pl.when(present(side))
        def _():
            for copy in flow_corners[1 - side]:
                copy.wait_recv()

    flows[...] = fb[...]

    for side in range(2):

        @pl.when(present(side))
        def _():
            for copy in [flow_rows[side]] + flow_corners[side]:
                copy.wait_send()
            for band in range(len(bands)):
                for copy in relays[band][side]:
                    copy.wait_send()

    for band in range(len(bands)):
        for side in range(2):

            @pl.when(goes_direct(side, band))
            def _():
                for copy in lat_sends[band][side]:
                    copy.wait_send()

        for side, (by, on) in enumerate(detours[band]):
            pl.when(by_way[side])(by.wait_send)
            pl.when(is_hub[side])(on.wait_send)

    for copy in strips + mains + earlies + lates + flow_cols:
        copy.wait_send()


def add_corners(base, rim_corner, fb, out_hbm, out, sem):
    rb_n, cb_n = fb.shape[0] - 2, fb.shape[1] - 2
    high = base.shape[1]
    edges = [slice(0, 8), slice(high - 8, high)]
    copies = [
        pltpu.make_async_copy(
            base.at[:, pl.ds(8, high - 16)], out_hbm.at[:, pl.ds(8, high - 16)], sem.at[2]
        )
    ]
    copies[0].start()
    for end in range(2):
        for d in range(2):
            out[end, d] = base[d, edges[end], :]
            for side in range(2):
                at = slice(0, BLOCK) if side == 0 else slice((cb_n - 1) * BLOCK, cb_n * BLOCK)
                lane = (BLOCK - BLOCK_COLS) * (1 - end) + (BLOCK_COLS - 1) * (1 - side)
                x = fb[end * (rb_n + 1), side * (cb_n + 1)][d : d + 1, lane : lane + 1]
                out[end, d, :, at] = out[end, d, :, at] + rim_corner[end, side] * x
        copies.append(
            pltpu.make_async_copy(out.at[end], out_hbm.at[:, pl.ds(end * (high - 8), 8)], sem.at[end])
        )
        copies[-1].start()
    for copy in copies:
        copy.wait()


def body(frame_one, frame_two, enc_weight, mask_weight):
    rows, cols, ch = frame_one.shape
    n_mask = mask_weight.shape[1]
    rb_n, cb_n = rows // BLOCK_ROWS, cols // BLOCK_COLS
    shape = (2, rows * UPSCALE, cols * UPSCALE)
    held = pl.pallas_call(
        kernel,
        out_shape=[
            jax.ShapeDtypeStruct(shape, F32),
            jax.ShapeDtypeStruct((2, 2, UPSCALE, BLOCK), F32),
            jax.ShapeDtypeStruct((rb_n + 2, cb_n + 2, 8, BLOCK), F32),
        ],
        in_specs=[pl.BlockSpec(memory_space=pltpu.HBM)] * 4,
        out_specs=[pl.BlockSpec(memory_space=pltpu.VMEM)] * 3,
        scratch_shapes=[
            pltpu.VMEM((rows + 2, cols, ch), BF16),
            pltpu.VMEM((rows + 2 * BLOCK_ROWS + 2, cols + 2 * BLOCK_COLS, ch), BF16),
            pltpu.VMEM(enc_weight.shape, BF16),
            pltpu.VMEM((n_mask, ch), BF16),
            pltpu.VMEM((n_mask, ch), BF16),
            pltpu.VMEM((rows, cols, ch), F32),
            pltpu.VMEM((rows + 2 * BLOCK_ROWS, cols + 2 * BLOCK_COLS, ch), F32),
            pltpu.VMEM((2, 2 * rows, ch), BF16),
            pltpu.VMEM((2, 2 * rows, ch), BF16),
            pltpu.VMEM((2, 16, ch), BF16),
            pltpu.VMEM((2, 16, ch), BF16),
            pltpu.VMEM((2, 2 * BLOCK_ROWS, ch), BF16),
            pltpu.VMEM((2, 2 * BLOCK_ROWS, ch), BF16),
            pltpu.VMEM((rows + 2 * BLOCK_ROWS, cols + 2 * BLOCK_COLS, ch), BF16),
            pltpu.VMEM((cb_n, rb_n * BLOCK, ch), BF16),
            pltpu.VMEM((rb_n + 2, cb_n + 2, 8, BLOCK), F32),
            pltpu.VMEM((BLOCK_ROWS, cols, ch), BF16),
            pltpu.VMEM((cb_n, 9, UPSCALE * UPSCALE, rb_n * BLOCK), F32),
            pltpu.VMEM((2, 3, UPSCALE, cols * UPSCALE), F32),
            pltpu.VMEM((2, 3, rows * UPSCALE, BLOCK), F32),
            pltpu.VMEM((BLOCK, BLOCK), BF16),
            pltpu.VMEM((rows * UPSCALE, rb_n * BLOCK), BF16),
            pltpu.SemaphoreType.DMA((4,)),
            pltpu.SemaphoreType.DMA((64,)),
            pltpu.SemaphoreType.DMA((64,)),
            pltpu.SemaphoreType.REGULAR,
        ],
        compiler_params=pltpu.CompilerParams(
            collective_id=0, has_side_effects=True, vmem_limit_bytes=32 * 2**20
        ),
        name="flow",
    )(*[pltpu.with_memory_space_constraint(a, pltpu.HBM) for a in (frame_one, frame_two, enc_weight, mask_weight.T)])
    return pl.pallas_call(
        add_corners,
        out_shape=jax.ShapeDtypeStruct(shape, F32),
        in_specs=[pl.BlockSpec(memory_space=pltpu.VMEM)] * 3,
        out_specs=pl.BlockSpec(memory_space=pl.ANY),
        scratch_shapes=[
            pltpu.VMEM((2, 2, UPSCALE, cols * UPSCALE), F32),
            pltpu.SemaphoreType.DMA((3,)),
        ],
        compiler_params=pltpu.CompilerParams(vmem_limit_bytes=32 * 2**20),
        name="add_corners",
    )(*held)


def solution(mesh):
    in_specs = (P("lat", "lon", None), P("lat", "lon", None), P(), P())
    out_specs = P(None, "lat", "lon")
    return jax.shard_map(body, mesh=mesh, in_specs=in_specs, out_specs=out_specs, check_vma=False)
```
